32 devices in a mesh: gx: 8 (over y, x, core), gy: 4 (over z).
Axes of the slice: x: 2, y: 2, z: 4, core: 2. Of those that a mesh axis runs over, the one named last changes fastest.
Arguments:
- grad_p: float32 [3, 128, 64, 128], P(None, 'gx', 'gy'), may hold values from -6 to 6
- grad_s: float32 [3, 128, 64, 128], P(None, 'gx', 'gy'), may hold values from -6 to 6
- acc_p: float32 [128, 64, 128], P('gx', 'gy'), may hold values from 0.2 to 2
- acc_s: float32 [128, 64, 128], P('gx', 'gy'), may hold values from 0.2 to 2
- trans_x: float32 [128, 64, 128], P('gx', 'gy'), may hold values from 0.1 to 10
- trans_y: float32 [128, 64, 128], P('gx', 'gy'), may hold values from 0.1 to 10
- trans_z: float32 [128, 64, 128], P('gx', 'gy'), may hold values from 0.1 to 10
- c_pp: float32 [3, 128, 64, 128], P(None, 'gx', 'gy'), may hold values from 0.05 to 0.5
- c_ss: float32 [3, 128, 64, 128], P(None, 'gx', 'gy'), may hold values from 0.2 to 2
- c_ps: float32 [3, 128, 64, 128], P(None, 'gx', 'gy'), may hold values from -0.2 to 0.2
- c_sp: float32 [3, 128, 64, 128], P(None, 'gx', 'gy'), may hold values from -0.5 to 0.5
- frac: float32 [3, 128, 64, 128], P(None, 'gx', 'gy'), may hold values from 0 to 0.5
- mobility: float32 [3, 128, 64, 128], P(None, 'gx', 'gy'), may hold values from 0.5 to 2
- rate_mis: float32 [64, 3], P(('gx', 'gy')), may hold values from -6 to 6
- bhp_mis: float32 [64, 3], P(('gx', 'gy')), may hold values from -6 to 6
- control: int32 [64, 3], P(('gx', 'gy')), may hold values from 0 to 1
- perf_well: int32 [4096], P(('gx', 'gy')), may hold values from 0 to 63
- perf_cell: int32 [4096], P(('gx', 'gy')), may hold values from 0 to 32767
- perf_wi: float32 [4096], P(('gx', 'gy')), may hold values from 1 to 10
Outputs:
- lam_p: float32 [128, 64, 128], P('gx', 'gy')
- lam_s: float32 [128, 64, 128], P('gx', 'gy')
- well_grad: float32 [64, 3], P(('gx', 'gy'))
The draws below stay inside these ranges and needn't reach their ends.
Inputs may be any that keep to these rules, and one draw needn't show every extreme that they name: perf_cell indexes the block of the device that holds the slot, as (i * 16 + j) * 128 + k; slots may share a cell. `perf_well`: well w is held by the device of flat index w // 2 along gx+gy; a well's slots may lie on any devices.
All inputs are finite; a program needn't handle non-finite values.
Results may differ from the reference program's by a relative error of at most 0.0002.
Values sent between devices are 32-bit elements; how exact they have to be, the bound alone decides.
No kernel may reach another device: no remote copies, remote signals or barrier semaphores. Data moves between devices by JAX's collectives and lax.ppermute only.
A program may use at most 128 MiB of HBM per device.

```python
import math
import jax
import jax.numpy as jnp
import numpy as np

CX = 16
CY = 16
NZ = 128
STEPS = 3
SWEEPS = 8
PF_DEV = 128
NX = 128
NY = 64
NWELL = 64
NPERF = 4096
N_GY = 4


def with_ends(result, own_key, smallest, top_value):
    spot = [jax.random.randint(jax.random.fold_in(own_key, axis), (), 0, length) for axis, length in enumerate(result.shape)]
    longest = result.shape.index(max(result.shape))
    next_to = spot[:longest] + [(spot[longest] + 1) % result.shape[longest]] + spot[longest + 1:]
    return result.at[tuple(spot)].set(smallest).at[tuple(next_to)].set(top_value)


def steps_of(rng, dims, cuts, least, largest):
    factor_of = 1.0
    for axis_at, blocks in cuts:
        steps = jax.random.uniform(jax.random.fold_in(jax.random.fold_in(rng, 6), axis_at), (blocks,), jnp.float32, least / len(cuts), largest / len(cuts))
        factor_of = factor_of * jnp.repeat(jnp.exp(steps), dims[axis_at] // blocks).reshape((-1,) + (1,) * (len(dims) - 1 - axis_at))
    return factor_of


def rank_bounds(count, slope):
    loads = [(1 << 20) // math.isqrt(rank ** slope) + 1 for rank in range(1, count + 1)]
    width = 1 + sum(loads) // (1 << 30)
    return np.cumsum(np.array([max(1, weight // width) for weight in loads]))


def ranked_ids(rng, dims, count, lean):
    grid = rank_bounds(count, lean)
    pick = jax.random.randint(jax.random.fold_in(rng, 1), dims, 0, int(grid[count - 1]))
    standing = jnp.searchsorted(jnp.asarray(grid, jnp.int32), pick, side="right")
    return jax.random.permutation(jax.random.fold_in(rng, 2), count)[standing].astype(jnp.int32)


def normal_values(stream_key, dims, spread, reach, split=(), held_as=jnp.bfloat16):
    level = steps_of(stream_key, dims, split, -0.22, 0.18) if split else 1.0
    entries = jax.random.normal(stream_key, dims, jnp.float32) * spread * level
    return jnp.minimum(jnp.maximum(entries, -reach), reach).astype(held_as)


def setup_inputs(seed: int = 0) -> dict:
    seeds = jax.random.split(jax.random.key(seed), 20)
    grad_p = normal_values(seeds[0], (STEPS, NX, NY, NZ), 1.0, 6.0, ((1, 8), (2, 4)), jnp.float32)
    grad_s = normal_values(seeds[1], (STEPS, NX, NY, NZ), 1.0, 6.0, ((1, 8), (2, 4)), jnp.float32)
    acc_p = jnp.clip(jnp.exp(math.log(2.0) - 2.3025851 * jax.random.uniform(seeds[2], (NX, NY, NZ), jnp.float32) ** steps_of(seeds[2], (NX, NY, NZ), ((0, 8), (1, 4)), -0.2, 0.2)), 0.2, 2.0)
    acc_s = jnp.clip(jnp.exp(math.log(2.0) - 2.3025851 * jax.random.uniform(seeds[3], (NX, NY, NZ), jnp.float32) ** steps_of(seeds[3], (NX, NY, NZ), ((0, 8), (1, 4)), -0.2, 0.2)), 0.2, 2.0)
    trans_x = jnp.clip(jnp.exp(math.log(10.0) - 4.6051702 * jax.random.uniform(seeds[4], (NX, NY, NZ), jnp.float32) ** steps_of(seeds[4], (NX, NY, NZ), ((0, 8), (1, 4)), -0.2, 0.2)), 0.1, 10.0)
    trans_y = jnp.clip(jnp.exp(math.log(10.0) - 4.6051702 * jax.random.uniform(seeds[5], (NX, NY, NZ), jnp.float32) ** steps_of(seeds[5], (NX, NY, NZ), ((0, 8), (1, 4)), -0.2, 0.2)), 0.1, 10.0)
    trans_z = jnp.clip(jnp.exp(math.log(10.0) - 4.6051702 * jax.random.uniform(seeds[6], (NX, NY, NZ), jnp.float32) ** steps_of(seeds[6], (NX, NY, NZ), ((0, 8), (1, 4)), -0.2, 0.2)), 0.1, 10.0)
    c_pp = jnp.clip(jnp.exp(math.log(0.5) - 2.3025851 * jax.random.uniform(seeds[7], (STEPS, NX, NY, NZ), jnp.float32) ** steps_of(seeds[7], (STEPS, NX, NY, NZ), ((1, 8), (2, 4)), -0.2, 0.2)), 0.05, 0.5)
    c_ss = jnp.clip(jnp.exp(math.log(2.0) - 2.3025851 * jax.random.uniform(seeds[8], (STEPS, NX, NY, NZ), jnp.float32) ** steps_of(seeds[8], (STEPS, NX, NY, NZ), ((1, 8), (2, 4)), -0.2, 0.2)), 0.2, 2.0)
    c_ps = jnp.clip(jax.random.uniform(seeds[9], (STEPS, NX, NY, NZ), jnp.float32, -0.2, 0.2) * steps_of(seeds[9], (STEPS, NX, NY, NZ), ((1, 8), (2, 4)), -0.4, 0.0), -0.2, 0.2)
    c_sp = jnp.clip(jax.random.uniform(seeds[10], (STEPS, NX, NY, NZ), jnp.float32, -0.5, 0.5) * steps_of(seeds[10], (STEPS, NX, NY, NZ), ((1, 8), (2, 4)), -0.4, 0.0), -0.5, 0.5)
    frac = jnp.clip(0.5 * jax.random.uniform(seeds[11], (STEPS, NX, NY, NZ), jnp.float32) ** steps_of(seeds[11], (STEPS, NX, NY, NZ), ((1, 8), (2, 4)), -0.2, 0.2), 0.0, 0.5)
    mobility = jnp.clip(jnp.exp(math.log(2.0) - 1.3862944 * jax.random.uniform(seeds[12], (STEPS, NX, NY, NZ), jnp.float32) ** steps_of(seeds[12], (STEPS, NX, NY, NZ), ((1, 8), (2, 4)), -0.2, 0.2)), 0.5, 2.0)
    rate_mis = normal_values(seeds[13], (NWELL, STEPS), 1.0, 6.0, ((0, 32),), jnp.float32)
    bhp_mis = normal_values(seeds[14], (NWELL, STEPS), 1.0, 6.0, ((0, 32),), jnp.float32)
    control = with_ends(jax.random.randint(seeds[15], (NWELL, STEPS), 0, 2), jax.random.fold_in(seeds[15], 1), 0, 1).astype(jnp.int32)
    perf_well = with_ends(ranked_ids(seeds[16], (NPERF,), NWELL, 2), jax.random.fold_in(seeds[16], 3), 0, NWELL - 1).astype(jnp.int32)
    perf_cell = with_ends(jax.random.randint(seeds[17], (NPERF,), 0, CX * CY * NZ), jax.random.fold_in(seeds[17], 1), 0, (CX * CY * NZ) - 1).astype(jnp.int32)
    perf_wi = jnp.clip(jnp.exp(math.log(10.0) - 2.3025851 * jax.random.uniform(seeds[18], (NPERF,), jnp.float32) ** steps_of(seeds[18], (NPERF,), ((0, 32),), -0.2, 0.2)), 1.0, 10.0)
    return {"grad_p": grad_p, "grad_s": grad_s, "acc_p": acc_p, "acc_s": acc_s, "trans_x": trans_x, "trans_y": trans_y, "trans_z": trans_z, "c_pp": c_pp, "c_ss": c_ss, "c_ps": c_ps, "c_sp": c_sp, "frac": frac, "mobility": mobility, "rate_mis": rate_mis, "bhp_mis": bhp_mis, "control": control, "perf_well": perf_well, "perf_cell": perf_cell, "perf_wi": perf_wi}


omega_factor = 0.8


def neighbour_terms(field, weights):
    padded = jnp.pad(field, 1)
    total = weights[0] * padded[2:, 1:-1, 1:-1] + weights[1] * padded[:-2, 1:-1, 1:-1]
    total = total + weights[2] * padded[1:-1, 2:, 1:-1] + weights[3] * padded[1:-1, :-2, 1:-1]
    total = total + weights[4] * padded[1:-1, 1:-1, 2:] + weights[5] * padded[1:-1, 1:-1, :-2]
    return total


def reference(grad_p, grad_s, acc_p, acc_s, trans_x, trans_y, trans_z, c_pp, c_ss, c_ps, c_sp, frac, mobility, rate_mis, bhp_mis, control, perf_well, perf_cell, perf_wi):
    zero_x = jnp.zeros((1, NY, NZ), jnp.float32)
    zero_y = jnp.zeros((NX, 1, NZ), jnp.float32)
    zero_z = jnp.zeros((NX, NY, 1), jnp.float32)
    w_east = jnp.concatenate([trans_x[1:], zero_x], axis=0)
    w_west = jnp.concatenate([zero_x, trans_x[1:]], axis=0)
    w_north = jnp.concatenate([trans_y[:, 1:], zero_y], axis=1)
    w_south = jnp.concatenate([zero_y, trans_y[:, 1:]], axis=1)
    w_up = jnp.concatenate([trans_z[:, :, 1:], zero_z], axis=2)
    w_down = jnp.concatenate([zero_z, trans_z[:, :, 1:]], axis=2)
    weights = (w_east, w_west, w_north, w_south, w_up, w_down)
    weight_sum = w_east + w_west + w_north + w_south + w_up + w_down

    slots = jnp.arange(NPERF, dtype=jnp.int32)
    device = slots // PF_DEV
    local_i = perf_cell // (CY * NZ)
    local_j = (perf_cell // NZ) % CY
    local_k = perf_cell % NZ
    global_x = (device // N_GY) * CX + local_i
    global_y = (device % N_GY) * CY + local_j
    flat_cell = ((global_x * NY + global_y) * NZ + local_k).astype(jnp.int32)

    effective = jnp.where(control == 1, rate_mis, bhp_mis)
    lam_a = jnp.zeros((NX, NY, NZ), jnp.float32)
    lam_b = jnp.zeros((NX, NY, NZ), jnp.float32)
    sensitivities = []
    for step_index in reversed(range(STEPS)):
        source = jnp.zeros((NX * NY * NZ,), jnp.float32).at[flat_cell].add(perf_wi * effective[perf_well, step_index]).reshape(NX, NY, NZ)
        right_a = grad_p[step_index] + source + acc_p * lam_a
        right_b = grad_s[step_index] + acc_s * lam_b
        scale_a = omega_factor / (c_pp[step_index] + weight_sum)
        scale_b = omega_factor / (c_ss[step_index] + mobility[step_index] * weight_sum)
        for sweep_index in range(SWEEPS):
            lap_a = weight_sum * lam_a - neighbour_terms(lam_a, weights)
            lap_b = weight_sum * lam_b - neighbour_terms(lam_b, weights)
            out_a = c_pp[step_index] * lam_a + lap_a + c_sp[step_index] * lam_b + frac[step_index] * lap_b
            out_b = c_ps[step_index] * lam_a + c_ss[step_index] * lam_b + mobility[step_index] * lap_b
            lam_a, lam_b = lam_a + scale_a * (right_a - out_a), lam_b + scale_b * (right_b - out_b)
        at_a = lam_a.reshape(-1)[flat_cell]
        at_b = lam_b.reshape(-1)[flat_cell]
        at_frac = frac[step_index].reshape(-1)[flat_cell]
        values = perf_wi * (at_a + at_frac * at_b)
        sensitivities.insert(0, jax.ops.segment_sum(values, perf_well, num_segments=NWELL))
    well_grad = jnp.stack(sensitivities, axis=1)
    return lam_a, lam_b, well_grad
```

```python
import functools

import jax
import jax.numpy as jnp
from jax import lax
from jax.experimental import pallas as pl
from jax.experimental.pallas import tpu as pltpu
from jax.sharding import PartitionSpec as P

SWEEPS = 8
OMEGA = 0.8
H = 8
HIGHEST = lax.Precision.HIGHEST
STEP_NAMES = 8


def shifted(value, axis, by):
    length = lax.axis_size(axis)
    pairs = [(i, i + by) for i in range(length) if 0 <= i + by < length]
    return lax.ppermute(value, axis, pairs)


def place_edges(dst, n, own, z_low, z_high, x_low, x_high):
    rx, ry, _ = own.shape
    dst[n, H : H + rx, H : H + ry, :] = own
    dst[n, H : H + rx, 0:H, :] = z_low
    dst[n, H : H + rx, H + ry : H + ry + H, :] = z_high
    dst[n, 0:H, 0 : ry + 2 * H, :] = x_low
    dst[n, H + rx : H + rx + H, 0 : ry + 2 * H, :] = x_high


def build_source(src, table_ref, ids_ref, step, steps, wells, rx, ry):
    f32 = jnp.float32
    count = table_ref.shape[0]
    rows_of = table_ref[:, 0, :]
    owner_iota = lax.broadcasted_iota(jnp.int32, (count, 128), 0)
    lane_iota = lax.broadcasted_iota(jnp.int32, (128, 128), 0)
    spans = ((0, H, rx - H), (H, rx, 0), (H + rx, H, 0))
    spans_y = ((0, H, ry - H), (H, ry, 0), (H + ry, H, 0))
    for dx in range(3):
        for dy in range(3):
            k = dx * 3 + dy
            at = ids_ref[k]
            live = ids_ref[9 + k].astype(f32)
            slot = table_ref[at]
            cell = slot[1:2, :].astype(jnp.int32)
            well = slot[2:3, :].astype(jnp.int32)
            wi = slot[3:4, :] * live
            owner = well // wells
            within = well - owner * wells
            hot = jnp.where(owner_iota == owner, 1.0, 0.0).astype(f32)
            rows = lax.dot_general(
                rows_of, hot, (((0,), (0,)), ((), ())), precision=HIGHEST,
                preferred_element_type=f32,
            )
            value = jnp.zeros((1, 128), f32)
            for u in range(wells):
                c = u * steps + step
                value = value + jnp.where(within == u, rows[c : c + 1, :], 0.0)
            value = value * wi
            lane = cell & 127
            row = cell >> 7
            by_lane = jnp.where(lane_iota == lane, value, 0.0)
            x0, nx, from_x = spans[dx]
            y0, ny, from_y = spans_y[dy]
            xi = lax.broadcasted_iota(jnp.int32, (nx, ny, 128), 0) + from_x
            yi = lax.broadcasted_iota(jnp.int32, (nx, ny, 128), 1) + from_y
            target = (xi * ry + yi).reshape(nx * ny, 128)
            by_row = jnp.where(target == row, 1.0, 0.0).astype(f32)
            part = lax.dot_general(
                by_row, by_lane, (((1,), (1,)), ((), ())), precision=HIGHEST,
                preferred_element_type=f32,
            )
            src[x0 : x0 + nx, y0 : y0 + ny, :] = part.reshape(nx, ny, 128)


def step_kernel(first, last, step, steps, wells, *refs):
    f32 = jnp.float32
    it = iter(refs)
    ids_ref, table_ref = next(it), next(it)
    own = [next(it) for _ in range(STEP_NAMES)]
    got = [next(it) for _ in range(4)]
    if first:
        own_geo = [next(it) for _ in range(3)]
    else:
        geo_in = next(it)
        own_acc = [next(it) for _ in range(2)] if step == steps - 2 else None
        acc_in = None if own_acc is not None else next(it)
        lam_own = next(it)
        lam_got = [next(it) for _ in range(4)]
        wells_in = next(it)
    if first:
        geo = next(it)
    else:
        geo = geo_in
    if last:
        out_a, out_b = next(it), next(it)
    else:
        out_lam, out_low, out_high = next(it), next(it), next(it)
        if not first:
            acc_out = next(it)
    out_wells = next(it)
    raw, coef, fields, src = next(it), next(it), next(it), next(it)

    rx, ry, nz = own[0].shape[-3:]
    ex, ey = rx + 2 * H, ry + 2 * H
    got_base = 3 if first else 0

    if first:
        for n in range(3):
            place_edges(geo, n, own_geo[n][...], *[g[n] for g in got])
        geo[1, :, ey : ey + 8, :] = jnp.zeros((ex, 8, nz), f32)

        lane = lax.broadcasted_iota(jnp.int32, (ey, nz), 1)

        def mask_z(x, _):
            geo[2, x, 0:ey, :] = jnp.where(lane == 0, 0.0, geo[2, x, 0:ey, :])
            return 0

        lax.fori_loop(0, ex, mask_z, 0)

        @pl.when(ids_ref[18] == 0)
        def _():
            geo[0, H, :, :] = jnp.zeros(geo.shape[2:], f32)

        @pl.when(ids_ref[19] == 0)
        def _():
            geo[1, :, H : H + 1, :] = jnp.zeros((ex, 1, nz), f32)

    for n in range(STEP_NAMES):
        place_edges(raw, n, own[n][0], *[g[got_base + n] for g in got])
    if not first:
        if own_acc is not None:
            acc = acc_out
            for n in range(2):
                place_edges(acc, n, own_acc[n][...], *[g[STEP_NAMES + n] for g in got])
        else:
            acc = acc_in

    build_source(src, table_ref, ids_ref, step, steps, wells, rx, ry)

    zero_pad = jnp.zeros((ex, 8, nz), f32)
    for buf in range(2):
        for f in range(2):
            fields[buf, f, :, 0:8, :] = zero_pad
            fields[buf, f, :, 8 + ey : 16 + ey, :] = zero_pad
            fields[buf, f, 0, 8 : 8 + ey, :] = jnp.zeros((ey, nz), f32)
            fields[buf, f, ex - 1, 8 : 8 + ey, :] = jnp.zeros((ey, nz), f32)

    if not first:
        for f in range(2):
            lo = 8 + H
            fields[0, f, H : H + rx, lo : lo + ry, :] = lam_own[f]
            fields[0, f, H : H + rx, 8:lo, :] = lam_got[0][f]
            fields[0, f, H : H + rx, lo + ry : lo + ry + H, :] = lam_got[1][f]
            fields[0, f, 0:H, 8 : 8 + ey, :] = lam_got[2][f]
            fields[0, f, H + rx : ex, 8 : 8 + ey, :] = lam_got[3][f]

    def prepare(x, _):
        tz = geo[2, x, 0:ey, :]
        total = (
            geo[0, x + 1, 0:ey, :]
            + geo[0, x, 0:ey, :]
            + geo[1, x, 1 : ey + 1, :]
            + geo[1, x, 0:ey, :]
            + pltpu.roll(tz, nz - 1, 1)
            + tz
        )
        c_pp, c_ss, c_ps, c_sp, frac, mob, g_p, g_s = [raw[n, x] for n in range(STEP_NAMES)]
        den_a = c_pp + total
        den_b = c_ss + mob * total
        s_a = jnp.where(den_a > 0, OMEGA / den_a, 0.0)
        s_b = jnp.where(den_b > 0, OMEGA / den_b, 0.0)
        r_a = g_p + src[x]
        r_b = g_s
        if not first:
            r_a = r_a + acc[0, x] * fields[0, 0, x, 8 : 8 + ey, :]
            r_b = r_b + acc[1, x] * fields[0, 1, x, 8 : 8 + ey, :]
        coef[0, x] = s_a
        coef[1, x] = r_a
        coef[2, x] = c_sp + frac * total
        coef[3, x] = s_b * r_b
        coef[4, x] = s_b * c_ps
        coef[5, x] = s_b * mob
        if first:
            fields[1, 0, x, 8 : 8 + ey, :] = s_a * r_a
            fields[1, 1, x, 8 : 8 + ey, :] = s_b * r_b
        return 0

    lax.fori_loop(0, ex - 1, prepare, 0)

    def sweep(number):
        old, new = (number - 1) % 2, number % 2
        y0, y1 = (H, H + ry) if number == SWEEPS else (0, ey)

        def body(x, _):
            def gather(f):
                def at(i, shift):
                    return fields[old, f, i, 8 + y0 + shift : 8 + y1 + shift, :]

                centre = at(x, 0)
                return (
                    centre, at(x + 1, 0), at(x - 1, 0), at(x, 1), at(x, -1),
                    pltpu.roll(centre, nz - 1, 1), pltpu.roll(centre, 1, 1),
                )

            tz = geo[2, x, y0:y1, :]
            weights = (
                geo[0, x + 1, y0:y1, :], geo[0, x, y0:y1, :],
                geo[1, x, y0 + 1 : y1 + 1, :], geo[1, x, y0:y1, :],
                pltpu.roll(tz, nz - 1, 1), tz,
            )

            def around(values):
                total = weights[0] * values[1]
                for w, v in zip(weights[1:], values[2:]):
                    total = total + w * v
                return total

            va, vb = gather(0), gather(1)
            n_a, n_b = around(va), around(vb)
            a, b = va[0], vb[0]

            def co(n):
                return coef[n, x, y0:y1, :]

            frac = raw[4, x, y0:y1, :]
            fields[new, 0, x, 8 + y0 : 8 + y1, :] = (1.0 - OMEGA) * a + co(0) * (
                co(1) + n_a - co(2) * b + frac * n_b
            )
            fields[new, 1, x, 8 + y0 : 8 + y1, :] = (
                (1.0 - OMEGA) * b + co(3) - co(4) * a + co(5) * n_b
            )
            return 0

        lax.fori_loop(number, ex - number, body, 0)

    for number in range(2 if first else 1, SWEEPS + 1):
        sweep(number)

    end = SWEEPS % 2
    lo = 8 + H
    lam = [fields[end, f, H : H + rx, lo : lo + ry, :] for f in range(2)]
    if last:
        out_a[...] = lam[0]
        out_b[...] = lam[1]
    else:
        for f in range(2):
            out_lam[f] = lam[f]
            out_low[f] = fields[end, f, H : H + rx, lo : lo + H, :]
            out_high[f] = fields[end, f, H : H + rx, lo + ry - H : lo + ry, :]

    mix = (lam[0] + own[4][0] * lam[1]).reshape(rx * ry, nz)
    slot = table_ref[ids_ref[4]]
    cell = slot[1:2, :].astype(jnp.int32)
    well = slot[2:3, :].astype(jnp.int32)
    wi = slot[3:4, :]
    row = cell >> 7
    lane = cell & 127
    by_row = jnp.where(
        lax.broadcasted_iota(jnp.int32, (rx * ry, 128), 0) == row, 1.0, 0.0
    ).astype(f32)
    picked = lax.dot_general(
        mix, by_row, (((0,), (0,)), ((), ())), precision=HIGHEST, preferred_element_type=f32
    )
    sub = lax.broadcasted_iota(jnp.int32, (128, 128), 0)
    values = jnp.sum(jnp.where(sub == lane, picked, 0.0), axis=0, keepdims=True) * wi
    count = table_ref.shape[0]
    owner = well // wells
    column = (well - owner * wells) * steps + step
    spread = jnp.where(sub == column, values, 0.0)
    hot = jnp.where(
        lax.broadcasted_iota(jnp.int32, (count, 128), 0) == owner, 1.0, 0.0
    ).astype(f32)
    dense = lax.dot_general(
        hot, spread, (((1,), (1,)), ((), ())), precision=HIGHEST, preferred_element_type=f32
    )
    if not first:
        dense = dense + wells_in[...]
    out_wells[...] = dense


def whole(shape):
    return pl.BlockSpec(memory_space=pltpu.VMEM)


def run_step(first, last, step, steps, wells, ids, table, own, got, more, shapes):
    f32 = jnp.float32
    rx, ry, nz = shapes
    ex, ey = rx + 2 * H, ry + 2 * H
    vmem = pl.BlockSpec(memory_space=pltpu.VMEM)
    pick = pl.BlockSpec((1, rx, ry, nz), lambda i: (step, 0, 0, 0))
    in_specs = [pl.BlockSpec(memory_space=pltpu.SMEM), vmem] + [pick] * STEP_NAMES
    in_specs += [vmem] * (len(got) + len(more))
    sds = jax.ShapeDtypeStruct
    out_shape = []
    if first:
        out_shape.append(sds((3, ex, ey + 8, nz), f32))
    if last:
        out_shape += [sds((rx, ry, nz), f32)] * 2
    else:
        out_shape.append(sds((2, rx, ry, nz), f32))
        out_shape += [sds((2, rx, H, nz), f32)] * 2
        if not first:
            out_shape.append(sds((2, ex, ey, nz), f32))
    out_shape.append(sds((table.shape[0], 128), f32))
    return pl.pallas_call(
        functools.partial(step_kernel, first, last, step, steps, wells),
        grid=(1,),
        in_specs=in_specs,
        out_specs=[vmem] * len(out_shape),
        out_shape=out_shape,
        scratch_shapes=[
            pltpu.VMEM((STEP_NAMES, ex, ey, nz), f32),
            pltpu.VMEM((6, ex, ey, nz), f32),
            pltpu.VMEM((2, 2, ex, ey + 16, nz), f32),
            pltpu.VMEM((ex, ey, nz), f32),
        ],
        compiler_params=pltpu.CompilerParams(vmem_limit_bytes=48 * 1024 * 1024),
        name="step" + str(step),
    )(ids, table, *own, *got, *more)


def exchange(blocks):
    z_low = shifted(blocks[:, :, -H:, :], "gy", 1)
    z_high = shifted(blocks[:, :, :H, :], "gy", -1)
    return z_low, z_high, *exchange_x(blocks, z_low, z_high)


def exchange_x(blocks, z_low, z_high):
    rx = blocks.shape[1]
    x_low = shifted(
        jnp.concatenate([s[:, rx - H :] for s in (z_low, blocks, z_high)], axis=2), "gx", 1
    )
    x_high = shifted(
        jnp.concatenate([s[:, :H] for s in (z_low, blocks, z_high)], axis=2), "gx", -1
    )
    return x_low, x_high


def local(
    grad_p, grad_s, acc_p, acc_s, trans_x, trans_y, trans_z, c_pp, c_ss, c_ps, c_sp,
    frac, mobility, rate_mis, bhp_mis, control, perf_well, perf_cell, perf_wi,
):
    f32 = jnp.float32
    shapes = trans_x.shape
    rx, ry, nz = shapes
    steps = grad_p.shape[0]
    wells = rate_mis.shape[0]
    n_x, n_y = lax.axis_size("gx"), lax.axis_size("gy")
    devices = n_x * n_y
    gx_at, gy_at = lax.axis_index("gx"), lax.axis_index("gy")
    own = [c_pp, c_ss, c_ps, c_sp, frac, mobility, grad_p, grad_s]

    effective = jnp.where(control == 1, rate_mis, bhp_mis).reshape(1, wells * steps)
    effective = jnp.pad(effective, ((0, 0), (0, 128 - wells * steps)))
    mine = jnp.concatenate(
        [effective, perf_cell.astype(f32)[None], perf_well.astype(f32)[None], perf_wi[None]]
    )
    table = lax.all_to_all(
        jnp.broadcast_to(mine[None], (devices, 4, 128)), ("gx", "gy"), 0, 0, tiled=True
    )

    ids, live = [], []
    for dx in (-1, 0, 1):
        for dy in (-1, 0, 1):
            x, y = gx_at + dx, gy_at + dy
            inside = (x >= 0) & (x < n_x) & (y >= 0) & (y < n_y)
            ids.append(jnp.where(inside, x * n_y + y, 0))
            live.append(inside.astype(jnp.int32))
    ids = jnp.stack(ids + live + [gx_at, gy_at]).astype(jnp.int32)

    lam = None
    geo = acc = dense = None
    for step in reversed(range(steps)):
        first, last = step == steps - 1, step == 0
        group = [a[step] for a in own]
        if first:
            group = [trans_x, trans_y, trans_z] + group
        elif step == steps - 2:
            group = group + [acc_p, acc_s]
        got = exchange(jnp.stack(group))
        if first:
            more = [trans_x, trans_y, trans_z]
        else:
            lam_all, low, high = lam
            z_low = shifted(high, "gy", 1)
            z_high = shifted(low, "gy", -1)
            x_low, x_high = exchange_x(lam_all, z_low, z_high)
            more = [geo] + ([acc_p, acc_s] if step == steps - 2 else [acc])
            more += [lam_all, z_low, z_high, x_low, x_high, dense]
        outs = run_step(first, last, step, steps, wells, ids, table, own, got, more, shapes)
        if first:
            geo = outs[0]
            lam = outs[1:4]
        elif not last:
            lam = outs[0:3]
            acc = outs[3]
        dense = outs[-1]
    out_a, out_b = outs[0], outs[1]
    parts = lax.all_to_all(dense[:, None, :], ("gx", "gy"), 0, 0, tiled=True)
    well_grad = jnp.sum(parts, axis=(0, 1))[: wells * steps].reshape(wells, steps)
    return out_a, out_b, well_grad


def solution(mesh):
    cells3 = P("gx", "gy", None)
    cells4 = P(None, "gx", "gy", None)
    flat = ("gx", "gy")
    placed = (cells4,) * 2 + (cells3,) * 5 + (cells4,) * 6 + (P(flat, None),) * 3 + (P(flat),) * 3
    return jax.shard_map(
        local,
        mesh=mesh,
        in_specs=placed,
        out_specs=(cells3, cells3, P(flat, None)),
        check_vma=False,
    )
```

```python
import functools

import jax
import jax.numpy as jnp
from jax import lax
from jax.experimental import pallas as pl
from jax.experimental.pallas import tpu as pltpu
from jax.sharding import PartitionSpec as P

SWEEPS = 8
OMEGA = 0.8
KEEP = 1.0 - OMEGA
H = 8
V = 4
HIGHEST = lax.Precision.HIGHEST
F32 = jnp.float32
BF16 = jnp.bfloat16

VMEM = pl.BlockSpec(memory_space=pltpu.VMEM)
SMEM = pl.BlockSpec(memory_space=pltpu.SMEM)
ANY = pl.BlockSpec(memory_space=pl.ANY)


def sds(*shape):
    return jax.ShapeDtypeStruct(shape, F32)


def params():
    return pltpu.CompilerParams(vmem_limit_bytes=40 * 1024 * 1024)


def shifted(value, axis, by):
    length = lax.axis_size(axis)
    pairs = [(i, i + by) for i in range(length) if 0 <= i + by < length]
    return lax.ppermute(value, axis, pairs)


def copy_kernel(plan, n_in, *refs):
    ins, outs, sems = refs[:n_in], refs[n_in:-1], refs[-1]
    copies = [
        pltpu.make_async_copy(ins[i].at[s], outs[o].at[d], sems.at[k])
        for k, (i, s, o, d) in enumerate(plan)
    ]
    for c in copies:
        c.start()
    for c in copies:
        c.wait()


def copied(name, ins, plan, outs):
    return pl.pallas_call(
        functools.partial(copy_kernel, plan, len(ins)),
        in_specs=[ANY] * len(ins),
        out_specs=[ANY] * len(outs),
        out_shape=outs,
        scratch_shapes=[pltpu.SemaphoreType.DMA((len(plan),))],
        name=name,
    )(*ins)


def rows(at, size):
    return slice(at, at + size)


ALL = slice(None)


def pack_z(name, arrays, at, dims, after=()):
    rx, ry, nz = dims
    plan = []
    for n, lead in enumerate(at):
        pre = () if lead is None else (lead,)
        plan.append((n, pre + (ALL, rows(0, H)), 0, (n,)))
        plan.append((n, pre + (ALL, rows(ry - H, H)), 1, (n,)))
    count = len(arrays)
    return copied(name, list(arrays) + list(after), plan, [sds(count, rx, H, nz)] * 2)


def pack_x_edges(name, arrays, at, dims):
    rx, ry, nz = dims
    plan = []
    for n, lead in enumerate(at):
        pre = () if lead is None else (lead,)
        plan.append((n, pre + (rows(0, H),), 0, (n,)))
        plan.append((n, pre + (rows(rx - H, H),), 1, (n,)))
    return copied(name, arrays, plan, [sds(len(arrays), H, ry, nz)] * 2)


def pack_corners(name, z_low, z_high):
    count, rx, _, nz = z_low.shape
    plan = []
    for o, x in ((0, 0), (1, rx - H)):
        for i in (0, 1):
            plan.append((i, (ALL, rows(x, H)), o, (ALL, ALL, rows(i * H, H))))
    return copied(name, [z_low, z_high], plan, [sds(count, H, 2 * H, nz)] * 2)


def pack_x(name, arrays, at, z_low, z_high, dims):
    rx, ry, nz = dims
    count = z_low.shape[0]
    plan = []
    base = len(arrays)
    for o, x in ((0, 0), (1, rx - H)):
        plan.append((base, (ALL, rows(x, H)), o, (ALL, ALL, rows(0, H))))
        plan.append((base + 1, (ALL, rows(x, H)), o, (ALL, ALL, rows(H + ry, H))))
        if at is None:
            plan.append((0, (ALL, rows(x, H)), o, (ALL, ALL, rows(H, ry))))
        else:
            for n, lead in enumerate(at):
                pre = () if lead is None else (lead,)
                plan.append((n, pre + (rows(x, H),), o, (n, ALL, rows(H, ry))))
    return copied(
        name, list(arrays) + [z_low, z_high], plan, [sds(count, H, ry + 2 * H, nz)] * 2
    )


def source_kernel(steps, wells, ry, ids_ref, table_ref, src_ref):
    count = table_ref.shape[0]
    rx = src_ref.shape[1] // 3
    of_wells = table_ref[:, 0, :]
    owner_iota = lax.broadcasted_iota(jnp.int32, (count, 128), 0)
    sub = lax.broadcasted_iota(jnp.int32, (128, 128), 0)
    row_iota = lax.broadcasted_iota(jnp.int32, (rx * ry, 128), 0)

    def block(k, _):
        slot = table_ref[ids_ref[k]]
        cell = slot[1:2, :].astype(jnp.int32)
        well = slot[2:3, :].astype(jnp.int32)
        wi = slot[3:4, :] * ids_ref[9 + k].astype(F32)
        owner = well // wells
        within = well - owner * wells
        hot = jnp.where(owner_iota == owner, 1.0, 0.0).astype(F32)
        found = lax.dot_general(
            of_wells, hot, (((0,), (0,)), ((), ())), precision=HIGHEST,
            preferred_element_type=F32,
        )
        by_row = jnp.where(row_iota == (cell >> 7), 1.0, 0.0).astype(BF16)
        in_lane = sub == (cell & 127)
        dx = k // 3
        dy = k - 3 * dx
        for step in range(steps):
            value = jnp.zeros((1, 128), F32)
            for u in range(wells):
                c = u * steps + step
                value = value + jnp.where(within == u, found[c : c + 1, :], 0.0)
            value = value * wi
            part = None
            for _ in range(3):
                piece = value.astype(BF16)
                value = value - piece.astype(F32)
                by_lane = jnp.where(in_lane, piece.astype(F32), 0.0).astype(BF16)
                add = lax.dot_general(
                    by_row, by_lane, (((1,), (1,)), ((), ())), preferred_element_type=F32
                )
                part = add if part is None else part + add
            src_ref[
                step, pl.ds(pl.multiple_of(dx * rx, rx), rx),
                pl.ds(pl.multiple_of(dy * ry, ry), ry), :,
            ] = part.reshape(rx, ry, 128)
        return 0

    lax.fori_loop(0, 9, block, 0)


def by_v(ref, lead, x, offset=0):
    return jnp.stack(
        [ref[(*lead, x, pl.ds(offset + v, 8, stride=V), slice(None))] for v in range(V)]
    )


def up_v(value):
    return jnp.concatenate([value[1:], pltpu.roll(value[0], 7, 0)[None]])


def down_v(value):
    return jnp.concatenate([pltpu.roll(value[V - 1], 1, 0)[None], value[:-1]])


def roll_z(value, by):
    return pltpu.roll(value, by, 2)


def fill(dst, base, own, leads, z_low, z_high, x_low, x_high, corners, offset=0):
    count = len(own)
    rx, ry = own[0].shape[-3], own[0].shape[-2]

    def middle(x, _):
        for n in range(count):
            pre = () if leads[n] is None else (leads[n],)
            dst[base + n, H + x, 0:H, :] = z_low[offset + n, x]
            dst[base + n, H + x, H : H + ry, :] = own[n][pre + (x,)]
            dst[base + n, H + x, H + ry : 2 * H + ry, :] = z_high[offset + n, x]
        return 0

    lax.fori_loop(0, rx, middle, 0)

    def outer(x, _):
        for n in range(count):
            for at, edge, corner in (
                (x, x_low, corners and corners[0]),
                (H + rx + x, x_high, corners and corners[1]),
            ):
                if corner is None:
                    dst[base + n, at, :, :] = edge[offset + n, x]
                else:
                    dst[base + n, at, 0:H, :] = corner[offset + n, x, 0:H]
                    dst[base + n, at, H : H + ry, :] = edge[offset + n, x]
                    dst[base + n, at, H + ry : 2 * H + ry, :] = corner[offset + n, x, H : 2 * H]
        return 0

    lax.fori_loop(0, H, outer, 0)


SA, RA, PC, FR, RB, QC, MC, AA, AB = range(9)
TX, TY, TZ, TU, WS = range(5)


def coefficients(raw, base, src_ref, step, x, total, src_x, src_y):
    c_pp, c_ss, c_ps, c_sp, frac, mob, g_p, g_s = [by_v(raw, (base + n,), x) for n in range(8)]
    den_a = c_pp + total
    den_b = c_ss + mob * total
    s_a = jnp.where(den_a > 0, OMEGA / den_a, 0.0)
    s_b = jnp.where(den_b > 0, OMEGA / den_b, 0.0)
    r_a = g_p + by_v(src_ref, (step,), x + src_x, src_y)
    return s_a, r_a, c_sp + frac * total, frac, s_b * g_s, s_b * c_ps, s_b * mob, s_b


def sweeps(coef, geo, fields, lin, begin, ex):
    def sweep(number):
        old, new = (number - 1) % 2, number % 2

        def body(x, _):
            tx_up, tx_low = geo[TX, x + 1], geo[TX, x]
            ty_low = geo[TY, x]
            ty_up = up_v(ty_low)
            tz_low, tz_up = geo[TZ, x], geo[TU, x]

            def around(f):
                c = fields[old, f, x]
                total = tx_up * fields[old, f, x + 1] + tx_low * fields[old, f, x - 1]
                total = total + (ty_up * up_v(c) + ty_low * down_v(c))
                total = total + (tz_up * roll_z(c, 127) + tz_low * roll_z(c, 1))
                return c, total

            a, n_a = around(0)
            b, n_b = around(1)
            new_a = KEEP * a + coef[SA, x] * (
                (coef[RA, x] + n_a) + (coef[FR, x] * n_b - coef[PC, x] * b)
            )
            new_b = (KEEP * b + coef[RB, x]) + (coef[MC, x] * n_b - coef[QC, x] * a)
            if number == SWEEPS:
                for v in range(V):
                    lin[0, x, pl.ds(v, 8, stride=V), :] = new_a[v]
                    lin[1, x, pl.ds(v, 8, stride=V), :] = new_b[v]
            else:
                fields[new, 0, x] = new_a
                fields[new, 1, x] = new_b
            return 0

        lax.fori_loop(number, ex - number, body, 0, unroll=2)

    for number in range(begin, SWEEPS + 1):
        sweep(number)


def finish(last, step, steps, wells, lin, frac, ids_ref, table_ref, column_ref, before, outs):
    rx, ry, nz = frac.shape[-3:]
    out_wells = outs[-1]

    def copy(x, _):
        for f in range(2):
            row = lin[f, H + x, H : H + ry, :]
            if last:
                outs[f][x] = row
            else:
                outs[0][f, x] = row
                outs[1][f, x] = row[0:H]
                outs[2][f, x] = row[ry - H :]
        return 0

    lax.fori_loop(0, rx, copy, 0, unroll=2)
    mix = lin[0, H : H + rx, H : H + ry, :] + frac[0] * lin[1, H : H + rx, H : H + ry, :]
    mix = mix.reshape(rx * ry, nz)
    cell = column_ref[:, 1:2].astype(jnp.int32)
    by_row = jnp.where(
        lax.broadcasted_iota(jnp.int32, (128, rx * ry), 1) == (cell >> 7), 1.0, 0.0
    ).astype(BF16)
    picked = None
    for _ in range(3):
        piece = mix.astype(BF16)
        mix = mix - piece.astype(F32)
        add = jnp.dot(by_row, piece, preferred_element_type=F32)
        picked = add if picked is None else picked + add
    lane = lax.broadcasted_iota(jnp.int32, (128, 128), 1)
    values = jnp.sum(jnp.where(lane == (cell & 127), picked, 0.0), axis=1, keepdims=True)
    values = values * column_ref[:, 3:4]
    well = column_ref[:, 2:3].astype(jnp.int32)
    owner = well // wells
    spread = jnp.where(lane == (well - owner * wells) * steps + step, values, 0.0)
    flat = table_ref[ids_ref[4]][2:3, :].astype(jnp.int32) // wells
    count = table_ref.shape[0]
    hot = jnp.where(
        lax.broadcasted_iota(jnp.int32, (count, 128), 0) == flat, 1.0, 0.0
    ).astype(F32)
    dense = jnp.dot(hot, spread, precision=HIGHEST, preferred_element_type=F32)
    if before is not None:
        dense = dense + before[...]
    out_wells[...] = dense


def first_kernel(step, steps, wells, *refs):
    ids_ref, table_ref, column_ref, src_ref = refs[:4]
    own_geo, own = refs[4:7], refs[7:15]
    z_low, z_high, x_low, x_high, c_low, c_high = refs[15:21]
    geo = refs[21]
    outs = refs[22:26]
    raw, coef, fields, lin = refs[26:]
    rx, ry, nz = own[0].shape[-3:]
    ex = rx + 2 * H
    got = (z_low, z_high, x_low, x_high, (c_low, c_high))
    fill(raw, 0, own_geo + own, [None] * 3 + [0] * 8, *got)

    @pl.when(ids_ref[18] == 0)
    def _():
        raw[0, H, :, :] = jnp.zeros(raw.shape[2:], F32)

    @pl.when(ids_ref[19] == 0)
    def _():
        def clear(x, _):
            raw[1, x, H : H + 1, :] = jnp.zeros((1, nz), F32)
            return 0

        lax.fori_loop(0, ex, clear, 0)

    def geometry(x, _):
        lane = lax.broadcasted_iota(jnp.int32, (V, 8, nz), 2)
        tz = jnp.where(lane == 0, 0.0, by_v(raw, (2,), x))
        geo[TX, x] = by_v(raw, (0,), x)
        geo[TY, x] = by_v(raw, (1,), x)
        geo[TZ, x] = tz
        geo[TU, x] = roll_z(tz, 127)
        return 0

    lax.fori_loop(0, ex, geometry, 0)

    def prepare(x, _):
        ty = geo[TY, x]
        total = (
            (geo[TX, x + 1] + geo[TX, x]) + (up_v(ty) + ty) + (geo[TU, x] + geo[TZ, x])
        )
        geo[WS, x] = total
        s_a, r_a, p, frac, r_b, q, m, _ = coefficients(
            raw, 3, src_ref, step, x, total, rx - H, ry - H
        )
        coef[SA, x] = s_a
        coef[RA, x] = r_a
        coef[PC, x] = p
        coef[FR, x] = frac
        coef[RB, x] = r_b
        coef[QC, x] = q
        coef[MC, x] = m
        fields[1, 0, x] = s_a * r_a
        fields[1, 1, x] = r_b
        return 0

    lax.fori_loop(0, ex - 1, prepare, 0)
    sweeps(coef, geo, fields, lin, 2, ex)
    finish(False, step, steps, wells, lin, own[4], ids_ref, table_ref, column_ref, None, outs)


def prepare_kernel(step, with_acc, *refs):
    src_ref, geo = refs[:2]
    own = refs[2:10]
    at = 10
    acc = ()
    if with_acc:
        acc = refs[10:12]
        at = 12
    got = refs[at : at + 4]
    at += 4
    if not with_acc:
        acc_raw = refs[at]
        at += 1
    coef = refs[at]
    raw = refs[-1]
    rx, ry, nz = own[0].shape[-3:]
    ex = rx + 2 * H
    fill(raw, 0, own, [0] * 8, *got, None)
    if with_acc:
        acc_raw = refs[at + 1]
        fill(acc_raw, 0, acc, [None] * 2, *got, None, offset=8)

    def prepare(x, _):
        s_a, r_a, p, frac, r_b, q, m, s_b = coefficients(
            raw, 0, src_ref, step, x, geo[WS, x], rx - H, ry - H
        )
        coef[SA, x] = s_a
        coef[RA, x] = r_a
        coef[PC, x] = p
        coef[FR, x] = frac
        coef[RB, x] = r_b
        coef[QC, x] = q
        coef[MC, x] = m
        coef[AA, x] = by_v(acc_raw, (0,), x)
        coef[AB, x] = s_b * by_v(acc_raw, (1,), x)
        return 0

    lax.fori_loop(0, ex - 1, prepare, 0)


def sweep_kernel(last, step, steps, wells, *refs):
    ids_ref, table_ref, column_ref, coef, geo, frac, lam = refs[:7]
    got = refs[7:11]
    before = refs[11]
    outs = refs[12:-3]
    now, fields, lin = refs[-3:]
    rx, ry, nz = frac.shape[-3:]
    ex = rx + 2 * H
    fill(lin, 0, [lam.at[0], lam.at[1]], [None] * 2, *got, None)

    def begin(x, _):
        a, b = by_v(lin, (0,), x), by_v(lin, (1,), x)
        fields[0, 0, x] = a
        fields[0, 1, x] = b
        now[0, x] = coef[RA, x] + coef[AA, x] * a
        now[1, x] = coef[RB, x] + coef[AB, x] * b
        return 0

    lax.fori_loop(0, ex, begin, 0)

    class Joined:
        def __getitem__(self, at):
            n, x = at
            return now[0, x] if n == RA else now[1, x] if n == RB else coef[n, x]

    sweeps(Joined(), geo, fields, lin, 1, ex)
    finish(last, step, steps, wells, lin, frac, ids_ref, table_ref, column_ref, before, outs)


def local(
    grad_p, grad_s, acc_p, acc_s, trans_x, trans_y, trans_z, c_pp, c_ss, c_ps, c_sp,
    frac, mobility, rate_mis, bhp_mis, control, perf_well, perf_cell, perf_wi,
):
    dims = rx, ry, nz = trans_x.shape
    ex, ey = rx + 2 * H, ry + 2 * H
    steps = grad_p.shape[0]
    wells = rate_mis.shape[0]
    n_x, n_y = lax.axis_size("gx"), lax.axis_size("gy")
    devices = n_x * n_y
    gx_at, gy_at = lax.axis_index("gx"), lax.axis_index("gy")
    own = [c_pp, c_ss, c_ps, c_sp, frac, mobility, grad_p, grad_s]
    geo_own = [trans_x, trans_y, trans_z]
    top = steps - 1

    def sent(low, high, axis):
        return shifted(high, axis, 1), shifted(low, axis, -1)

    group = geo_own + own
    at = [None] * 3 + [top] * 8
    z_got = sent(*pack_z("pack_z2", group, at, dims), "gy")
    x_got = sent(*pack_x_edges("pack_x2", group, at, dims), "gx")

    effective = jnp.where(control == 1, rate_mis, bhp_mis).reshape(1, wells * steps)
    effective = jnp.pad(effective, ((0, 0), (0, 128 - wells * steps)))
    mine = jnp.concatenate(
        [effective, perf_cell.astype(F32)[None], perf_well.astype(F32)[None], perf_wi[None]]
    )
    table = lax.all_to_all(
        jnp.broadcast_to(mine[None], (devices, 4, 128)), ("gx", "gy"), 0, 0, tiled=True
    )
    column = mine.T

    ids, live = [], []
    for dx in (-1, 0, 1):
        for dy in (-1, 0, 1):
            x, y = gx_at + dx, gy_at + dy
            inside = (x >= 0) & (x < n_x) & (y >= 0) & (y < n_y)
            ids.append(jnp.where(inside, x * n_y + y, 0))
            live.append(inside.astype(jnp.int32))
    ids = jnp.stack(ids + live + [gx_at, gy_at]).astype(jnp.int32)

    src = pl.pallas_call(
        functools.partial(source_kernel, steps, wells, ry),
        in_specs=[SMEM, VMEM],
        out_specs=VMEM,
        out_shape=sds(steps, 3 * rx, 3 * ry, nz),
        compiler_params=params(),
        name="sources",
    )(ids, table)

    c_got = sent(*pack_corners("pack_c2", *z_got), "gx")

    def pick(step):
        return pl.BlockSpec((1, rx, ry, nz), lambda i: (step, 0, 0, 0))

    ext = (ex, V, 8, nz)
    lam_out = [sds(2, rx, ry, nz), sds(2, rx, H, nz), sds(2, rx, H, nz)]
    well_out = sds(devices, 128)

    geo, lam, low, high, dense = pl.pallas_call(
        functools.partial(first_kernel, top, steps, wells),
        grid=(1,),
        in_specs=[SMEM] + [VMEM] * 6 + [pick(top)] * 8 + [VMEM] * 6,
        out_specs=[VMEM] * 5,
        out_shape=[sds(5, *ext)] + lam_out + [well_out],
        scratch_shapes=[
            pltpu.VMEM((11, ex, ey, nz), F32),
            pltpu.VMEM((7, *ext), F32),
            pltpu.VMEM((2, 2, *ext), F32),
            pltpu.VMEM((2, ex, ey, nz), F32),
        ],
        compiler_params=params(),
        name="step_top",
    )(ids, table, column, src, *geo_own, *own, *z_got, *x_got, *c_got)

    acc_raw = None
    after = z_got
    for step in reversed(range(top)):
        last = step == 0
        with_acc = step == top - 1
        group = own + ([acc_p, acc_s] if with_acc else [])
        at = [step] * 8 + ([None] * 2 if with_acc else [])
        g_z = sent(*pack_z("pack_z", group, at, dims, after), "gy")
        g_x = sent(*pack_x("pack_x", group, at, *g_z, dims), "gx")
        after = g_z

        outs = [sds(9, *ext)] + ([sds(2, ex, ey, nz)] if with_acc else [])
        made = pl.pallas_call(
            functools.partial(prepare_kernel, step, with_acc),
            grid=(1,),
            in_specs=[VMEM] * 2 + [pick(step)] * 8 + [VMEM] * (6 if with_acc else 5),
            out_specs=[VMEM] * len(outs),
            out_shape=outs,
            scratch_shapes=[pltpu.VMEM((8, ex, ey, nz), F32)],
            compiler_params=params(),
            name="prepare",
        )(src, geo, *own, *((acc_p, acc_s) if with_acc else ()), *g_z, *g_x,
          *(() if with_acc else (acc_raw,)))
        coef = made[0]
        if with_acc:
            acc_raw = made[1]

        l_z = sent(low, high, "gy")
        l_x = sent(*pack_x("pack_lam", [lam], None, *l_z, dims), "gx")
        outs = [sds(rx, ry, nz)] * 2 if last else lam_out
        outs = pl.pallas_call(
            functools.partial(sweep_kernel, last, step, steps, wells),
            grid=(1,),
            in_specs=[SMEM] + [VMEM] * 4 + [pick(step)] + [VMEM] * 6,
            out_specs=[VMEM] * (len(outs) + 1),
            out_shape=outs + [well_out],
            scratch_shapes=[
                pltpu.VMEM((2, *ext), F32),
                pltpu.VMEM((2, 2, *ext), F32),
                pltpu.VMEM((2, ex, ey, nz), F32),
            ],
            compiler_params=params(),
            name="step",
        )(ids, table, column, coef, geo, frac, lam, *l_z, *l_x, dense)
        dense = outs[-1]
        if not last:
            lam, low, high = outs[:3]

    parts = lax.all_to_all(dense[:, None, :], ("gx", "gy"), 0, 0, tiled=True)
    well_grad = jnp.sum(parts, axis=(0, 1))[: wells * steps].reshape(wells, steps)
    return outs[0], outs[1], well_grad


def solution(mesh):
    cells3 = P("gx", "gy", None)
    cells4 = P(None, "gx", "gy", None)
    flat = ("gx", "gy")
    placed = (cells4,) * 2 + (cells3,) * 5 + (cells4,) * 6 + (P(flat, None),) * 3 + (P(flat),) * 3
    return jax.shard_map(
        local,
        mesh=mesh,
        in_specs=placed,
        out_specs=(cells3, cells3, P(flat, None)),
        check_vma=False,
    )
```

```python
import functools

import jax
import jax.numpy as jnp
from jax import lax
from jax.experimental import pallas as pl
from jax.experimental.pallas import tpu as pltpu
from jax.sharding import PartitionSpec as P

SWEEPS = 8
OMEGA = 0.8
KEEP = 1.0 - OMEGA
H = 8
V = 4
HIGHEST = lax.Precision.HIGHEST
F32 = jnp.float32
BF16 = jnp.bfloat16

VMEM = pl.BlockSpec(memory_space=pltpu.VMEM)
ANY = pl.BlockSpec(memory_space=pl.ANY)
HBM = pl.BlockSpec(memory_space=pltpu.HBM)


def sds(*shape):
    return jax.ShapeDtypeStruct(shape, F32)


def params(mib):
    return pltpu.CompilerParams(vmem_limit_bytes=mib * 1024 * 1024)


def call(kernel, ins, outs, name, mib, specs=None, scratch=()):
    return pl.pallas_call(
        kernel,
        in_specs=specs or [VMEM] * len(ins),
        out_specs=[VMEM] * len(outs),
        out_shape=outs,
        scratch_shapes=list(scratch),
        compiler_params=params(mib),
        name=name,
    )(*ins)


def shifted(value, axis, by):
    length = lax.axis_size(axis)
    pairs = [(i, i + by) for i in range(length) if 0 <= i + by < length]
    return lax.ppermute(value, axis, pairs)


def load_kernel(leads, split, *refs):
    count = len(leads)
    ins, (top, rest, y_low, y_high, x_low, x_high), sems = refs[:count], refs[count:-1], refs[-1]
    rx, ry = top.shape[1:3]
    copies = []
    for n, lead in enumerate(leads):
        to = top.at[n] if n < split else rest.at[n - split]
        copies.append(
            pltpu.make_async_copy(
                ins[n] if lead is None else ins[n].at[lead], to, sems.at[n]
            )
        )
    for c in copies:
        c.start()
    for c in copies[:split]:
        c.wait()
    edges_body(top, y_low, y_high, x_low, x_high)
    for c in copies[split:]:
        c.wait()


def edges_body(own, y_low, y_high, x_low, x_high):
    rx, ry = own.shape[1:3]

    def one(n, _):
        y_low[n] = own[n, :, 0:H, :]
        y_high[n] = own[n, :, ry - H :, :]
        x_low[n] = own[n, 0:H]
        x_high[n] = own[n, rx - H :]
        return 0

    lax.fori_loop(0, own.shape[0], one, 0)


def edge_shapes(n, dims):
    rx, ry, nz = dims
    return [sds(n, rx, H, nz)] * 2 + [sds(n, H, ry, nz)] * 2


def load(arrays, leads, split, dims):
    n = len(leads)
    return pl.pallas_call(
        functools.partial(load_kernel, leads, split),
        in_specs=[HBM] * n,
        out_specs=[VMEM] * 6,
        out_shape=[sds(split, *dims), sds(n - split, *dims)] + edge_shapes(split, dims),
        scratch_shapes=[pltpu.SemaphoreType.DMA((n,))],
        name="load",
    )(*arrays)


def edges_kernel(own, *refs):
    edges_body(own, *refs[-4:])


def fold(rows_of, high):
    tiles = []
    for dx in range(1, 5):
        near, far = rows_of(dx), rows_of(8 - dx)
        sub = lax.broadcasted_iota(jnp.int32, near.shape, 0)
        if high:
            tiles.append(jnp.where(sub < 8 - dx, near, pltpu.roll(far, 8 - dx, 0)))
        else:
            tiles.append(jnp.where(sub >= dx, near, pltpu.roll(far, dx, 0)))
    return tiles


def unfold(tile, dx, high):
    return tile, pltpu.roll(tile, dx if high else 8 - dx, 0)


def corner_tiles(n, z_low, z_high, put):
    rx = z_low.shape[1]
    for side in (0, 1):
        for high, z in ((False, z_low), (True, z_high)):

            def rows_of(dx):
                return z[n, dx - 1 if side == 0 else rx - dx]

            for t, tile in enumerate(fold(rows_of, high)):
                put(side, int(high), t, tile)


def corner_kernel(z_low, z_high, *refs):
    outs = refs[-2:]

    def one(n, _):
        def put(side, y, t, tile):
            outs[side][n, t, y * H : (y + 1) * H, :] = tile

        corner_tiles(n, z_low, z_high, put)
        return 0

    lax.fori_loop(0, z_low.shape[0], one, 0)


def pack_corners(name, z_low, z_high, after):
    count, _, _, nz = z_low.shape
    return call(
        corner_kernel, [z_low, z_high, *after], [sds(count, 4, 2 * H, nz)] * 2, name, 4,
        [VMEM] * 2 + [ANY] * len(after),
    )


def widen_kernel(own, z_low, z_high, *outs):
    rx = own.shape[1]

    def one(n, _):
        def put(side, y, t, tile):
            outs[side][n, H + t, y * H : (y + 1) * H, :] = tile

        corner_tiles(n, z_low, z_high, put)
        outs[0][n, 0:H] = own[n, 0:H]
        outs[1][n, 0:H] = own[n, rx - H :]
        return 0

    lax.fori_loop(0, own.shape[0], one, 0)


def widen(own, z_low, z_high):
    count, rx, ry, nz = own.shape
    return call(widen_kernel, [own, z_low, z_high], [sds(count, H + 4, ry, nz)] * 2, "widen", 4)


def table_kernel(steps, rate, bhp, control, perf_well, perf_cell, perf_wi, _, out):
    wells = rate.shape[0]
    effective = jnp.where(control[...] == 1, rate[...], bhp[...])
    lane = lax.broadcasted_iota(jnp.int32, (1, 128), 1)
    row = jnp.zeros((1, 128), F32)
    for u in range(wells):
        for n in range(steps):
            row = jnp.where(lane == u * steps + n, effective[u : u + 1, n : n + 1], row)
    mine = jnp.concatenate(
        [row, perf_cell[...].astype(F32), perf_well[...].astype(F32), perf_wi[...]]
    )
    out[...] = jnp.broadcast_to(mine[None], out.shape)


def spot():
    n_x, n_y = lax.axis_size("gx"), lax.axis_size("gy")
    x, y = lax.axis_index("gx"), lax.axis_index("gy")
    return x, y, n_x, n_y


def source_kernel(steps, wells, ry, table_ref, src_ref):
    here_x, here_y, n_x, n_y = spot()
    count = table_ref.shape[0]
    rx = src_ref.shape[1] // 3
    of_wells = table_ref[:, 0, :]
    owner_iota = lax.broadcasted_iota(jnp.int32, (count, 128), 0)
    sub = lax.broadcasted_iota(jnp.int32, (128, 128), 0)
    row_iota = lax.broadcasted_iota(jnp.int32, (rx * ry, 128), 0)

    def block(k, _):
        dx = k // 3
        dy = k - 3 * dx
        at_x, at_y = here_x + dx - 1, here_y + dy - 1
        inside = (at_x >= 0) & (at_x < n_x) & (at_y >= 0) & (at_y < n_y)
        slot = table_ref[jnp.where(inside, at_x * n_y + at_y, 0)]
        cell = slot[1:2, :].astype(jnp.int32)
        well = slot[2:3, :].astype(jnp.int32)
        wi = slot[3:4, :] * inside.astype(F32)
        owner = well // wells
        within = well - owner * wells
        hot = jnp.where(owner_iota == owner, 1.0, 0.0).astype(F32)
        found = lax.dot_general(
            of_wells, hot, (((0,), (0,)), ((), ())), precision=HIGHEST,
            preferred_element_type=F32,
        )
        by_row = jnp.where(row_iota == (cell >> 7), 1.0, 0.0).astype(BF16)
        in_lane = sub == (cell & 127)
        for step in range(steps):
            value = jnp.zeros((1, 128), F32)
            for u in range(wells):
                c = u * steps + step
                value = value + jnp.where(within == u, found[c : c + 1, :], 0.0)
            value = value * wi
            part = None
            for _ in range(3):
                piece = value.astype(BF16)
                value = value - piece.astype(F32)
                by_lane = jnp.where(in_lane, piece.astype(F32), 0.0).astype(BF16)
                add = lax.dot_general(
                    by_row, by_lane, (((1,), (1,)), ((), ())), preferred_element_type=F32
                )
                part = add if part is None else part + add
            src_ref[
                step, pl.ds(pl.multiple_of(dx * rx, rx), rx),
                pl.ds(pl.multiple_of(dy * ry, ry), ry), :,
            ] = part.reshape(rx, ry, 128)
        return 0

    lax.fori_loop(0, 9, block, 0)


def by_v(ref, lead, x, offset=0):
    return jnp.stack(
        [ref[(*lead, x, pl.ds(offset + v, 8, stride=V), slice(None))] for v in range(V)]
    )


def up_v(value):
    return jnp.concatenate([value[1:], pltpu.roll(value[0], 7, 0)[None]])


def down_v(value):
    return jnp.concatenate([pltpu.roll(value[V - 1], 1, 0)[None], value[:-1]])


def roll_z(value, by):
    return pltpu.roll(value, by, 2)


def fill(dst, own, z_low, z_high, x_edges, corners, base, first=0):
    count, (rx, ry, nz) = dst.shape[0], own.shape[1:]

    def one(n, _):
        m = n + first
        dst[n, H : H + rx, 0:H, :] = z_low[m]
        dst[n, H : H + rx, H : H + ry, :] = own[m]
        dst[n, H : H + rx, H + ry : 2 * H + ry, :] = z_high[m]
        for side in (0, 1):
            at = side * (H + rx)
            dst[n, at : at + H, H : H + ry, :] = x_edges[side][m, 0:H]
            for y in (0, 1):
                to = y * (H + ry)
                for t in range(4):
                    tile = corners[side][m, base + t, y * H : (y + 1) * H, :]
                    near, far = unfold(tile, t + 1, y == 1)
                    for dx, row in ((t + 1, near), (7 - t, far)):
                        x = H - dx if side == 0 else H + rx + dx - 1
                        dst[n, x, to : to + H, :] = row
                x = 0 if side == 0 else 2 * H + rx - 1
                dst[n, x, to : to + H, :] = jnp.zeros((H, nz), F32)
        return 0

    lax.fori_loop(0, count, one, 0)


SA, RA, PC, FR, RB, QC, MC, AA, AB = range(9)
TX, TY, TZ, TU, WS = range(5)


def coefficients(raw, base, src_ref, step, x, total, src_x, src_y):
    c_pp, c_ss, c_ps, c_sp, frac, mob, g_p, g_s = [by_v(raw, (base + n,), x) for n in range(8)]
    den_a = c_pp + total
    den_b = c_ss + mob * total
    s_a = jnp.where(den_a > 0, OMEGA / den_a, 0.0)
    s_b = jnp.where(den_b > 0, OMEGA / den_b, 0.0)
    r_a = g_p + by_v(src_ref, (step,), x + src_x, src_y)
    return s_a, r_a, c_sp + frac * total, frac, s_b * g_s, s_b * c_ps, s_b * mob, s_b


BLOCK = 2
UNROLL = 4


def sweeps(coef, geo, bufs, lin, begin, ex):
    def work(number, x, count):
        old, new = bufs[(number - 1) % 2], bufs[number % 2]
        tx = [geo[TX, x + r] for r in range(count + 1)]
        values = [[old[f][x - 1 + r] for r in range(count + 2)] for f in range(2)]
        results = []
        for r in range(count):
            at = x + r
            ty = geo[TY, at]
            ty_up = up_v(ty)
            tz, tz_up = geo[TZ, at], geo[TU, at]

            def around(v):
                c = v[r + 1]
                total = tx[r + 1] * v[r + 2] + tx[r] * v[r]
                total = total + (ty_up * up_v(c) + ty * down_v(c))
                total = total + (tz_up * roll_z(c, 127) + tz * roll_z(c, 1))
                return c, total

            a, n_a = around(values[0])
            b, n_b = around(values[1])
            new_a = KEEP * a + coef[SA, at] * (
                (coef[RA, at] + n_a) + (coef[FR, at] * n_b - coef[PC, at] * b)
            )
            new_b = (KEEP * b + coef[RB, at]) + (coef[MC, at] * n_b - coef[QC, at] * a)
            results.append((new_a, new_b))
        for r in range(count):
            for f in range(2):
                if number == SWEEPS:
                    for v in range(V):
                        lin[f, x + r, pl.ds(v, 8, stride=V), :] = results[r][f][v]
                else:
                    new[f][x + r] = results[r][f]

    for number in range(begin, SWEEPS + 1):
        size = BLOCK * UNROLL
        total = ex - 2 * number

        def many(i, _):
            for u in range(UNROLL):
                work(number, number + i * size + u * BLOCK, BLOCK)
            return 0

        lax.fori_loop(0, total // size, many, 0)
        for at in range(total - total % size, total, BLOCK):
            work(number, number + at, BLOCK)


def finish(last, step, steps, wells, lin, frac, table_ref, before, outs):
    rx, ry, nz = frac.shape[-3:]
    out_wells = outs[-1]

    def copy(x, _):
        for f in range(2):
            row = lin[f, H + x, H : H + ry, :]
            if last:
                outs[f][x] = row
            else:
                outs[0][f, x] = row
                outs[1][f, x] = row[0:H]
                outs[2][f, x] = row[ry - H :]
        return 0

    lax.fori_loop(0, rx, copy, 0, unroll=2)
    mix = lin[0, H : H + rx, H : H + ry, :] + frac[...] * lin[1, H : H + rx, H : H + ry, :]
    mix = mix.reshape(rx * ry, nz)
    here_x, here_y, _, n_y = spot()
    slot = table_ref[here_x * n_y + here_y]
    lane = lax.broadcasted_iota(jnp.int32, (128, 128), 1)
    diagonal = lax.broadcasted_iota(jnp.int32, (128, 128), 0) == lane

    def upright(row):
        return jnp.sum(jnp.where(diagonal, row, 0.0), axis=1, keepdims=True)

    cell = upright(slot[1:2, :]).astype(jnp.int32)
    well = upright(slot[2:3, :]).astype(jnp.int32)
    wi = upright(slot[3:4, :])
    by_row = jnp.where(
        lax.broadcasted_iota(jnp.int32, (128, rx * ry), 1) == (cell >> 7), 1.0, 0.0
    ).astype(BF16)
    picked = None
    for _ in range(3):
        piece = mix.astype(BF16)
        mix = mix - piece.astype(F32)
        add = jnp.dot(by_row, piece, preferred_element_type=F32)
        picked = add if picked is None else picked + add
    values = jnp.sum(jnp.where(lane == (cell & 127), picked, 0.0), axis=1, keepdims=True)
    values = values * wi
    owner = well // wells
    spread = jnp.where(lane == (well - owner * wells) * steps + step, values, 0.0)
    flat = slot[2:3, :].astype(jnp.int32) // wells
    count = table_ref.shape[0]
    hot = jnp.where(
        lax.broadcasted_iota(jnp.int32, (count, 128), 0) == flat, 1.0, 0.0
    ).astype(F32)
    dense = jnp.dot(hot, spread, precision=HIGHEST, preferred_element_type=F32)
    if before is not None:
        dense = dense + before[...]
    out_wells[...] = dense


def first_kernel(step, steps, wells, *refs):
    table_ref, src_ref, own, z_low, z_high, x_low, x_high, c_low, c_high = refs[:9]
    geo = refs[9]
    outs = refs[10:14]
    raw, coef, fa0, fb0, fa1, fb1, lin = refs[14:]
    rx, ry, nz = own.shape[1:]
    ex = rx + 2 * H
    fill(raw, own, z_low, z_high, (x_low, x_high), (c_low, c_high), 0)
    here_x, here_y, _, _ = spot()

    @pl.when(here_x == 0)
    def _():
        raw[0, H, :, :] = jnp.zeros(raw.shape[2:], F32)

    @pl.when(here_y == 0)
    def _():
        def clear(x, _):
            raw[1, x, H : H + 1, :] = jnp.zeros((1, nz), F32)
            return 0

        lax.fori_loop(0, ex, clear, 0)

    def geometry(x, _):
        lane = lax.broadcasted_iota(jnp.int32, (V, 8, nz), 2)
        tz = jnp.where(lane == 0, 0.0, by_v(raw, (2,), x))
        geo[TX, x] = by_v(raw, (0,), x)
        geo[TY, x] = by_v(raw, (1,), x)
        geo[TZ, x] = tz
        geo[TU, x] = roll_z(tz, 127)
        return 0

    lax.fori_loop(0, ex, geometry, 0, unroll=4)

    def prepare(x, _):
        ty = geo[TY, x]
        total = (
            (geo[TX, x + 1] + geo[TX, x]) + (up_v(ty) + ty) + (geo[TU, x] + geo[TZ, x])
        )
        geo[WS, x] = total
        s_a, r_a, p, frac, r_b, q, m, _ = coefficients(
            raw, 3, src_ref, step, x, total, rx - H, ry - H
        )
        coef[SA, x] = s_a
        coef[RA, x] = r_a
        coef[PC, x] = p
        coef[FR, x] = frac
        coef[RB, x] = r_b
        coef[QC, x] = q
        coef[MC, x] = m
        fa1[x] = s_a * r_a
        fb1[x] = r_b
        return 0

    lax.fori_loop(0, ex - 1, prepare, 0)
    sweeps(coef, geo, ((fa0, fb0), (fa1, fb1)), lin, 2, ex)
    finish(False, step, steps, wells, lin, own.at[7], table_ref, None, outs)


def prepare_kernel(step, first, with_acc, *refs):
    src_ref, geo, own, z_low, z_high, x_low, x_high, c_low, c_high = refs[:9]
    if with_acc:
        coef, acc_out, raw = refs[9:]
    else:
        acc, coef, raw = refs[9:]
    rx, ry, nz = own.shape[1:]
    ex = rx + 2 * H
    fill(raw, own, z_low, z_high, (x_low, x_high), (c_low, c_high), 0, first)

    def prepare(x, _):
        s_a, r_a, p, frac, r_b, q, m, s_b = coefficients(
            raw, 0, src_ref, step, x, geo[WS, x], rx - H, ry - H
        )
        coef[SA, x] = s_a
        coef[RA, x] = r_a
        coef[PC, x] = p
        coef[FR, x] = frac
        coef[RB, x] = r_b
        coef[QC, x] = q
        coef[MC, x] = m
        if with_acc:
            a, b = by_v(raw, (8,), x), by_v(raw, (9,), x)
            acc_out[0, x] = a
            acc_out[1, x] = b
        else:
            a, b = acc[0, x], acc[1, x]
        coef[AA, x] = a
        coef[AB, x] = s_b * b
        return 0

    lax.fori_loop(0, ex - 1, prepare, 0)


def sweep_kernel(last, step, frac_at, steps, wells, *refs):
    table_ref, coef, geo, own, lam, z_low, z_high, x_low, x_high, before = refs[:10]
    outs = refs[10:-6]
    now, fa0, fb0, fa1, fb1, lin = refs[-6:]
    rx, ry, nz = own.shape[1:]
    ex = rx + 2 * H
    fill(lin, lam, z_low, z_high, (x_low, x_high), (x_low, x_high), H)

    def begin(x, _):
        a, b = by_v(lin, (0,), x), by_v(lin, (1,), x)
        fa0[x] = a
        fb0[x] = b
        now[0, x] = coef[RA, x] + coef[AA, x] * a
        now[1, x] = coef[RB, x] + coef[AB, x] * b
        return 0

    lax.fori_loop(0, ex, begin, 0, unroll=4)

    class Joined:
        def __getitem__(self, at):
            n, x = at
            return now[0, x] if n == RA else now[1, x] if n == RB else coef[n, x]

    sweeps(Joined(), geo, ((fa0, fb0), (fa1, fb1)), lin, 1, ex)
    finish(last, step, steps, wells, lin, own.at[frac_at], table_ref, before, outs)


def local(
    grad_p, grad_s, acc_p, acc_s, trans_x, trans_y, trans_z, c_pp, c_ss, c_ps, c_sp,
    frac, mobility, rate_mis, bhp_mis, control, perf_well, perf_cell, perf_wi,
):
    dims = rx, ry, nz = trans_x.shape
    ex, ey = rx + 2 * H, ry + 2 * H
    steps = grad_p.shape[0]
    wells = rate_mis.shape[0]
    devices = lax.axis_size("gx") * lax.axis_size("gy")
    own = [c_pp, c_ss, c_ps, c_sp, frac, mobility, grad_p, grad_s]
    top = steps - 1

    def sent(low, high, axis):
        return shifted(high, axis, 1), shifted(low, axis, -1)

    arrays = [trans_x, trans_y, trans_z] + own
    leads = [None] * 3 + [top] * 8
    split = len(arrays)
    places = {}
    for step in reversed(range(top)):
        places[step] = len(arrays) - split
        arrays += own
        leads += [step] * 8
        if step == top - 1:
            arrays += [acc_p, acc_s]
            leads += [None] * 2
    blocks, more, y_low, y_high, e_low, e_high = load(arrays, leads, split, dims)

    z_got = sent(y_low, y_high, "gy")
    x_got = sent(e_low, e_high, "gx")

    mine = call(
        functools.partial(table_kernel, steps),
        [rate_mis, bhp_mis, control] + [p[None] for p in (perf_well, perf_cell, perf_wi)]
        + [y_low], [sds(devices, 4, 128)], "table", 4, [VMEM] * 6 + [ANY],
    )[0]
    table = lax.all_to_all(mine, ("gx", "gy"), 0, 0, tiled=True)
    src = call(
        functools.partial(source_kernel, steps, wells, ry), [table],
        [sds(steps, 3 * rx, 3 * ry, nz)], "sources", 8,
    )[0]

    corners = pack_corners("corners", *z_got, (*x_got, table))
    c_got = sent(*corners, "gx")

    edges = call(
        edges_kernel, [more, *corners, src], edge_shapes(len(arrays) - split, dims), "edges", 4,
        [VMEM] + [ANY] * 3,
    )
    m_z = sent(*edges[:2], "gy")
    m_x = sent(*edges[2:], "gx")

    ext = (ex, V, 8, nz)
    lam_out = [sds(2, rx, ry, nz), sds(2, rx, H, nz), sds(2, rx, H, nz)]
    well_out = sds(devices, 128)
    fields = [pltpu.VMEM(ext, F32)] * 4 + [pltpu.VMEM((2, ex, ey, nz), F32)]

    geo, lam, low, high, dense = call(
        functools.partial(first_kernel, top, steps, wells),
        [table, src, blocks, *z_got, *x_got, *c_got],
        [sds(5, *ext)] + lam_out + [well_out], "step_top", 16,
        scratch=[pltpu.VMEM((split, ex, ey, nz), F32), pltpu.VMEM((7, *ext), F32)] + fields,
    )

    m_c = sent(*pack_corners("corners_more", *m_z, (low,)), "gx")

    acc = None
    for step in reversed(range(top)):
        last = step == 0
        with_acc = step == top - 1
        at = places[step]
        made = call(
            functools.partial(prepare_kernel, step, at, with_acc),
            [src, geo, more, *m_z, *m_x, *m_c] + ([] if with_acc else [acc]),
            [sds(9, *ext)] + ([sds(2, *ext)] if with_acc else []), "prepare", 8,
            scratch=[pltpu.VMEM((10 if with_acc else 8, ex, ey, nz), F32)],
        )
        coef = made[0]
        if with_acc:
            acc = made[1]

        l_z = sent(low, high, "gy")
        l_x = sent(*widen(lam, *l_z), "gx")
        outs = [sds(rx, ry, nz)] * 2 if last else lam_out
        outs = call(
            functools.partial(sweep_kernel, last, step, at + 4, steps, wells),
            [table, coef, geo, more, lam, *l_z, *l_x, dense],
            outs + [well_out], "step", 8, scratch=[pltpu.VMEM((2, *ext), F32)] + fields,
        )
        dense = outs[-1]
        if not last:
            lam, low, high = outs[:3]

    parts = lax.all_to_all(dense[:, None, :], ("gx", "gy"), 0, 0, tiled=True)
    well_grad = jnp.sum(parts, axis=(0, 1))[: wells * steps].reshape(wells, steps)
    return outs[0], outs[1], well_grad


def solution(mesh):
    cells3 = P("gx", "gy", None)
    cells4 = P(None, "gx", "gy", None)
    flat = ("gx", "gy")
    placed = (cells4,) * 2 + (cells3,) * 5 + (cells4,) * 6 + (P(flat, None),) * 3 + (P(flat),) * 3
    return jax.shard_map(
        local,
        mesh=mesh,
        in_specs=placed,
        out_specs=(cells3, cells3, P(flat, None)),
        check_vma=False,
    )
```

```python
import functools

import jax
import jax.numpy as jnp
from jax import lax
from jax.experimental import pallas as pl
from jax.experimental.pallas import tpu as pltpu
from jax.sharding import PartitionSpec as P

SWEEPS = 8
OMEGA = 0.8
KEEP = 1.0 - OMEGA
H = 8
V = 4
HIGHEST = lax.Precision.HIGHEST
F32 = jnp.float32
BF16 = jnp.bfloat16

VMEM = pl.BlockSpec(memory_space=pltpu.VMEM)
ANY = pl.BlockSpec(memory_space=pl.ANY)
HBM = pl.BlockSpec(memory_space=pltpu.HBM)


def sds(*shape):
    return jax.ShapeDtypeStruct(shape, F32)


def params(mib):
    return pltpu.CompilerParams(vmem_limit_bytes=mib * 1024 * 1024)


def call(kernel, ins, outs, name, mib, specs=None, scratch=()):
    return pl.pallas_call(
        kernel,
        in_specs=specs or [VMEM] * len(ins),
        out_specs=[VMEM] * len(outs),
        out_shape=outs,
        scratch_shapes=list(scratch),
        compiler_params=params(mib),
        name=name,
    )(*ins)


def shifted(value, axis, by):
    length = lax.axis_size(axis)
    pairs = [(i, i + by) for i in range(length) if 0 <= i + by < length]
    return lax.ppermute(value, axis, pairs)


def load_kernel(leads, *refs):
    count = len(leads)
    ins, (own, y_low, y_high, x_low, x_high, token), sems = refs[:count], refs[count:-1], refs[-1]
    token[...] = jnp.zeros(token.shape, F32)
    rx, ry = own.shape[1:3]
    copies = [
        pltpu.make_async_copy(
            ins[n] if lead is None else ins[n].at[lead], own.at[n], sems.at[n]
        )
        for n, lead in enumerate(leads)
    ]
    for c in copies:
        c.start()

    def one(n):
        y_low[n] = own[n, :, 0:H, :]
        y_high[n] = own[n, :, ry - H :, :]
        x_low[n] = own[n, 0:H]
        x_high[n] = own[n, rx - H :]

    for n, c in enumerate(copies):
        c.wait()
        one(n)


def load(arrays, leads, dims):
    n = len(leads)
    rx, ry, nz = dims
    return pl.pallas_call(
        functools.partial(load_kernel, leads),
        in_specs=[HBM] * n,
        out_specs=[VMEM] * 6,
        out_shape=[sds(n, *dims)] + [sds(n, rx, H, nz)] * 2 + [sds(n, H, ry, nz)] * 2
        + [sds(8, 128)],
        scratch_shapes=[pltpu.SemaphoreType.DMA((n,))],
        name="load",
    )(*arrays)


def fold(rows_of, high):
    tiles = []
    for dx in range(1, 5):
        near, far = rows_of(dx), rows_of(8 - dx)
        sub = lax.broadcasted_iota(jnp.int32, near.shape, 0)
        if high:
            tiles.append(jnp.where(sub < 8 - dx, near, pltpu.roll(far, 8 - dx, 0)))
        else:
            tiles.append(jnp.where(sub >= dx, near, pltpu.roll(far, dx, 0)))
    return tiles


def unfold(tile, dx, high):
    return tile, pltpu.roll(tile, dx if high else 8 - dx, 0)


def corner_tiles(n, z_low, z_high, put):
    rx = z_low.shape[1]
    for side in (0, 1):
        for high, z in ((False, z_low), (True, z_high)):

            def rows_of(dx):
                return z[n, dx - 1 if side == 0 else rx - dx]

            for t, tile in enumerate(fold(rows_of, high)):
                put(side, int(high), t, tile)


def corner_kernel(first, z_low, z_high, *refs):
    outs = refs[-2:]

    def one(n, _):
        def put(side, y, t, tile):
            outs[side][n, t, y * H : (y + 1) * H, :] = tile

        corner_tiles(n + first, z_low, z_high, put)
        return 0

    lax.fori_loop(0, outs[0].shape[0], one, 0)


def pack_corners(name, z_low, z_high, first, count, after):
    nz = z_low.shape[-1]
    return call(
        functools.partial(corner_kernel, first), [z_low, z_high, *after],
        [sds(count, 4, 2 * H, nz)] * 2, name, 4,
        [VMEM] * 2 + [ANY] * len(after),
    )


def widen_kernel(own, z_low, z_high, *outs):
    rx = own.shape[1]

    def one(n, _):
        def put(side, y, t, tile):
            outs[side][n, H + t, y * H : (y + 1) * H, :] = tile

        corner_tiles(n, z_low, z_high, put)
        outs[0][n, 0:H] = own[n, 0:H]
        outs[1][n, 0:H] = own[n, rx - H :]
        return 0

    lax.fori_loop(0, own.shape[0], one, 0)


def widen(own, z_low, z_high):
    count, rx, ry, nz = own.shape
    return call(widen_kernel, [own, z_low, z_high], [sds(count, H + 4, ry, nz)] * 2, "widen", 4)


def table_kernel(steps, rate, bhp, control, perf_well, perf_cell, perf_wi, _, out):
    wells = rate.shape[0]
    effective = jnp.where(control[...] == 1, rate[...], bhp[...])
    lane = lax.broadcasted_iota(jnp.int32, (1, 128), 1)
    row = jnp.zeros((1, 128), F32)
    for u in range(wells):
        for n in range(steps):
            row = jnp.where(lane == u * steps + n, effective[u : u + 1, n : n + 1], row)
    mine = jnp.concatenate(
        [row, perf_cell[...].astype(F32), perf_well[...].astype(F32), perf_wi[...]]
    )
    out[...] = jnp.broadcast_to(mine[None], out.shape)


def spot():
    n_x, n_y = lax.axis_size("gx"), lax.axis_size("gy")
    x, y = lax.axis_index("gx"), lax.axis_index("gy")
    return x, y, n_x, n_y


def source_kernel(steps, wells, ry, table_ref, _, src_ref):
    here_x, here_y, n_x, n_y = spot()
    count = table_ref.shape[0]
    rx = src_ref.shape[1] // 3
    of_wells = table_ref[:, 0, :]
    owner_iota = lax.broadcasted_iota(jnp.int32, (count, 128), 0)
    sub = lax.broadcasted_iota(jnp.int32, (128, 128), 0)
    row_iota = lax.broadcasted_iota(jnp.int32, (rx * ry, 128), 0)

    def block(k, _):
        dx = k // 3
        dy = k - 3 * dx
        at_x, at_y = here_x + dx - 1, here_y + dy - 1
        inside = (at_x >= 0) & (at_x < n_x) & (at_y >= 0) & (at_y < n_y)
        slot = table_ref[jnp.where(inside, at_x * n_y + at_y, 0)]
        cell = slot[1:2, :].astype(jnp.int32)
        well = slot[2:3, :].astype(jnp.int32)
        wi = slot[3:4, :] * inside.astype(F32)
        owner = well // wells
        within = well - owner * wells
        hot = jnp.where(owner_iota == owner, 1.0, 0.0).astype(F32)
        found = lax.dot_general(
            of_wells, hot, (((0,), (0,)), ((), ())), precision=HIGHEST,
            preferred_element_type=F32,
        )
        by_row = jnp.where(row_iota == (cell >> 7), 1.0, 0.0).astype(BF16)
        in_lane = sub == (cell & 127)
        for step in range(steps):
            value = jnp.zeros((1, 128), F32)
            for u in range(wells):
                c = u * steps + step
                value = value + jnp.where(within == u, found[c : c + 1, :], 0.0)
            value = value * wi
            part = None
            for _ in range(3):
                piece = value.astype(BF16)
                value = value - piece.astype(F32)
                by_lane = jnp.where(in_lane, piece.astype(F32), 0.0).astype(BF16)
                add = lax.dot_general(
                    by_row, by_lane, (((1,), (1,)), ((), ())), preferred_element_type=F32
                )
                part = add if part is None else part + add
            src_ref[
                step, pl.ds(pl.multiple_of(dx * rx, rx), rx),
                pl.ds(pl.multiple_of(dy * ry, ry), ry), :,
            ] = part.reshape(rx, ry, 128)
        return 0

    lax.fori_loop(0, 9, block, 0)


def by_v(ref, lead, x, offset=0):
    return jnp.stack(
        [ref[(*lead, x, pl.ds(offset + v, 8, stride=V), slice(None))] for v in range(V)]
    )


def up_v(value):
    return jnp.concatenate([value[1:], pltpu.roll(value[0], 7, 0)[None]])


def down_v(value):
    return jnp.concatenate([pltpu.roll(value[V - 1], 1, 0)[None], value[:-1]])


def roll_z(value, by):
    return pltpu.roll(value, by, 2)


def fill(dst, own, z_low, z_high, x_edges, corners, base, first=0, corner_first=0):
    count, (rx, ry, nz) = dst.shape[0], own.shape[1:]

    def one(n, _):
        m = n + first
        dst[n, H : H + rx, 0:H, :] = z_low[m]
        dst[n, H : H + rx, H : H + ry, :] = own[m]
        dst[n, H : H + rx, H + ry : 2 * H + ry, :] = z_high[m]
        for side in (0, 1):
            at = side * (H + rx)
            dst[n, at : at + H, H : H + ry, :] = x_edges[side][m, 0:H]
            for y in (0, 1):
                to = y * (H + ry)
                for t in range(4):
                    tile = corners[side][n + corner_first, base + t, y * H : (y + 1) * H, :]
                    near, far = unfold(tile, t + 1, y == 1)
                    for dx, row in ((t + 1, near), (7 - t, far)):
                        x = H - dx if side == 0 else H + rx + dx - 1
                        dst[n, x, to : to + H, :] = row
                x = 0 if side == 0 else 2 * H + rx - 1
                dst[n, x, to : to + H, :] = jnp.zeros((H, nz), F32)
        return 0

    lax.fori_loop(0, count, one, 0)


SA, RA, PC, FR, RB, QC, MC, AA, AB = range(9)
TX, TY, TZ, TU, WS = range(5)


def coefficients(raw, base, src_ref, step, x, total, src_x, src_y):
    c_pp, c_ss, c_ps, c_sp, frac, mob, g_p, g_s = [by_v(raw, (base + n,), x) for n in range(8)]
    den_a = c_pp + total
    den_b = c_ss + mob * total
    s_a = jnp.where(den_a > 0, OMEGA / den_a, 0.0)
    s_b = jnp.where(den_b > 0, OMEGA / den_b, 0.0)
    r_a = g_p + by_v(src_ref, (step,), x + src_x, src_y)
    return s_a, r_a, c_sp + frac * total, frac, s_b * g_s, s_b * c_ps, s_b * mob, s_b


BLOCK = 2
UNROLL = 4


def sweeps(coef, geo, bufs, lin, begin, ex):
    def work(number, x, count):
        old, new = bufs[(number - 1) % 2], bufs[number % 2]
        tx = [geo[TX, x + r] for r in range(count + 1)]
        values = [[old[f][x - 1 + r] for r in range(count + 2)] for f in range(2)]
        results = []
        for r in range(count):
            at = x + r
            ty = geo[TY, at]
            ty_up = up_v(ty)
            tz, tz_up = geo[TZ, at], geo[TU, at]

            def around(v):
                c = v[r + 1]
                total = tx[r + 1] * v[r + 2] + tx[r] * v[r]
                total = total + (ty_up * up_v(c) + ty * down_v(c))
                total = total + (tz_up * roll_z(c, 127) + tz * roll_z(c, 1))
                return c, total

            a, n_a = around(values[0])
            b, n_b = around(values[1])
            new_a = KEEP * a + coef[SA, at] * (
                (coef[RA, at] + n_a) + (coef[FR, at] * n_b - coef[PC, at] * b)
            )
            new_b = (KEEP * b + coef[RB, at]) + (coef[MC, at] * n_b - coef[QC, at] * a)
            results.append((new_a, new_b))
        for r in range(count):
            for f in range(2):
                if number == SWEEPS:
                    for v in range(V):
                        lin[f, x + r, pl.ds(v, 8, stride=V), :] = results[r][f][v]
                else:
                    new[f][x + r] = results[r][f]

    for number in range(begin, SWEEPS + 1):
        size = BLOCK * UNROLL
        total = ex - 2 * number

        def many(i, _):
            for u in range(UNROLL):
                work(number, number + i * size + u * BLOCK, BLOCK)
            return 0

        lax.fori_loop(0, total // size, many, 0)
        for at in range(total - total % size, total, BLOCK):
            work(number, number + at, BLOCK)


def finish(last, step, steps, wells, lin, frac, table_ref, before, outs):
    rx, ry, nz = frac.shape[-3:]
    out_wells = outs[-1]

    def copy(x, _):
        for f in range(2):
            row = lin[f, H + x, H : H + ry, :]
            if last:
                outs[f][x] = row
            else:
                outs[0][f, x] = row
                outs[1][f, x] = row[0:H]
                outs[2][f, x] = row[ry - H :]
        return 0

    lax.fori_loop(0, rx, copy, 0, unroll=2)
    mix = lin[0, H : H + rx, H : H + ry, :] + frac[...] * lin[1, H : H + rx, H : H + ry, :]
    mix = mix.reshape(rx * ry, nz)
    here_x, here_y, _, n_y = spot()
    slot = table_ref[here_x * n_y + here_y]
    lane = lax.broadcasted_iota(jnp.int32, (128, 128), 1)
    diagonal = lax.broadcasted_iota(jnp.int32, (128, 128), 0) == lane

    def upright(row):
        return jnp.sum(jnp.where(diagonal, row, 0.0), axis=1, keepdims=True)

    cell = upright(slot[1:2, :]).astype(jnp.int32)
    well = upright(slot[2:3, :]).astype(jnp.int32)
    wi = upright(slot[3:4, :])
    by_row = jnp.where(
        lax.broadcasted_iota(jnp.int32, (128, rx * ry), 1) == (cell >> 7), 1.0, 0.0
    ).astype(BF16)
    picked = None
    for _ in range(3):
        piece = mix.astype(BF16)
        mix = mix - piece.astype(F32)
        add = jnp.dot(by_row, piece, preferred_element_type=F32)
        picked = add if picked is None else picked + add
    values = jnp.sum(jnp.where(lane == (cell & 127), picked, 0.0), axis=1, keepdims=True)
    values = values * wi
    owner = well // wells
    spread = jnp.where(lane == (well - owner * wells) * steps + step, values, 0.0)
    flat = slot[2:3, :].astype(jnp.int32) // wells
    count = table_ref.shape[0]
    hot = jnp.where(
        lax.broadcasted_iota(jnp.int32, (count, 128), 0) == flat, 1.0, 0.0
    ).astype(F32)
    dense = jnp.dot(hot, spread, precision=HIGHEST, preferred_element_type=F32)
    if before is not None:
        dense = dense + before[...]
    out_wells[...] = dense


def first_kernel(step, steps, wells, *refs):
    table_ref, src_ref, own, z_low, z_high, x_low, x_high, c_low, c_high = refs[:9]
    geo = refs[9]
    outs = refs[10:14]
    raw, coef, fa0, fb0, fa1, fb1, lin = refs[14:]
    rx, ry, nz = own.shape[1:]
    ex = rx + 2 * H
    fill(raw, own, z_low, z_high, (x_low, x_high), (c_low, c_high), 0)
    here_x, here_y, _, _ = spot()

    @pl.when(here_x == 0)
    def _():
        raw[0, H, :, :] = jnp.zeros(raw.shape[2:], F32)

    @pl.when(here_y == 0)
    def _():
        def clear(x, _):
            raw[1, x, H : H + 1, :] = jnp.zeros((1, nz), F32)
            return 0

        lax.fori_loop(0, ex, clear, 0)

    def geometry(x, _):
        lane = lax.broadcasted_iota(jnp.int32, (V, 8, nz), 2)
        tz = jnp.where(lane == 0, 0.0, by_v(raw, (2,), x))
        geo[TX, x] = by_v(raw, (0,), x)
        geo[TY, x] = by_v(raw, (1,), x)
        geo[TZ, x] = tz
        geo[TU, x] = roll_z(tz, 127)
        return 0

    lax.fori_loop(0, ex, geometry, 0, unroll=4)

    def prepare(x, _):
        ty = geo[TY, x]
        total = (
            (geo[TX, x + 1] + geo[TX, x]) + (up_v(ty) + ty) + (geo[TU, x] + geo[TZ, x])
        )
        geo[WS, x] = total
        s_a, r_a, p, frac, r_b, q, m, _ = coefficients(
            raw, 3, src_ref, step, x, total, rx - H, ry - H
        )
        coef[SA, x] = s_a
        coef[RA, x] = r_a
        coef[PC, x] = p
        coef[FR, x] = frac
        coef[RB, x] = r_b
        coef[QC, x] = q
        coef[MC, x] = m
        fa1[x] = s_a * r_a
        fb1[x] = r_b
        return 0

    lax.fori_loop(0, ex - 1, prepare, 0)
    sweeps(coef, geo, ((fa0, fb0), (fa1, fb1)), lin, 2, ex)
    finish(False, step, steps, wells, lin, own.at[7], table_ref, None, outs)


def prepare_kernel(step, first, corner_first, with_acc, *refs):
    src_ref, geo, own, z_low, z_high, x_low, x_high, c_low, c_high = refs[:9]
    if with_acc:
        coef, acc_out, raw = refs[9:]
    else:
        acc, coef, raw = refs[9:]
    rx, ry, nz = own.shape[1:]
    ex = rx + 2 * H
    fill(raw, own, z_low, z_high, (x_low, x_high), (c_low, c_high), 0, first, corner_first)

    def prepare(x, _):
        s_a, r_a, p, frac, r_b, q, m, s_b = coefficients(
            raw, 0, src_ref, step, x, geo[WS, x], rx - H, ry - H
        )
        coef[SA, x] = s_a
        coef[RA, x] = r_a
        coef[PC, x] = p
        coef[FR, x] = frac
        coef[RB, x] = r_b
        coef[QC, x] = q
        coef[MC, x] = m
        if with_acc:
            a, b = by_v(raw, (8,), x), by_v(raw, (9,), x)
            acc_out[0, x] = a
            acc_out[1, x] = b
        else:
            a, b = acc[0, x], acc[1, x]
        coef[AA, x] = a
        coef[AB, x] = s_b * b
        return 0

    lax.fori_loop(0, ex - 1, prepare, 0)


def sweep_kernel(last, step, frac_at, steps, wells, *refs):
    table_ref, coef, geo, own, lam, z_low, z_high, x_low, x_high, before = refs[:10]
    outs = refs[10:-6]
    now, fa0, fb0, fa1, fb1, lin = refs[-6:]
    rx, ry, nz = own.shape[1:]
    ex = rx + 2 * H
    fill(lin, lam, z_low, z_high, (x_low, x_high), (x_low, x_high), H)

    def begin(x, _):
        a, b = by_v(lin, (0,), x), by_v(lin, (1,), x)
        fa0[x] = a
        fb0[x] = b
        now[0, x] = coef[RA, x] + coef[AA, x] * a
        now[1, x] = coef[RB, x] + coef[AB, x] * b
        return 0

    lax.fori_loop(0, ex, begin, 0, unroll=4)

    class Joined:
        def __getitem__(self, at):
            n, x = at
            return now[0, x] if n == RA else now[1, x] if n == RB else coef[n, x]

    sweeps(Joined(), geo, ((fa0, fb0), (fa1, fb1)), lin, 1, ex)
    finish(last, step, steps, wells, lin, own.at[frac_at], table_ref, before, outs)


def local(
    grad_p, grad_s, acc_p, acc_s, trans_x, trans_y, trans_z, c_pp, c_ss, c_ps, c_sp,
    frac, mobility, rate_mis, bhp_mis, control, perf_well, perf_cell, perf_wi,
):
    dims = rx, ry, nz = trans_x.shape
    ex, ey = rx + 2 * H, ry + 2 * H
    steps = grad_p.shape[0]
    wells = rate_mis.shape[0]
    devices = lax.axis_size("gx") * lax.axis_size("gy")
    own = [c_pp, c_ss, c_ps, c_sp, frac, mobility, grad_p, grad_s]
    top = steps - 1

    def sent(low, high, axis):
        return shifted(high, axis, 1), shifted(low, axis, -1)

    arrays = [trans_x, trans_y, trans_z] + own
    leads = [None] * 3 + [top] * 8
    split = len(arrays)
    places = {}
    for step in reversed(range(top)):
        places[step] = len(arrays)
        arrays += own
        leads += [step] * 8
        if step == top - 1:
            arrays += [acc_p, acc_s]
            leads += [None] * 2
    blocks, y_low, y_high, e_low, e_high, token = load(arrays, leads, dims)

    z_got = sent(y_low, y_high, "gy")
    x_got = sent(e_low, e_high, "gx")

    mine = call(
        functools.partial(table_kernel, steps),
        [rate_mis, bhp_mis, control] + [p[None] for p in (perf_well, perf_cell, perf_wi)]
        + [token], [sds(devices, 4, 128)], "table", 4, [VMEM] * 6 + [ANY],
    )[0]
    table = lax.all_to_all(mine, ("gx", "gy"), 0, 0, tiled=True)

    corners = pack_corners("corners", *z_got, 0, split, (*x_got, table))
    c_got = sent(*corners, "gx")
    src = call(
        functools.partial(source_kernel, steps, wells, ry), [table, corners[0]],
        [sds(steps, 3 * rx, 3 * ry, nz)], "sources", 8, [VMEM, ANY],
    )[0]
    rest = len(arrays) - split
    m_c = sent(*pack_corners("corners_more", *z_got, split, rest, (src,)), "gx")

    ext = (ex, V, 8, nz)
    lam_out = [sds(2, rx, ry, nz), sds(2, rx, H, nz), sds(2, rx, H, nz)]
    well_out = sds(devices, 128)
    fields = [pltpu.VMEM(ext, F32)] * 4 + [pltpu.VMEM((2, ex, ey, nz), F32)]

    geo, lam, low, high, dense = call(
        functools.partial(first_kernel, top, steps, wells),
        [table, src, blocks, *z_got, *x_got, *c_got],
        [sds(5, *ext)] + lam_out + [well_out], "step_top", 16,
        scratch=[pltpu.VMEM((split, ex, ey, nz), F32), pltpu.VMEM((7, *ext), F32)] + fields,
    )

    acc = None
    for step in reversed(range(top)):
        last = step == 0
        with_acc = step == top - 1
        at = places[step]
        made = call(
            functools.partial(prepare_kernel, step, at, at - split, with_acc),
            [src, geo, blocks, *z_got, *x_got, *m_c] + ([] if with_acc else [acc]),
            [sds(9, *ext)] + ([sds(2, *ext)] if with_acc else []), "prepare", 8,
            scratch=[pltpu.VMEM((10 if with_acc else 8, ex, ey, nz), F32)],
        )
        coef = made[0]
        if with_acc:
            acc = made[1]

        l_z = sent(low, high, "gy")
        l_x = sent(*widen(lam, *l_z), "gx")
        outs = [sds(rx, ry, nz)] * 2 if last else lam_out
        outs = call(
            functools.partial(sweep_kernel, last, step, at + 4, steps, wells),
            [table, coef, geo, blocks, lam, *l_z, *l_x, dense],
            outs + [well_out], "step", 8, scratch=[pltpu.VMEM((2, *ext), F32)] + fields,
        )
        dense = outs[-1]
        if not last:
            lam, low, high = outs[:3]

    parts = lax.all_to_all(dense[:, None, :], ("gx", "gy"), 0, 0, tiled=True)
    well_grad = jnp.sum(parts, axis=(0, 1))[: wells * steps].reshape(wells, steps)
    return outs[0], outs[1], well_grad


def solution(mesh):
    cells3 = P("gx", "gy", None)
    cells4 = P(None, "gx", "gy", None)
    flat = ("gx", "gy")
    placed = (cells4,) * 2 + (cells3,) * 5 + (cells4,) * 6 + (P(flat, None),) * 3 + (P(flat),) * 3
    return jax.shard_map(
        local,
        mesh=mesh,
        in_specs=placed,
        out_specs=(cells3, cells3, P(flat, None)),
        check_vma=False,
    )
```

```python
import functools

import jax
import jax.numpy as jnp
from jax import lax
from jax.experimental import pallas as pl
from jax.experimental.pallas import tpu as pltpu
from jax.sharding import PartitionSpec as P

SWEEPS = 8
OMEGA = 0.8
KEEP = 1.0 - OMEGA
H = 8
V = 4
HIGHEST = lax.Precision.HIGHEST
F32 = jnp.float32
BF16 = jnp.bfloat16
FLOPS = 1e9

VMEM = pl.BlockSpec(memory_space=pltpu.VMEM)
ANY = pl.BlockSpec(memory_space=pl.ANY)
HBM = pl.BlockSpec(memory_space=pltpu.HBM)


def sds(*shape):
    return jax.ShapeDtypeStruct(shape, F32)


def params(mib):
    return pltpu.CompilerParams(vmem_limit_bytes=mib * 1024 * 1024)


TIMES = {"step_top": 7, "step": 6, "sources": 3, "prepare": 1.5}


def estimate(name):
    work = TIMES.get(name, 0.5)
    return pl.CostEstimate(
        flops=int(work * FLOPS), bytes_accessed=int(work * 3.0e6), transcendentals=0
    )


def call(kernel, ins, outs, name, mib, specs=None, scratch=()):
    return pl.pallas_call(
        kernel,
        in_specs=specs or [VMEM] * len(ins),
        out_specs=[VMEM] * len(outs),
        out_shape=outs,
        scratch_shapes=list(scratch),
        compiler_params=params(mib),
        cost_estimate=estimate(name),
        name=name,
    )(*ins)


def shifted(value, axis, by):
    length = lax.axis_size(axis)
    pairs = [(i, i + by) for i in range(length) if 0 <= i + by < length]
    return lax.ppermute(value, axis, pairs)


def load_kernel(leads, *refs):
    count = len(leads)
    ins, (own, y_low, y_high, x_low, x_high), sems = refs[:count], refs[-6:-1], refs[-1]
    copies = [
        pltpu.make_async_copy(
            ins[n] if lead is None else ins[n].at[lead], own.at[n], sems.at[n]
        )
        for n, lead in enumerate(leads)
    ]
    for c in copies:
        c.start()
    for c in copies:
        c.wait()
    y_edges(own, y_low, y_high)
    x_edges(own, x_low, x_high)


def y_edges(own, low, high):
    ry = own.shape[2]

    def one(n, _):
        low[n] = own[n, :, 0:H, :]
        high[n] = own[n, :, ry - H :, :]
        return 0

    lax.fori_loop(0, own.shape[0], one, 0)


def x_edges(own, low, high):
    rx = own.shape[1]

    def one(n, _):
        low[n] = own[n, 0:H]
        high[n] = own[n, rx - H :]
        return 0

    lax.fori_loop(0, own.shape[0], one, 0)


def load(arrays, leads, dims, after):
    n = len(leads)
    rx, ry, nz = dims
    return pl.pallas_call(
        functools.partial(load_kernel, leads),
        in_specs=[HBM] * n + [ANY] * len(after),
        out_specs=[VMEM] * 5,
        out_shape=[sds(n, *dims)] + [sds(n, rx, H, nz)] * 2 + [sds(n, H, ry, nz)] * 2,
        scratch_shapes=[pltpu.SemaphoreType.DMA((n,))],
        name="load",
    )(*arrays, *after)


def more_kernel(leads, *refs):
    count = len(leads)
    ins, (own, y_low, y_high), sems = refs[:count], refs[-4:-1], refs[-1]
    copies = [
        pltpu.make_async_copy(
            ins[n] if lead is None else ins[n].at[lead], own.at[n], sems.at[n]
        )
        for n, lead in enumerate(leads)
    ]
    for c in copies:
        c.start()
    for c in copies:
        c.wait()
    y_edges(own, y_low, y_high)


def more(arrays, leads, dims, after):
    n = len(leads)
    rx, ry, nz = dims
    return call(
        functools.partial(more_kernel, leads), list(arrays) + list(after),
        [sds(n, *dims)] + [sds(n, rx, H, nz)] * 2, "more", 4,
        [ANY] * (n + len(after)), [pltpu.SemaphoreType.DMA((n,))],
    )


def fold(rows_of, high):
    tiles = []
    for dx in range(1, 5):
        near, far = rows_of(dx), rows_of(8 - dx)
        sub = lax.broadcasted_iota(jnp.int32, near.shape, 0)
        if high:
            tiles.append(jnp.where(sub < 8 - dx, near, pltpu.roll(far, 8 - dx, 0)))
        else:
            tiles.append(jnp.where(sub >= dx, near, pltpu.roll(far, dx, 0)))
    return tiles


def unfold(tile, dx, high):
    return tile, pltpu.roll(tile, dx if high else 8 - dx, 0)


def corner_tiles(n, z_low, z_high, put):
    rx = z_low.shape[1]
    for side in (0, 1):
        for high, z in ((False, z_low), (True, z_high)):

            def rows_of(dx):
                return z[n, dx - 1 if side == 0 else rx - dx]

            for t, tile in enumerate(fold(rows_of, high)):
                put(side, int(high), t, tile)


def corner_kernel(z_low, z_high, *refs):
    outs = refs[-2:]

    def one(n, _):
        def put(side, y, t, tile):
            outs[side][n, t, y * H : (y + 1) * H, :] = tile

        corner_tiles(n, z_low, z_high, put)
        return 0

    lax.fori_loop(0, z_low.shape[0], one, 0)


def pack_corners(name, z_low, z_high, after):
    count, _, _, nz = z_low.shape
    return call(
        corner_kernel, [z_low, z_high, *after],
        [sds(count, 4, 2 * H, nz)] * 2, name, 4,
        [VMEM] * 2 + [ANY] * len(after),
    )


def widen_kernel(own, z_low, z_high, *refs):
    outs = refs[-2:]
    rx = own.shape[1]

    def one(n, _):
        def put(side, y, t, tile):
            outs[side][n, H + t, y * H : (y + 1) * H, :] = tile

        corner_tiles(n, z_low, z_high, put)
        outs[0][n, 0:H] = own[n, 0:H]
        outs[1][n, 0:H] = own[n, rx - H :]
        return 0

    lax.fori_loop(0, own.shape[0], one, 0)


def widen(own, z_low, z_high, after=()):
    count, rx, ry, nz = own.shape
    return call(
        widen_kernel, [own, z_low, z_high, *after], [sds(count, H + 4, ry, nz)] * 2, "widen", 4,
        [VMEM] * 3 + [ANY] * len(after),
    )


def table_kernel(steps, *refs):
    ins, out, held, sems = refs[:6], refs[6], refs[7:13], refs[13]
    copies = [pltpu.make_async_copy(i, h, sems.at[n]) for n, (i, h) in enumerate(zip(ins, held))]
    for c in copies:
        c.start()
    for c in copies:
        c.wait()
    rate, bhp, control, perf_well, perf_cell, perf_wi = [h[...] for h in held]
    wells = rate.shape[0]
    effective = jnp.where(control == 1, rate, bhp)
    lane = lax.broadcasted_iota(jnp.int32, (1, 128), 1)
    row = jnp.zeros((1, 128), F32)
    for u in range(wells):
        for n in range(steps):
            row = jnp.where(lane == u * steps + n, effective[u : u + 1, n : n + 1], row)
    mine = jnp.concatenate([row, perf_cell.astype(F32), perf_well.astype(F32), perf_wi])
    out[...] = jnp.broadcast_to(mine[None], out.shape)


def spot():
    n_x, n_y = lax.axis_size("gx"), lax.axis_size("gy")
    x, y = lax.axis_index("gx"), lax.axis_index("gy")
    return x, y, n_x, n_y


def source_kernel(wanted, steps, wells, ry, table_ref, _, src_ref):
    here_x, here_y, n_x, n_y = spot()
    count = table_ref.shape[0]
    rx = src_ref.shape[1] // 3
    of_wells = table_ref[:, 0, :]
    owner_iota = lax.broadcasted_iota(jnp.int32, (count, 128), 0)
    sub = lax.broadcasted_iota(jnp.int32, (128, 128), 0)
    row_iota = lax.broadcasted_iota(jnp.int32, (rx * ry, 128), 0)

    def block(k, _):
        dx = k // 3
        dy = k - 3 * dx
        at_x, at_y = here_x + dx - 1, here_y + dy - 1
        inside = (at_x >= 0) & (at_x < n_x) & (at_y >= 0) & (at_y < n_y)
        slot = table_ref[jnp.where(inside, at_x * n_y + at_y, 0)]
        cell = slot[1:2, :].astype(jnp.int32)
        well = slot[2:3, :].astype(jnp.int32)
        wi = slot[3:4, :] * inside.astype(F32)
        owner = well // wells
        within = well - owner * wells
        hot = jnp.where(owner_iota == owner, 1.0, 0.0).astype(F32)
        found = lax.dot_general(
            of_wells, hot, (((0,), (0,)), ((), ())), precision=HIGHEST,
            preferred_element_type=F32,
        )
        by_row = jnp.where(row_iota == (cell >> 7), 1.0, 0.0).astype(BF16)
        in_lane = sub == (cell & 127)
        for place, step in enumerate(wanted):
            value = jnp.zeros((1, 128), F32)
            for u in range(wells):
                c = u * steps + step
                value = value + jnp.where(within == u, found[c : c + 1, :], 0.0)
            value = value * wi
            part = None
            for _ in range(3):
                piece = value.astype(BF16)
                value = value - piece.astype(F32)
                by_lane = jnp.where(in_lane, piece.astype(F32), 0.0).astype(BF16)
                add = lax.dot_general(
                    by_row, by_lane, (((1,), (1,)), ((), ())), preferred_element_type=F32
                )
                part = add if part is None else part + add
            src_ref[
                place, pl.ds(pl.multiple_of(dx * rx, rx), rx),
                pl.ds(pl.multiple_of(dy * ry, ry), ry), :,
            ] = part.reshape(rx, ry, 128)
        return 0

    lax.fori_loop(0, 9, block, 0)


def by_v(ref, lead, x, offset=0):
    return jnp.stack(
        [ref[(*lead, x, pl.ds(offset + v, 8, stride=V), slice(None))] for v in range(V)]
    )


def up_v(value):
    return jnp.concatenate([value[1:], pltpu.roll(value[0], 7, 0)[None]])


def down_v(value):
    return jnp.concatenate([pltpu.roll(value[V - 1], 1, 0)[None], value[:-1]])


def roll_z(value, by):
    return pltpu.roll(value, by, 2)


def fill(dst, own, z_low, z_high, x_edges, corners, base):
    count, (rx, ry, nz) = dst.shape[0], own.shape[1:]

    def one(n, _):
        dst[n, H : H + rx, 0:H, :] = z_low[n]
        dst[n, H : H + rx, H : H + ry, :] = own[n]
        dst[n, H : H + rx, H + ry : 2 * H + ry, :] = z_high[n]
        for side in (0, 1):
            at = side * (H + rx)
            dst[n, at : at + H, H : H + ry, :] = x_edges[side][n, 0:H]
            for y in (0, 1):
                to = y * (H + ry)
                for t in range(4):
                    tile = corners[side][n, base + t, y * H : (y + 1) * H, :]
                    near, far = unfold(tile, t + 1, y == 1)
                    for dx, row in ((t + 1, near), (7 - t, far)):
                        x = H - dx if side == 0 else H + rx + dx - 1
                        dst[n, x, to : to + H, :] = row
                x = 0 if side == 0 else 2 * H + rx - 1
                dst[n, x, to : to + H, :] = jnp.zeros((H, nz), F32)
        return 0

    lax.fori_loop(0, count, one, 0)


SA, RA, PC, FR, RB, QC, MC, AA, AB = range(9)
TX, TY, TZ, TU, WS = range(5)


def coefficients(raw, base, src_ref, step, x, total, src_x, src_y):
    c_pp, c_ss, c_ps, c_sp, frac, mob, g_p, g_s = [by_v(raw, (base + n,), x) for n in range(8)]
    den_a = c_pp + total
    den_b = c_ss + mob * total
    s_a = jnp.where(den_a > 0, OMEGA / den_a, 0.0)
    s_b = jnp.where(den_b > 0, OMEGA / den_b, 0.0)
    r_a = g_p + by_v(src_ref, (step,), x + src_x, src_y)
    return s_a, r_a, c_sp + frac * total, frac, s_b * g_s, s_b * c_ps, s_b * mob, s_b


BLOCK = 2
UNROLL = 4


def sweeps(coef, geo, bufs, lin, begin, ex):
    def work(number, x, count):
        old, new = bufs[(number - 1) % 2], bufs[number % 2]
        tx = [geo[TX, x + r] for r in range(count + 1)]
        values = [[old[f][x - 1 + r] for r in range(count + 2)] for f in range(2)]
        results = []
        for r in range(count):
            at = x + r
            ty = geo[TY, at]
            ty_up = up_v(ty)
            tz, tz_up = geo[TZ, at], geo[TU, at]

            def around(v):
                c = v[r + 1]
                total = tx[r + 1] * v[r + 2] + tx[r] * v[r]
                total = total + (ty_up * up_v(c) + ty * down_v(c))
                total = total + (tz_up * roll_z(c, 127) + tz * roll_z(c, 1))
                return c, total

            a, n_a = around(values[0])
            b, n_b = around(values[1])
            new_a = KEEP * a + coef[SA, at] * (
                (coef[RA, at] + n_a) + (coef[FR, at] * n_b - coef[PC, at] * b)
            )
            new_b = (KEEP * b + coef[RB, at]) + (coef[MC, at] * n_b - coef[QC, at] * a)
            results.append((new_a, new_b))
        for r in range(count):
            for f in range(2):
                if number == SWEEPS:
                    for v in range(V):
                        lin[f, x + r, pl.ds(v, 8, stride=V), :] = results[r][f][v]
                else:
                    new[f][x + r] = results[r][f]

    for number in range(begin, SWEEPS + 1):
        size = BLOCK * UNROLL
        total = ex - 2 * number

        def many(i, _):
            for u in range(UNROLL):
                work(number, number + i * size + u * BLOCK, BLOCK)
            return 0

        lax.fori_loop(0, total // size, many, 0)
        for at in range(total - total % size, total, BLOCK):
            work(number, number + at, BLOCK)


def finish(last, step, steps, wells, lin, frac, table_ref, before, outs):
    rx, ry, nz = frac.shape[-3:]
    out_wells = outs[-1]

    def copy(x, _):
        for f in range(2):
            row = lin[f, H + x, H : H + ry, :]
            if last:
                outs[f][x] = row
            else:
                outs[0][f, x] = row
                outs[1][f, x] = row[0:H]
                outs[2][f, x] = row[ry - H :]
        return 0

    lax.fori_loop(0, rx, copy, 0, unroll=2)
    mix = lin[0, H : H + rx, H : H + ry, :] + frac[...] * lin[1, H : H + rx, H : H + ry, :]
    mix = mix.reshape(rx * ry, nz)
    here_x, here_y, _, n_y = spot()
    slot = table_ref[here_x * n_y + here_y]
    lane = lax.broadcasted_iota(jnp.int32, (128, 128), 1)
    diagonal = lax.broadcasted_iota(jnp.int32, (128, 128), 0) == lane

    def upright(row):
        return jnp.sum(jnp.where(diagonal, row, 0.0), axis=1, keepdims=True)

    cell = upright(slot[1:2, :]).astype(jnp.int32)
    well = upright(slot[2:3, :]).astype(jnp.int32)
    wi = upright(slot[3:4, :])
    by_row = jnp.where(
        lax.broadcasted_iota(jnp.int32, (128, rx * ry), 1) == (cell >> 7), 1.0, 0.0
    ).astype(BF16)
    picked = None
    for _ in range(3):
        piece = mix.astype(BF16)
        mix = mix - piece.astype(F32)
        add = jnp.dot(by_row, piece, preferred_element_type=F32)
        picked = add if picked is None else picked + add
    values = jnp.sum(jnp.where(lane == (cell & 127), picked, 0.0), axis=1, keepdims=True)
    values = values * wi
    owner = well // wells
    spread = jnp.where(lane == (well - owner * wells) * steps + step, values, 0.0)
    flat = slot[2:3, :].astype(jnp.int32) // wells
    count = table_ref.shape[0]
    hot = jnp.where(
        lax.broadcasted_iota(jnp.int32, (count, 128), 0) == flat, 1.0, 0.0
    ).astype(F32)
    dense = jnp.dot(hot, spread, precision=HIGHEST, preferred_element_type=F32)
    if before is not None:
        dense = dense + before[...]
    out_wells[...] = dense


def first_kernel(step, steps, wells, *refs):
    table_ref, src_ref, own, z_low, z_high, x_low, x_high, c_low, c_high = refs[:9]
    geo = refs[9]
    outs = refs[10:14]
    raw, coef, fa0, fb0, fa1, fb1, lin = refs[14:]
    rx, ry, nz = own.shape[1:]
    ex = rx + 2 * H
    fill(raw, own, z_low, z_high, (x_low, x_high), (c_low, c_high), 0)
    here_x, here_y, _, _ = spot()

    @pl.when(here_x == 0)
    def _():
        raw[0, H, :, :] = jnp.zeros(raw.shape[2:], F32)

    @pl.when(here_y == 0)
    def _():
        def clear(x, _):
            raw[1, x, H : H + 1, :] = jnp.zeros((1, nz), F32)
            return 0

        lax.fori_loop(0, ex, clear, 0)

    def geometry(x, _):
        lane = lax.broadcasted_iota(jnp.int32, (V, 8, nz), 2)
        tz = jnp.where(lane == 0, 0.0, by_v(raw, (2,), x))
        geo[TX, x] = by_v(raw, (0,), x)
        geo[TY, x] = by_v(raw, (1,), x)
        geo[TZ, x] = tz
        geo[TU, x] = roll_z(tz, 127)
        return 0

    lax.fori_loop(0, ex, geometry, 0, unroll=4)

    def prepare(x, _):
        ty = geo[TY, x]
        total = (
            (geo[TX, x + 1] + geo[TX, x]) + (up_v(ty) + ty) + (geo[TU, x] + geo[TZ, x])
        )
        geo[WS, x] = total
        s_a, r_a, p, frac, r_b, q, m, _ = coefficients(
            raw, 3, src_ref, 0, x, total, rx - H, ry - H
        )
        coef[SA, x] = s_a
        coef[RA, x] = r_a
        coef[PC, x] = p
        coef[FR, x] = frac
        coef[RB, x] = r_b
        coef[QC, x] = q
        coef[MC, x] = m
        fa1[x] = s_a * r_a
        fb1[x] = r_b
        return 0

    lax.fori_loop(0, ex - 1, prepare, 0)
    sweeps(coef, geo, ((fa0, fb0), (fa1, fb1)), lin, 2, ex)
    finish(False, step, steps, wells, lin, own.at[7], table_ref, None, outs)


def prepare_kernel(step, with_acc, *refs):
    src_ref, geo, own, z_low, z_high, x_low, x_high = refs[:7]
    if with_acc:
        coef, acc_out, raw = refs[7:]
    else:
        acc, coef, raw = refs[7:]
    rx, ry, nz = own.shape[1:]
    ex = rx + 2 * H
    fill(raw, own, z_low, z_high, (x_low, x_high), (x_low, x_high), H)

    def prepare(x, _):
        s_a, r_a, p, frac, r_b, q, m, s_b = coefficients(
            raw, 0, src_ref, step, x, geo[WS, x], rx - H, ry - H
        )
        coef[SA, x] = s_a
        coef[RA, x] = r_a
        coef[PC, x] = p
        coef[FR, x] = frac
        coef[RB, x] = r_b
        coef[QC, x] = q
        coef[MC, x] = m
        if with_acc:
            a, b = by_v(raw, (8,), x), by_v(raw, (9,), x)
            acc_out[0, x] = a
            acc_out[1, x] = b
        else:
            a, b = acc[0, x], acc[1, x]
        coef[AA, x] = a
        coef[AB, x] = s_b * b
        return 0

    lax.fori_loop(0, ex - 1, prepare, 0)


def sweep_kernel(last, step, steps, wells, *refs):
    table_ref, coef, geo, own, lam, z_low, z_high, x_low, x_high, before = refs[:10]
    outs = refs[10:-6]
    now, fa0, fb0, fa1, fb1, lin = refs[-6:]
    rx, ry, nz = own.shape[1:]
    ex = rx + 2 * H
    fill(lin, lam, z_low, z_high, (x_low, x_high), (x_low, x_high), H)

    def begin(x, _):
        a, b = by_v(lin, (0,), x), by_v(lin, (1,), x)
        fa0[x] = a
        fb0[x] = b
        now[0, x] = coef[RA, x] + coef[AA, x] * a
        now[1, x] = coef[RB, x] + coef[AB, x] * b
        return 0

    lax.fori_loop(0, ex, begin, 0, unroll=4)

    class Joined:
        def __getitem__(self, at):
            n, x = at
            return now[0, x] if n == RA else now[1, x] if n == RB else coef[n, x]

    sweeps(Joined(), geo, ((fa0, fb0), (fa1, fb1)), lin, 1, ex)
    finish(last, step, steps, wells, lin, own.at[4], table_ref, before, outs)


def local(
    grad_p, grad_s, acc_p, acc_s, trans_x, trans_y, trans_z, c_pp, c_ss, c_ps, c_sp,
    frac, mobility, rate_mis, bhp_mis, control, perf_well, perf_cell, perf_wi,
):
    dims = rx, ry, nz = trans_x.shape
    ex, ey = rx + 2 * H, ry + 2 * H
    steps = grad_p.shape[0]
    wells = rate_mis.shape[0]
    devices = lax.axis_size("gx") * lax.axis_size("gy")
    own = [c_pp, c_ss, c_ps, c_sp, frac, mobility, grad_p, grad_s]
    top = steps - 1

    def sent(low, high, axis):
        return shifted(high, axis, 1), shifted(low, axis, -1)

    arrays = [trans_x, trans_y, trans_z] + own
    leads = [None] * 3 + [top] * 8
    split = len(arrays)
    small = [rate_mis, bhp_mis, control] + [p[None] for p in (perf_well, perf_cell, perf_wi)]
    mine = pl.pallas_call(
        functools.partial(table_kernel, steps),
        in_specs=[HBM] * 6,
        out_specs=VMEM,
        out_shape=sds(devices, 4, 128),
        scratch_shapes=[pltpu.VMEM(p.shape, p.dtype) for p in small]
        + [pltpu.SemaphoreType.DMA((6,))],
        name="table",
    )(*small)
    table = lax.all_to_all(mine, ("gx", "gy"), 0, 0, tiled=True)

    blocks, y_low, y_high, e_low, e_high = load(arrays, leads, dims, (table,))
    z_got = sent(y_low, y_high, "gy")
    x_got = sent(e_low, e_high, "gx")

    def sources(wanted, after):
        return call(
            functools.partial(source_kernel, wanted, steps, wells, ry), [table, after],
            [sds(len(wanted), 3 * rx, 3 * ry, nz)], "sources", 8, [VMEM, ANY],
        )[0]

    def others(step, after):
        with_acc = step == top - 1
        arrays = own + ([acc_p, acc_s] if with_acc else [])
        leads = [step] * 8 + ([None] * 2 if with_acc else [])
        held, low, high = more(arrays, leads, dims, (after,))
        return held, sent(low, high, "gy"), low

    ready = {top - 1: others(top - 1, blocks)}
    corners = pack_corners("corners", *z_got, (*x_got, ready[top - 1][2]))
    c_got = sent(*corners, "gx")
    src = sources((top,), corners[0])
    sides = {top - 1: sent(*widen(*ready[top - 1][:1], *ready[top - 1][1], (src,)), "gx")}

    ext = (ex, V, 8, nz)
    lam_out = [sds(2, rx, ry, nz), sds(2, rx, H, nz), sds(2, rx, H, nz)]
    well_out = sds(devices, 128)
    fields = [pltpu.VMEM(ext, F32)] * 4 + [pltpu.VMEM((2, ex, ey, nz), F32)]

    geo, lam, low, high, dense = call(
        functools.partial(first_kernel, top, steps, wells),
        [table, src, blocks, *z_got, *x_got, *c_got],
        [sds(5, *ext)] + lam_out + [well_out], "step_top", 16,
        scratch=[pltpu.VMEM((split, ex, ey, nz), F32), pltpu.VMEM((7, *ext), F32)] + fields,
    )

    acc = None
    src = None
    for step in reversed(range(top)):
        last = step == 0
        with_acc = step == top - 1
        if src is None:
            src = sources(tuple(range(top)), low)
        held, m_z, _ = ready[step]
        if step not in sides:
            sides[step] = sent(*widen(held, *m_z, (low,)), "gx")
        made = call(
            functools.partial(prepare_kernel, step, with_acc),
            [src, geo, held, *m_z, *sides[step]] + ([] if with_acc else [acc]),
            [sds(9, *ext)] + ([sds(2, *ext)] if with_acc else []), "prepare", 8,
            scratch=[pltpu.VMEM((10 if with_acc else 8, ex, ey, nz), F32)],
        )
        coef = made[0]
        if with_acc:
            acc = made[1]

        if not last:
            ready[step - 1] = others(step - 1, low)
        l_z = sent(low, high, "gy")
        l_x = sent(*widen(lam, *l_z), "gx")
        outs = [sds(rx, ry, nz)] * 2 if last else lam_out
        outs = call(
            functools.partial(sweep_kernel, last, step, steps, wells),
            [table, coef, geo, held, lam, *l_z, *l_x, dense],
            outs + [well_out], "step", 8, scratch=[pltpu.VMEM((2, *ext), F32)] + fields,
        )
        dense = outs[-1]
        if not last:
            lam, low, high = outs[:3]

    parts = lax.all_to_all(dense[:, None, :], ("gx", "gy"), 0, 0, tiled=True)
    well_grad = jnp.sum(parts, axis=(0, 1))[: wells * steps].reshape(wells, steps)
    return outs[0], outs[1], well_grad


def solution(mesh):
    cells3 = P("gx", "gy", None)
    cells4 = P(None, "gx", "gy", None)
    flat = ("gx", "gy")
    placed = (cells4,) * 2 + (cells3,) * 5 + (cells4,) * 6 + (P(flat, None),) * 3 + (P(flat),) * 3
    return jax.shard_map(
        local,
        mesh=mesh,
        in_specs=placed,
        out_specs=(cells3, cells3, P(flat, None)),
        check_vma=False,
    )
```

```python
import functools

import jax
import jax.numpy as jnp
from jax import lax
from jax.experimental import pallas as pl
from jax.experimental.pallas import tpu as pltpu
from jax.sharding import PartitionSpec as P

SWEEPS = 8
OMEGA = 0.8
KEEP = 1.0 - OMEGA
H = 8
V = 4
HIGHEST = lax.Precision.HIGHEST
F32 = jnp.float32
BF16 = jnp.bfloat16
FLOPS = 1e9

VMEM = pl.BlockSpec(memory_space=pltpu.VMEM)
ANY = pl.BlockSpec(memory_space=pl.ANY)
HBM = pl.BlockSpec(memory_space=pltpu.HBM)


def sds(*shape):
    return jax.ShapeDtypeStruct(shape, F32)


def params(mib):
    return pltpu.CompilerParams(vmem_limit_bytes=mib * 1024 * 1024)


TIMES = {"step_top": 7, "step": 6, "sources": 3, "prepare": 1.5}


def estimate(name):
    work = TIMES.get(name, 0.5)
    return pl.CostEstimate(
        flops=int(work * FLOPS), bytes_accessed=int(work * 3.0e6), transcendentals=0
    )


def call(kernel, ins, outs, name, mib, specs=None, scratch=()):
    return pl.pallas_call(
        kernel,
        in_specs=specs or [VMEM] * len(ins),
        out_specs=[VMEM] * len(outs),
        out_shape=outs,
        scratch_shapes=list(scratch),
        compiler_params=params(mib),
        cost_estimate=estimate(name),
        name=name,
    )(*ins)


def shifted(value, axis, by):
    length = lax.axis_size(axis)
    pairs = [(i, i + by) for i in range(length) if 0 <= i + by < length]
    return lax.ppermute(value, axis, pairs)


def load_kernel(leads, *refs):
    count = len(leads)
    ins, (own, y_low, y_high, token), sems = refs[:count], refs[-5:-1], refs[-1]
    token[...] = jnp.zeros(token.shape, F32)
    copies = [
        pltpu.make_async_copy(
            ins[n] if lead is None else ins[n].at[lead], own.at[n], sems.at[n]
        )
        for n, lead in enumerate(leads)
    ]
    for c in copies:
        c.start()
    for c in copies:
        c.wait()
    y_edges(own, y_low, y_high)


def y_edges(own, low, high):
    ry = own.shape[2]

    def one(n, _):
        low[n] = own[n, :, 0:H, :]
        high[n] = own[n, :, ry - H :, :]
        return 0

    lax.fori_loop(0, own.shape[0], one, 0)


def load(arrays, leads, dims, after):
    n = len(leads)
    rx, ry, nz = dims
    return pl.pallas_call(
        functools.partial(load_kernel, leads),
        in_specs=[HBM] * n + [ANY] * len(after),
        out_specs=[VMEM] * 4,
        out_shape=[sds(n, *dims)] + [sds(n, rx, H, nz)] * 2 + [sds(8, 128)],
        scratch_shapes=[pltpu.SemaphoreType.DMA((n,))],
        name="load",
    )(*arrays, *after)


def more_kernel(plan, count, *refs):
    ins, holders, (y_low, y_high) = refs[:count], refs[count + 1 : -2], refs[-2:]
    rx, ry = y_low.shape[1], holders[0].shape[2]

    def row(x, _):
        for n, (i, lead, h, m) in enumerate(plan):
            value = ins[i][x] if lead is None else ins[i][lead, x]
            holders[h][m, x] = value
            y_low[n, x] = value[0:H]
            y_high[n, x] = value[ry - H :]
        return 0

    lax.fori_loop(0, rx, row, 0)


def more(arrays, plan, sizes, dims, after):
    n = len(plan)
    rx, ry, nz = dims
    return call(
        functools.partial(more_kernel, plan, len(arrays)), list(arrays) + [after],
        [sds(m, *dims) for m in sizes] + [sds(n, rx, H, nz)] * 2, "more", 4,
        [VMEM] * len(arrays) + [ANY],
    )


def fold(rows_of, high):
    tiles = []
    for dx in range(1, 5):
        near, far = rows_of(dx), rows_of(8 - dx)
        sub = lax.broadcasted_iota(jnp.int32, near.shape, 0)
        if high:
            tiles.append(jnp.where(sub < 8 - dx, near, pltpu.roll(far, 8 - dx, 0)))
        else:
            tiles.append(jnp.where(sub >= dx, near, pltpu.roll(far, dx, 0)))
    return tiles


def unfold(tile, dx, high):
    return tile, pltpu.roll(tile, dx if high else 8 - dx, 0)


def corner_tiles(n, z_low, z_high, put):
    rx = z_low.shape[1]
    for side in (0, 1):
        for high, z in ((False, z_low), (True, z_high)):

            def rows_of(dx):
                return z[n, dx - 1 if side == 0 else rx - dx]

            for t, tile in enumerate(fold(rows_of, high)):
                put(side, int(high), t, tile)


def widen_kernel(first, own, z_low, z_high, *refs):
    outs = refs[-2:]
    rx = own.shape[1]

    def one(n, _):
        def put(side, y, t, tile):
            outs[side][n, H + t, y * H : (y + 1) * H, :] = tile

        corner_tiles(n + first, z_low, z_high, put)
        outs[0][n, 0:H] = own[n, 0:H]
        outs[1][n, 0:H] = own[n, rx - H :]
        return 0

    lax.fori_loop(0, own.shape[0], one, 0)


def widen(own, z_low, z_high, after=(), first=0):
    count, rx, ry, nz = own.shape
    return call(
        functools.partial(widen_kernel, first), [own, z_low, z_high, *after],
        [sds(count, H + 4, ry, nz)] * 2, "widen", 4,
        [VMEM] * 3 + [ANY] * len(after),
    )


def table_kernel(steps, *refs):
    ins, out, held, sems = refs[:6], refs[6], refs[7:13], refs[13]
    copies = [pltpu.make_async_copy(i, h, sems.at[n]) for n, (i, h) in enumerate(zip(ins, held))]
    for c in copies:
        c.start()
    for c in copies:
        c.wait()
    rate, bhp, control, perf_well, perf_cell, perf_wi = [h[...] for h in held]
    wells = rate.shape[0]
    effective = jnp.where(control == 1, rate, bhp)
    lane = lax.broadcasted_iota(jnp.int32, (1, 128), 1)
    row = jnp.zeros((1, 128), F32)
    for u in range(wells):
        for n in range(steps):
            row = jnp.where(lane == u * steps + n, effective[u : u + 1, n : n + 1], row)
    mine = jnp.concatenate([row, perf_cell.astype(F32), perf_well.astype(F32), perf_wi])
    out[...] = jnp.broadcast_to(mine[None], out.shape)


def spot():
    n_x, n_y = lax.axis_size("gx"), lax.axis_size("gy")
    x, y = lax.axis_index("gx"), lax.axis_index("gy")
    return x, y, n_x, n_y


def source_kernel(steps, wells, table_ref, _, src_ref):
    here_x, here_y, n_x, n_y = spot()
    count = table_ref.shape[0]
    rx, ry = src_ref.shape[1] - 2 * H, src_ref.shape[2] - 2 * H
    of_wells = table_ref[:, 0, :]
    columns = [
        jnp.broadcast_to(of_wells[:, c : c + 1], (count, 128)) for c in range(wells * steps)
    ]
    owner_iota = lax.broadcasted_iota(jnp.int32, (count, 128), 0)
    sub = lax.broadcasted_iota(jnp.int32, (128, 128), 0)

    def spans(length):
        return ((0, H, length - H), (H, length, 0), (H + length, H, 0))

    for dx, (x0, size_x, from_x) in enumerate(spans(rx)):
        for dy, (y0, size_y, from_y) in enumerate(spans(ry)):
            at_x, at_y = here_x + dx - 1, here_y + dy - 1
            inside = (at_x >= 0) & (at_x < n_x) & (at_y >= 0) & (at_y < n_y)
            slot = table_ref[jnp.where(inside, at_x * n_y + at_y, 0)]
            cell = slot[1:2, :].astype(jnp.int32)
            well = slot[2:3, :].astype(jnp.int32)
            wi = slot[3:4, :] * inside.astype(F32)
            owner = well // wells
            within = well - owner * wells
            hot = owner_iota == owner
            in_lane = sub == (cell & 127)
            pieces = []
            for step in range(steps):
                chosen = columns[step]
                for u in range(1, wells):
                    chosen = jnp.where(within == u, columns[u * steps + step], chosen)
                value = jnp.sum(jnp.where(hot, chosen, 0.0), axis=0, keepdims=True) * wi
                high = value.astype(BF16).astype(F32)
                for piece in (high, value - high):
                    pieces.append(jnp.where(in_lane, piece, 0.0).astype(BF16))
            xi = lax.broadcasted_iota(jnp.int32, (size_x, size_y, 128), 0) + from_x
            yi = lax.broadcasted_iota(jnp.int32, (size_x, size_y, 128), 1) + from_y
            target = (xi * ry + yi).reshape(size_x * size_y, 128)
            by_row = jnp.where(target == (cell >> 7), 1.0, 0.0).astype(BF16)
            found = lax.dot_general(
                by_row, jnp.concatenate(pieces), (((1,), (1,)), ((), ())),
                preferred_element_type=F32,
            )
            for step in range(steps):
                part = found[:, step * 256 : step * 256 + 128]
                part = part + found[:, step * 256 + 128 : step * 256 + 256]
                src_ref[step, x0 : x0 + size_x, y0 : y0 + size_y, :] = part.reshape(
                    size_x, size_y, 128
                )


def by_v(ref, lead, x):
    return jnp.stack([ref[(*lead, x, pl.ds(v, 8, stride=V), slice(None))] for v in range(V)])


def up_v(value):
    return jnp.concatenate([value[1:], pltpu.roll(value[0], 7, 0)[None]])


def down_v(value):
    return jnp.concatenate([pltpu.roll(value[V - 1], 1, 0)[None], value[:-1]])


def roll_z(value, by):
    return pltpu.roll(value, by, 2)


def fill(dst, own, z_low, z_high, sides, first=0):
    count, (rx, ry, nz) = dst.shape[0], own.shape[1:]

    def one(n, _):
        dst[n, H : H + rx, 0:H, :] = z_low[n + first]
        dst[n, H : H + rx, H : H + ry, :] = own[n]
        dst[n, H : H + rx, H + ry : 2 * H + ry, :] = z_high[n + first]
        for side in (0, 1):
            at = side * (H + rx)
            dst[n, at : at + H, H : H + ry, :] = sides[side][n, 0:H]
            for y in (0, 1):
                to = y * (H + ry)
                for t in range(4):
                    tile = sides[side][n, H + t, y * H : (y + 1) * H, :]
                    near, far = unfold(tile, t + 1, y == 1)
                    for dx, row in ((t + 1, near), (7 - t, far)):
                        x = H - dx if side == 0 else H + rx + dx - 1
                        dst[n, x, to : to + H, :] = row
                x = 0 if side == 0 else 2 * H + rx - 1
                dst[n, x, to : to + H, :] = jnp.zeros((H, nz), F32)
        return 0

    lax.fori_loop(0, count, one, 0)


SA, RA, PC, FR, RB, QC, MC, AA, AB = range(9)
TX, TY, TZ, TU, WS = range(5)


def coefficients(raw, base, src_ref, step, x, total):
    c_pp, c_ss, c_ps, c_sp, frac, mob, g_p, g_s = [by_v(raw, (base + n,), x) for n in range(8)]
    den_a = c_pp + total
    den_b = c_ss + mob * total
    s_a = jnp.where(den_a > 0, OMEGA / den_a, 0.0)
    s_b = jnp.where(den_b > 0, OMEGA / den_b, 0.0)
    r_a = g_p + by_v(src_ref, (step,), x)
    return s_a, r_a, c_sp + frac * total, frac, s_b * g_s, s_b * c_ps, s_b * mob, s_b


BLOCK = 2
UNROLL = 4


def sweeps(coef, geo, bufs, lin, begin, ex):
    def work(number, x, count):
        old, new = bufs[(number - 1) % 2], bufs[number % 2]
        tx = [geo[TX, x + r] for r in range(count + 1)]
        values = [[old[f][x - 1 + r] for r in range(count + 2)] for f in range(2)]
        results = []
        for r in range(count):
            at = x + r
            ty = geo[TY, at]
            ty_up = up_v(ty)
            tz, tz_up = geo[TZ, at], geo[TU, at]

            def around(v):
                c = v[r + 1]
                total = tx[r + 1] * v[r + 2] + tx[r] * v[r]
                total = total + (ty_up * up_v(c) + ty * down_v(c))
                total = total + (tz_up * roll_z(c, 127) + tz * roll_z(c, 1))
                return c, total

            a, n_a = around(values[0])
            b, n_b = around(values[1])
            new_a = KEEP * a + coef[SA, at] * (
                (coef[RA, at] + n_a) + (coef[FR, at] * n_b - coef[PC, at] * b)
            )
            new_b = (KEEP * b + coef[RB, at]) + (coef[MC, at] * n_b - coef[QC, at] * a)
            results.append((new_a, new_b))
        for r in range(count):
            for f in range(2):
                if number == SWEEPS:
                    for v in range(V):
                        lin[f, x + r, pl.ds(v, 8, stride=V), :] = results[r][f][v]
                else:
                    new[f][x + r] = results[r][f]

    for number in range(begin, SWEEPS + 1):
        size = BLOCK * UNROLL
        total = ex - 2 * number

        def many(i, _):
            for u in range(UNROLL):
                work(number, number + i * size + u * BLOCK, BLOCK)
            return 0

        lax.fori_loop(0, total // size, many, 0)
        for at in range(total - total % size, total, BLOCK):
            work(number, number + at, BLOCK)


def finish(last, step, steps, wells, lin, frac, table_ref, before, outs):
    rx, ry, nz = frac.shape[-3:]
    out_wells = outs[-1]

    def copy(x, _):
        for f in range(2):
            row = lin[f, H + x, H : H + ry, :]
            if last:
                outs[f][x] = row
            else:
                outs[0][f, x] = row
                outs[1][f, x] = row[0:H]
                outs[2][f, x] = row[ry - H :]
        return 0

    lax.fori_loop(0, rx, copy, 0, unroll=2)
    mix = lin[0, H : H + rx, H : H + ry, :] + frac[...] * lin[1, H : H + rx, H : H + ry, :]
    mix = mix.reshape(rx * ry, nz)
    here_x, here_y, _, n_y = spot()
    slot = table_ref[here_x * n_y + here_y]
    lane = lax.broadcasted_iota(jnp.int32, (128, 128), 1)
    diagonal = lax.broadcasted_iota(jnp.int32, (128, 128), 0) == lane

    def upright(row):
        return jnp.sum(jnp.where(diagonal, row, 0.0), axis=1, keepdims=True)

    cell = upright(slot[1:2, :]).astype(jnp.int32)
    well = upright(slot[2:3, :]).astype(jnp.int32)
    wi = upright(slot[3:4, :])
    by_row = jnp.where(
        lax.broadcasted_iota(jnp.int32, (128, rx * ry), 1) == (cell >> 7), 1.0, 0.0
    ).astype(BF16)
    picked = None
    for _ in range(3):
        piece = mix.astype(BF16)
        mix = mix - piece.astype(F32)
        add = jnp.dot(by_row, piece, preferred_element_type=F32)
        picked = add if picked is None else picked + add
    values = jnp.sum(jnp.where(lane == (cell & 127), picked, 0.0), axis=1, keepdims=True)
    values = values * wi
    owner = well // wells
    spread = jnp.where(lane == (well - owner * wells) * steps + step, values, 0.0)
    flat = slot[2:3, :].astype(jnp.int32) // wells
    count = table_ref.shape[0]
    hot = jnp.where(
        lax.broadcasted_iota(jnp.int32, (count, 128), 0) == flat, 1.0, 0.0
    ).astype(F32)
    dense = jnp.dot(hot, spread, precision=HIGHEST, preferred_element_type=F32)
    if before is not None:
        dense = dense + before[...]
    out_wells[...] = dense


def first_kernel(step, steps, wells, *refs):
    table_ref, src_ref, own, z_low, z_high, x_low, x_high = refs[:7]
    geo = refs[7]
    outs = refs[8:12]
    raw, coef, fa0, fb0, fa1, fb1, lin = refs[12:]
    rx, ry, nz = own.shape[1:]
    ex = rx + 2 * H
    fill(raw, own, z_low, z_high, (x_low, x_high))
    here_x, here_y, _, _ = spot()

    @pl.when(here_x == 0)
    def _():
        raw[0, H, :, :] = jnp.zeros(raw.shape[2:], F32)

    @pl.when(here_y == 0)
    def _():
        def clear(x, _):
            raw[1, x, H : H + 1, :] = jnp.zeros((1, nz), F32)
            return 0

        lax.fori_loop(0, ex, clear, 0)

    def geometry(x, _):
        lane = lax.broadcasted_iota(jnp.int32, (V, 8, nz), 2)
        tz = jnp.where(lane == 0, 0.0, by_v(raw, (2,), x))
        geo[TX, x] = by_v(raw, (0,), x)
        geo[TY, x] = by_v(raw, (1,), x)
        geo[TZ, x] = tz
        geo[TU, x] = roll_z(tz, 127)
        return 0

    lax.fori_loop(0, ex, geometry, 0, unroll=4)

    def prepare(x, _):
        ty = geo[TY, x]
        total = (
            (geo[TX, x + 1] + geo[TX, x]) + (up_v(ty) + ty) + (geo[TU, x] + geo[TZ, x])
        )
        geo[WS, x] = total
        s_a, r_a, p, frac, r_b, q, m, _ = coefficients(
            raw, 3, src_ref, step, x, total
        )
        coef[SA, x] = s_a
        coef[RA, x] = r_a
        coef[PC, x] = p
        coef[FR, x] = frac
        coef[RB, x] = r_b
        coef[QC, x] = q
        coef[MC, x] = m
        fa1[x] = s_a * r_a
        fb1[x] = r_b
        return 0

    lax.fori_loop(0, ex - 1, prepare, 0)
    sweeps(coef, geo, ((fa0, fb0), (fa1, fb1)), lin, 2, ex)
    finish(False, step, steps, wells, lin, own.at[7], table_ref, None, outs)


def prepare_kernel(step, first, with_acc, *refs):
    src_ref, geo, own, z_low, z_high, x_low, x_high = refs[:7]
    if with_acc:
        coef, acc_out, raw = refs[7:]
    else:
        acc, coef, raw = refs[7:]
    rx, ry, nz = own.shape[1:]
    ex = rx + 2 * H
    fill(raw, own, z_low, z_high, (x_low, x_high), first)

    def prepare(x, _):
        s_a, r_a, p, frac, r_b, q, m, s_b = coefficients(
            raw, 0, src_ref, step, x, geo[WS, x]
        )
        coef[SA, x] = s_a
        coef[RA, x] = r_a
        coef[PC, x] = p
        coef[FR, x] = frac
        coef[RB, x] = r_b
        coef[QC, x] = q
        coef[MC, x] = m
        if with_acc:
            a, b = by_v(raw, (8,), x), by_v(raw, (9,), x)
            acc_out[0, x] = a
            acc_out[1, x] = b
        else:
            a, b = acc[0, x], acc[1, x]
        coef[AA, x] = a
        coef[AB, x] = s_b * b
        return 0

    lax.fori_loop(0, ex - 1, prepare, 0)


def sweep_kernel(last, step, steps, wells, *refs):
    table_ref, coef, geo, own, lam, z_low, z_high, x_low, x_high, before = refs[:10]
    outs = refs[10:-6]
    now, fa0, fb0, fa1, fb1, lin = refs[-6:]
    rx, ry, nz = own.shape[1:]
    ex = rx + 2 * H
    fill(lin, lam, z_low, z_high, (x_low, x_high))

    def begin(x, _):
        a, b = by_v(lin, (0,), x), by_v(lin, (1,), x)
        fa0[x] = a
        fb0[x] = b
        now[0, x] = coef[RA, x] + coef[AA, x] * a
        now[1, x] = coef[RB, x] + coef[AB, x] * b
        return 0

    lax.fori_loop(0, ex, begin, 0, unroll=4)

    class Joined:
        def __getitem__(self, at):
            n, x = at
            return now[0, x] if n == RA else now[1, x] if n == RB else coef[n, x]

    sweeps(Joined(), geo, ((fa0, fb0), (fa1, fb1)), lin, 1, ex)
    finish(last, step, steps, wells, lin, own.at[4], table_ref, before, outs)


def local(
    grad_p, grad_s, acc_p, acc_s, trans_x, trans_y, trans_z, c_pp, c_ss, c_ps, c_sp,
    frac, mobility, rate_mis, bhp_mis, control, perf_well, perf_cell, perf_wi,
):
    dims = rx, ry, nz = trans_x.shape
    ex, ey = rx + 2 * H, ry + 2 * H
    steps = grad_p.shape[0]
    wells = rate_mis.shape[0]
    devices = lax.axis_size("gx") * lax.axis_size("gy")
    own = [c_pp, c_ss, c_ps, c_sp, frac, mobility, grad_p, grad_s]
    top = steps - 1

    def sent(low, high, axis):
        return shifted(high, axis, 1), shifted(low, axis, -1)

    arrays = [trans_x, trans_y, trans_z] + own
    leads = [None] * 3 + [top] * 8
    split = len(arrays)
    small = [rate_mis, bhp_mis, control] + [p[None] for p in (perf_well, perf_cell, perf_wi)]
    mine = pl.pallas_call(
        functools.partial(table_kernel, steps),
        in_specs=[HBM] * 6,
        out_specs=VMEM,
        out_shape=sds(devices, 4, 128),
        scratch_shapes=[pltpu.VMEM(p.shape, p.dtype) for p in small]
        + [pltpu.SemaphoreType.DMA((6,))],
        name="table",
    )(*small)
    table = lax.all_to_all(mine, ("gx", "gy"), 0, 0, tiled=True)

    blocks, y_low, y_high, token = load(arrays, leads, dims, (table,))
    z_got = sent(y_low, y_high, "gy")
    plan, places, sizes = [], {}, []
    for h, step in enumerate(reversed(range(top))):
        places[step] = len(plan)
        plan += [(n, step, h, n) for n in range(8)]
        if h == 0:
            plan += [(8, None, h, 8), (9, None, h, 9)]
        sizes.append(len(plan) - places[step])
    *holders, m_low, m_high = more(own + [acc_p, acc_s], plan, sizes, dims, token)
    m_z = sent(m_low, m_high, "gy")
    held = dict(zip(reversed(range(top)), holders))

    wide = widen(blocks, *z_got)
    x_got = sent(*wide, "gx")
    src = call(
        functools.partial(source_kernel, steps, wells), [table, wide[0]],
        [sds(steps, ex, ey, nz)], "sources", 8, [VMEM, ANY],
    )[0]

    def beside(step, after):
        return sent(*widen(held[step], *m_z, (after,), places[step]), "gx")

    sides = beside(top - 1, src)

    ext = (ex, V, 8, nz)
    lam_out = [sds(2, rx, ry, nz), sds(2, rx, H, nz), sds(2, rx, H, nz)]
    well_out = sds(devices, 128)
    fields = [pltpu.VMEM(ext, F32)] * 4 + [pltpu.VMEM((2, ex, ey, nz), F32)]

    geo, lam, low, high, dense = call(
        functools.partial(first_kernel, top, steps, wells),
        [table, src, blocks, *z_got, *x_got],
        [sds(5, *ext)] + lam_out + [well_out], "step_top", 16,
        scratch=[pltpu.VMEM((split, ex, ey, nz), F32), pltpu.VMEM((7, *ext), F32)] + fields,
    )

    acc = None
    for step in reversed(range(top)):
        last = step == 0
        with_acc = step == top - 1
        if not with_acc:
            sides = beside(step, coef)
        made = call(
            functools.partial(prepare_kernel, step, places[step], with_acc),
            [src, geo, held[step], *m_z, *sides] + ([] if with_acc else [acc]),
            [sds(9, *ext)] + ([sds(2, *ext)] if with_acc else []), "prepare", 8,
            scratch=[pltpu.VMEM((10 if with_acc else 8, ex, ey, nz), F32)],
        )
        coef = made[0]
        if with_acc:
            acc = made[1]

        l_z = sent(low, high, "gy")
        l_x = sent(*widen(lam, *l_z), "gx")
        outs = [sds(rx, ry, nz)] * 2 if last else lam_out
        outs = call(
            functools.partial(sweep_kernel, last, step, steps, wells),
            [table, coef, geo, held[step], lam, *l_z, *l_x, dense],
            outs + [well_out], "step", 8, scratch=[pltpu.VMEM((2, *ext), F32)] + fields,
        )
        dense = outs[-1]
        if not last:
            lam, low, high = outs[:3]

    parts = lax.all_to_all(dense[:, None, :], ("gx", "gy"), 0, 0, tiled=True)
    well_grad = jnp.sum(parts, axis=(0, 1))[: wells * steps].reshape(wells, steps)
    return outs[0], outs[1], well_grad


def solution(mesh):
    cells3 = P("gx", "gy", None)
    cells4 = P(None, "gx", "gy", None)
    flat = ("gx", "gy")
    placed = (cells4,) * 2 + (cells3,) * 5 + (cells4,) * 6 + (P(flat, None),) * 3 + (P(flat),) * 3
    return jax.shard_map(
        local,
        mesh=mesh,
        in_specs=placed,
        out_specs=(cells3, cells3, P(flat, None)),
        check_vma=False,
    )
```

```python
import functools

import jax
import jax.numpy as jnp
from jax import lax
from jax.experimental import pallas as pl
from jax.experimental.pallas import tpu as pltpu
from jax.sharding import PartitionSpec as P

SWEEPS = 8
OMEGA = 0.8
KEEP = 1.0 - OMEGA
H = 8
V = 4
HIGHEST = lax.Precision.HIGHEST
F32 = jnp.float32
BF16 = jnp.bfloat16
FLOPS = 1e9

VMEM = pl.BlockSpec(memory_space=pltpu.VMEM)
ANY = pl.BlockSpec(memory_space=pl.ANY)
HBM = pl.BlockSpec(memory_space=pltpu.HBM)


def sds(*shape):
    return jax.ShapeDtypeStruct(shape, F32)


def params(mib):
    return pltpu.CompilerParams(vmem_limit_bytes=mib * 1024 * 1024)


TIMES = {"step_top": 7, "step": 6, "sources": 3, "prepare": 1.5}


def estimate(name):
    work = TIMES.get(name, 0.5)
    return pl.CostEstimate(
        flops=int(work * FLOPS), bytes_accessed=int(work * 3.0e6), transcendentals=0
    )


def call(kernel, ins, outs, name, mib, specs=None, scratch=()):
    return pl.pallas_call(
        kernel,
        in_specs=specs or [VMEM] * len(ins),
        out_specs=[VMEM] * len(outs),
        out_shape=outs,
        scratch_shapes=list(scratch),
        compiler_params=params(mib),
        cost_estimate=estimate(name),
        name=name,
    )(*ins)


def shifted(value, axis, by):
    length = lax.axis_size(axis)
    pairs = [(i, i + by) for i in range(length) if 0 <= i + by < length]
    return lax.ppermute(value, axis, pairs)


def load_kernel(leads, *refs):
    count = len(leads)
    ins, (own, y_low, y_high, token), sems = refs[:count], refs[-5:-1], refs[-1]
    token[...] = jnp.zeros(token.shape, F32)
    copies = [
        pltpu.make_async_copy(
            ins[n] if lead is None else ins[n].at[lead], own.at[n], sems.at[n]
        )
        for n, lead in enumerate(leads)
    ]
    for c in copies:
        c.start()
    for c in copies:
        c.wait()
    y_edges(own, y_low, y_high)


def y_edges(own, low, high):
    ry = own.shape[2]

    def one(n, _):
        low[n] = own[n, :, 0:H, :]
        high[n] = own[n, :, ry - H :, :]
        return 0

    lax.fori_loop(0, own.shape[0], one, 0)


def load(arrays, leads, dims, after):
    n = len(leads)
    rx, ry, nz = dims
    return pl.pallas_call(
        functools.partial(load_kernel, leads),
        in_specs=[HBM] * n + [ANY] * len(after),
        out_specs=[VMEM] * 4,
        out_shape=[sds(n, *dims)] + [sds(n, rx, H, nz)] * 2 + [sds(8, 128)],
        scratch_shapes=[pltpu.SemaphoreType.DMA((n,))],
        name="load",
    )(*arrays, *after)


def more_kernel(plan, count, *refs):
    ins, holders, (y_low, y_high) = refs[:count], refs[count + 1 : -2], refs[-2:]
    rx, ry = y_low.shape[1], holders[0].shape[2]

    def row(x, _):
        for n, (i, lead, h, m) in enumerate(plan):
            value = ins[i][x] if lead is None else ins[i][lead, x]
            holders[h][m, x] = value
            y_low[n, x] = value[0:H]
            y_high[n, x] = value[ry - H :]
        return 0

    lax.fori_loop(0, rx, row, 0)


def more(arrays, plan, sizes, dims, after):
    n = len(plan)
    rx, ry, nz = dims
    return call(
        functools.partial(more_kernel, plan, len(arrays)), list(arrays) + [after],
        [sds(m, *dims) for m in sizes] + [sds(n, rx, H, nz)] * 2, "more", 4,
        [VMEM] * len(arrays) + [ANY],
    )


def tiles_of(reach):
    return reach // 2


def rows_of_array(reach):
    return reach + tiles_of(reach)


def fold(row, reach, high):
    tiles = []
    for dx in range(1, tiles_of(reach) + 1):
        near, far = row(dx), row(reach - dx)
        sub = lax.broadcasted_iota(jnp.int32, near.shape, 0)
        if high:
            tiles.append(jnp.where(sub < 8 - dx, near, pltpu.roll(far, 8 - dx, 0)))
        else:
            tiles.append(jnp.where(sub >= dx, near, pltpu.roll(far, dx, 0)))
    return tiles


def unfold(tile, dx, high):
    return tile, pltpu.roll(tile, dx if high else 8 - dx, 0)


def parts_of(reaches):
    parts, row = [], 0
    for n, reach in enumerate(reaches):
        if parts and parts[-1][2] == reach:
            parts[-1][1] += 1
        else:
            parts.append([n, 1, reach, row])
        row += rows_of_array(reach)
    return parts, row


def widen_kernel(reaches, first, own, z_low, z_high, *refs):
    outs = refs[-2:]
    rx = own.shape[1]
    for begin, count, reach, base in parts_of(reaches)[0]:

        def one(k, _):
            n = begin + k
            at = base + k * rows_of_array(reach)
            for side in (0, 1):
                start = 0 if side == 0 else rx - reach
                outs[side][pl.ds(at, reach)] = own[n, start : start + reach]
                for high, z in ((0, z_low), (1, z_high)):

                    def row(dx):
                        return z[n + first, dx - 1 if side == 0 else rx - dx]

                    for t, tile in enumerate(fold(row, reach, high == 1)):
                        outs[side][at + reach + t, high * H : (high + 1) * H, :] = tile
            return 0

        lax.fori_loop(0, count, one, 0)


def widen(own, reaches, z_low, z_high, after=(), first=0):
    _, rx, ry, nz = own.shape
    return call(
        functools.partial(widen_kernel, reaches, first), [own, z_low, z_high, *after],
        [sds(parts_of(reaches)[1], ry, nz)] * 2, "widen", 4, [VMEM] * 3 + [ANY] * len(after),
    )


def table_kernel(steps, *refs):
    ins, out, held, sems = refs[:6], refs[6], refs[7:13], refs[13]
    copies = [pltpu.make_async_copy(i, h, sems.at[n]) for n, (i, h) in enumerate(zip(ins, held))]
    for c in copies:
        c.start()
    for c in copies:
        c.wait()
    rate, bhp, control, perf_well, perf_cell, perf_wi = [h[...] for h in held]
    wells = rate.shape[0]
    effective = jnp.where(control == 1, rate, bhp)
    lane = lax.broadcasted_iota(jnp.int32, (1, 128), 1)
    row = jnp.zeros((1, 128), F32)
    for u in range(wells):
        for n in range(steps):
            row = jnp.where(lane == u * steps + n, effective[u : u + 1, n : n + 1], row)
    mine = jnp.concatenate([row, perf_cell.astype(F32), perf_well.astype(F32), perf_wi])
    out[...] = jnp.broadcast_to(mine[None], out.shape)


def spot():
    n_x, n_y = lax.axis_size("gx"), lax.axis_size("gy")
    x, y = lax.axis_index("gx"), lax.axis_index("gy")
    return x, y, n_x, n_y


def source_kernel(steps, wells, table_ref, _, src_ref):
    here_x, here_y, n_x, n_y = spot()
    count = table_ref.shape[0]
    rx, ry = src_ref.shape[1] - 2 * H, src_ref.shape[2] - 2 * H
    of_wells = table_ref[:, 0, :]
    columns = [
        jnp.broadcast_to(of_wells[:, c : c + 1], (count, 128)) for c in range(wells * steps)
    ]
    owner_iota = lax.broadcasted_iota(jnp.int32, (count, 128), 0)
    sub = lax.broadcasted_iota(jnp.int32, (128, 128), 0)

    def spans(length):
        return ((0, H, length - H), (H, length, 0), (H + length, H, 0))

    for dx, (x0, size_x, from_x) in enumerate(spans(rx)):
        for dy, (y0, size_y, from_y) in enumerate(spans(ry)):
            at_x, at_y = here_x + dx - 1, here_y + dy - 1
            inside = (at_x >= 0) & (at_x < n_x) & (at_y >= 0) & (at_y < n_y)
            slot = table_ref[jnp.where(inside, at_x * n_y + at_y, 0)]
            cell = slot[1:2, :].astype(jnp.int32)
            well = slot[2:3, :].astype(jnp.int32)
            wi = slot[3:4, :] * inside.astype(F32)
            owner = well // wells
            within = well - owner * wells
            hot = owner_iota == owner
            in_lane = sub == (cell & 127)
            pieces = []
            for step in range(steps):
                chosen = columns[step]
                for u in range(1, wells):
                    chosen = jnp.where(within == u, columns[u * steps + step], chosen)
                value = jnp.sum(jnp.where(hot, chosen, 0.0), axis=0, keepdims=True) * wi
                high = value.astype(BF16).astype(F32)
                for piece in (high, value - high):
                    pieces.append(jnp.where(in_lane, piece, 0.0).astype(BF16))
            xi = lax.broadcasted_iota(jnp.int32, (size_x, size_y, 128), 0) + from_x
            yi = lax.broadcasted_iota(jnp.int32, (size_x, size_y, 128), 1) + from_y
            target = (xi * ry + yi).reshape(size_x * size_y, 128)
            by_row = jnp.where(target == (cell >> 7), 1.0, 0.0).astype(BF16)
            found = lax.dot_general(
                by_row, jnp.concatenate(pieces), (((1,), (1,)), ((), ())),
                preferred_element_type=F32,
            )
            for step in range(steps):
                part = found[:, step * 256 : step * 256 + 128]
                part = part + found[:, step * 256 + 128 : step * 256 + 256]
                src_ref[step, x0 : x0 + size_x, y0 : y0 + size_y, :] = part.reshape(
                    size_x, size_y, 128
                )


def by_v(ref, lead, x):
    return jnp.stack([ref[(*lead, x, pl.ds(v, 8, stride=V), slice(None))] for v in range(V)])


def up_v(value):
    return jnp.concatenate([value[1:], pltpu.roll(value[0], 7, 0)[None]])


def down_v(value):
    return jnp.concatenate([pltpu.roll(value[V - 1], 1, 0)[None], value[:-1]])


def roll_z(value, by):
    return pltpu.roll(value, by, 2)


def fill(dst, own, reaches, z_low, z_high, sides, first=0):
    rx, ry, nz = own.shape[1:]
    for begin, count, reach, base in parts_of(reaches)[0]:

        def one(k, _):
            n = begin + k
            row = base + k * rows_of_array(reach)
            dst[n, H : H + rx, 0:H, :] = z_low[n + first]
            dst[n, H : H + rx, H : H + ry, :] = own[n]
            dst[n, H : H + rx, H + ry : 2 * H + ry, :] = z_high[n + first]
            for side in (0, 1):
                at = H - reach if side == 0 else H + rx
                dst[n, at : at + reach, H : H + ry, :] = sides[side][pl.ds(row, reach)]
                known = set()
                for y in (0, 1):
                    to = y * (H + ry)
                    for t in range(tiles_of(reach)):
                        tile = sides[side][row + reach + t, y * H : (y + 1) * H, :]
                        near, far = unfold(tile, t + 1, y == 1)
                        for dx, value in ((t + 1, near), (reach - t - 1, far)):
                            x = H - dx if side == 0 else H + rx + dx - 1
                            dst[n, x, to : to + H, :] = value
                            known.add(dx)
                for dx in range(1, H + 1):
                    x = H - dx if side == 0 else H + rx + dx - 1
                    if dx not in known:
                        for y in (0, H + ry):
                            dst[n, x, y : y + H, :] = jnp.zeros((H, nz), F32)
                    if dx > reach:
                        dst[n, x, H : H + ry, :] = jnp.zeros((ry, nz), F32)
            return 0

        lax.fori_loop(0, count, one, 0)


GEO, COEF = 8, 7
TOP_REACH = (GEO,) * 3 + (COEF,) * 8
LAM_REACH = (GEO,) * 2


SA, RA, PC, FR, RB, QC, MC, AA, AB = range(9)
TX, TY, TZ, TU, WS = range(5)


def coefficients(raw, base, src_ref, step, x, total):
    c_pp, c_ss, c_ps, c_sp, frac, mob, g_p, g_s = [by_v(raw, (base + n,), x) for n in range(8)]
    den_a = c_pp + total
    den_b = c_ss + mob * total
    s_a = jnp.where(den_a > 0, OMEGA / den_a, 0.0)
    s_b = jnp.where(den_b > 0, OMEGA / den_b, 0.0)
    r_a = g_p + by_v(src_ref, (step,), x)
    return s_a, r_a, c_sp + frac * total, frac, s_b * g_s, s_b * c_ps, s_b * mob, s_b


BLOCK = 2
UNROLL = 4


def sweeps(coef, geo, bufs, lin, begin, ex):
    def work(number, x, count):
        old, new = bufs[(number - 1) % 2], bufs[number % 2]
        tx = [geo[TX, x + r] for r in range(count + 1)]
        values = [[old[f][x - 1 + r] for r in range(count + 2)] for f in range(2)]
        results = []
        for r in range(count):
            at = x + r
            ty = geo[TY, at]
            ty_up = up_v(ty)
            tz, tz_up = geo[TZ, at], geo[TU, at]

            def around(v):
                c = v[r + 1]
                total = tx[r + 1] * v[r + 2] + tx[r] * v[r]
                total = total + (ty_up * up_v(c) + ty * down_v(c))
                total = total + (tz_up * roll_z(c, 127) + tz * roll_z(c, 1))
                return c, total

            a, n_a = around(values[0])
            b, n_b = around(values[1])
            new_a = KEEP * a + coef[SA, at] * (
                (coef[RA, at] + n_a) + (coef[FR, at] * n_b - coef[PC, at] * b)
            )
            new_b = (KEEP * b + coef[RB, at]) + (coef[MC, at] * n_b - coef[QC, at] * a)
            results.append((new_a, new_b))
        for r in range(count):
            for f in range(2):
                if number == SWEEPS:
                    for v in range(V):
                        lin[f, x + r, pl.ds(v, 8, stride=V), :] = results[r][f][v]
                else:
                    new[f][x + r] = results[r][f]

    for number in range(begin, SWEEPS + 1):
        size = BLOCK * UNROLL
        total = ex - 2 * number

        def many(i, _):
            for u in range(UNROLL):
                work(number, number + i * size + u * BLOCK, BLOCK)
            return 0

        lax.fori_loop(0, total // size, many, 0)
        for at in range(total - total % size, total, BLOCK):
            work(number, number + at, BLOCK)


def finish(last, step, steps, wells, lin, frac, table_ref, before, outs):
    rx, ry, nz = frac.shape[-3:]
    out_wells = outs[-1]

    def copy(x, _):
        for f in range(2):
            row = lin[f, H + x, H : H + ry, :]
            if last:
                outs[f][x] = row
            else:
                outs[0][f, x] = row
                outs[1][f, x] = row[0:H]
                outs[2][f, x] = row[ry - H :]
        return 0

    lax.fori_loop(0, rx, copy, 0, unroll=2)
    mix = lin[0, H : H + rx, H : H + ry, :] + frac[...] * lin[1, H : H + rx, H : H + ry, :]
    mix = mix.reshape(rx * ry, nz)
    here_x, here_y, _, n_y = spot()
    slot = table_ref[here_x * n_y + here_y]
    lane = lax.broadcasted_iota(jnp.int32, (128, 128), 1)
    diagonal = lax.broadcasted_iota(jnp.int32, (128, 128), 0) == lane

    def upright(row):
        return jnp.sum(jnp.where(diagonal, row, 0.0), axis=1, keepdims=True)

    cell = upright(slot[1:2, :]).astype(jnp.int32)
    well = upright(slot[2:3, :]).astype(jnp.int32)
    wi = upright(slot[3:4, :])
    by_row = jnp.where(
        lax.broadcasted_iota(jnp.int32, (128, rx * ry), 1) == (cell >> 7), 1.0, 0.0
    ).astype(BF16)
    picked = None
    for _ in range(3):
        piece = mix.astype(BF16)
        mix = mix - piece.astype(F32)
        add = jnp.dot(by_row, piece, preferred_element_type=F32)
        picked = add if picked is None else picked + add
    values = jnp.sum(jnp.where(lane == (cell & 127), picked, 0.0), axis=1, keepdims=True)
    values = values * wi
    owner = well // wells
    spread = jnp.where(lane == (well - owner * wells) * steps + step, values, 0.0)
    flat = slot[2:3, :].astype(jnp.int32) // wells
    count = table_ref.shape[0]
    hot = jnp.where(
        lax.broadcasted_iota(jnp.int32, (count, 128), 0) == flat, 1.0, 0.0
    ).astype(F32)
    dense = jnp.dot(hot, spread, precision=HIGHEST, preferred_element_type=F32)
    if before is not None:
        dense = dense + before[...]
    out_wells[...] = dense


def first_kernel(step, steps, wells, *refs):
    table_ref, src_ref, own, z_low, z_high, x_low, x_high = refs[:7]
    geo = refs[7]
    outs = refs[8:12]
    raw, coef, fa0, fb0, fa1, fb1, lin = refs[12:]
    rx, ry, nz = own.shape[1:]
    ex = rx + 2 * H
    fill(raw, own, TOP_REACH, z_low, z_high, (x_low, x_high))
    here_x, here_y, _, _ = spot()

    @pl.when(here_x == 0)
    def _():
        raw[0, H, :, :] = jnp.zeros(raw.shape[2:], F32)

    @pl.when(here_y == 0)
    def _():
        def clear(x, _):
            raw[1, x, H : H + 1, :] = jnp.zeros((1, nz), F32)
            return 0

        lax.fori_loop(0, ex, clear, 0)

    def geometry(x, _):
        lane = lax.broadcasted_iota(jnp.int32, (V, 8, nz), 2)
        tz = jnp.where(lane == 0, 0.0, by_v(raw, (2,), x))
        geo[TX, x] = by_v(raw, (0,), x)
        geo[TY, x] = by_v(raw, (1,), x)
        geo[TZ, x] = tz
        geo[TU, x] = roll_z(tz, 127)
        return 0

    lax.fori_loop(0, ex, geometry, 0, unroll=4)

    def prepare(x, _):
        ty = geo[TY, x]
        total = (
            (geo[TX, x + 1] + geo[TX, x]) + (up_v(ty) + ty) + (geo[TU, x] + geo[TZ, x])
        )
        geo[WS, x] = total
        s_a, r_a, p, frac, r_b, q, m, _ = coefficients(
            raw, 3, src_ref, step, x, total
        )
        coef[SA, x] = s_a
        coef[RA, x] = r_a
        coef[PC, x] = p
        coef[FR, x] = frac
        coef[RB, x] = r_b
        coef[QC, x] = q
        coef[MC, x] = m
        fa1[x] = s_a * r_a
        fb1[x] = r_b
        return 0

    lax.fori_loop(0, ex - 1, prepare, 0)
    sweeps(coef, geo, ((fa0, fb0), (fa1, fb1)), lin, 2, ex)
    finish(False, step, steps, wells, lin, own.at[7], table_ref, None, outs)


def prepare_kernel(step, first, with_acc, *refs):
    src_ref, geo, own, z_low, z_high, x_low, x_high = refs[:7]
    if with_acc:
        coef, acc_out, raw = refs[7:]
    else:
        acc, coef, raw = refs[7:]
    rx, ry, nz = own.shape[1:]
    ex = rx + 2 * H
    fill(raw, own, (COEF,) * own.shape[0], z_low, z_high, (x_low, x_high), first)

    def prepare(x, _):
        s_a, r_a, p, frac, r_b, q, m, s_b = coefficients(
            raw, 0, src_ref, step, x, geo[WS, x]
        )
        coef[SA, x] = s_a
        coef[RA, x] = r_a
        coef[PC, x] = p
        coef[FR, x] = frac
        coef[RB, x] = r_b
        coef[QC, x] = q
        coef[MC, x] = m
        if with_acc:
            a, b = by_v(raw, (8,), x), by_v(raw, (9,), x)
            acc_out[0, x] = a
            acc_out[1, x] = b
        else:
            a, b = acc[0, x], acc[1, x]
        coef[AA, x] = a
        coef[AB, x] = s_b * b
        return 0

    lax.fori_loop(0, ex - 1, prepare, 0)


def sweep_kernel(last, step, steps, wells, *refs):
    table_ref, coef, geo, own, lam, z_low, z_high, x_low, x_high, before = refs[:10]
    outs = refs[10:-6]
    now, fa0, fb0, fa1, fb1, lin = refs[-6:]
    rx, ry, nz = own.shape[1:]
    ex = rx + 2 * H
    fill(lin, lam, LAM_REACH, z_low, z_high, (x_low, x_high))

    def begin(x, _):
        a, b = by_v(lin, (0,), x), by_v(lin, (1,), x)
        fa0[x] = a
        fb0[x] = b
        now[0, x] = coef[RA, x] + coef[AA, x] * a
        now[1, x] = coef[RB, x] + coef[AB, x] * b
        return 0

    lax.fori_loop(0, ex, begin, 0, unroll=4)

    class Joined:
        def __getitem__(self, at):
            n, x = at
            return now[0, x] if n == RA else now[1, x] if n == RB else coef[n, x]

    sweeps(Joined(), geo, ((fa0, fb0), (fa1, fb1)), lin, 1, ex)
    finish(last, step, steps, wells, lin, own.at[4], table_ref, before, outs)


def local(
    grad_p, grad_s, acc_p, acc_s, trans_x, trans_y, trans_z, c_pp, c_ss, c_ps, c_sp,
    frac, mobility, rate_mis, bhp_mis, control, perf_well, perf_cell, perf_wi,
):
    dims = rx, ry, nz = trans_x.shape
    ex, ey = rx + 2 * H, ry + 2 * H
    steps = grad_p.shape[0]
    wells = rate_mis.shape[0]
    devices = lax.axis_size("gx") * lax.axis_size("gy")
    own = [c_pp, c_ss, c_ps, c_sp, frac, mobility, grad_p, grad_s]
    top = steps - 1

    def sent(low, high, axis):
        return shifted(high, axis, 1), shifted(low, axis, -1)

    arrays = [trans_x, trans_y, trans_z] + own
    leads = [None] * 3 + [top] * 8
    split = len(arrays)
    small = [rate_mis, bhp_mis, control] + [p[None] for p in (perf_well, perf_cell, perf_wi)]
    mine = pl.pallas_call(
        functools.partial(table_kernel, steps),
        in_specs=[HBM] * 6,
        out_specs=VMEM,
        out_shape=sds(devices, 4, 128),
        scratch_shapes=[pltpu.VMEM(p.shape, p.dtype) for p in small]
        + [pltpu.SemaphoreType.DMA((6,))],
        name="table",
    )(*small)
    blocks, y_low, y_high, token = load(arrays, leads, dims, (mine,))
    z_got = sent(y_low, y_high, "gy")
    mine, _ = lax.optimization_barrier((mine, token))
    table = lax.all_to_all(mine, ("gx", "gy"), 0, 0, tiled=True)

    wide = widen(blocks, TOP_REACH, *z_got, (table,))
    x_got = sent(*wide, "gx")
    src = call(
        functools.partial(source_kernel, steps, wells), [table, wide[0]],
        [sds(steps, ex, ey, nz)], "sources", 8, [VMEM, ANY],
    )[0]

    plan, places, sizes = [], {}, []
    for h, step in enumerate(reversed(range(top))):
        places[step] = len(plan)
        plan += [(n, step, h, n) for n in range(8)]
        if h == 0:
            plan += [(8, None, h, 8), (9, None, h, 9)]
        sizes.append(len(plan) - places[step])
    *holders, m_low, m_high = more(own + [acc_p, acc_s], plan, sizes, dims, table)
    m_z = sent(m_low, m_high, "gy")
    held = dict(zip(reversed(range(top)), holders))

    def beside(step, after):
        group = held[step]
        return sent(
            *widen(group, (COEF,) * group.shape[0], *m_z, (after,), places[step]), "gx"
        )

    sides = beside(top - 1, src)

    ext = (ex, V, 8, nz)
    lam_out = [sds(2, rx, ry, nz), sds(2, rx, H, nz), sds(2, rx, H, nz)]
    well_out = sds(devices, 128)
    fields = [pltpu.VMEM(ext, F32)] * 4 + [pltpu.VMEM((2, ex, ey, nz), F32)]

    geo, lam, low, high, dense = call(
        functools.partial(first_kernel, top, steps, wells),
        [table, src, blocks, *z_got, *x_got],
        [sds(5, *ext)] + lam_out + [well_out], "step_top", 16,
        scratch=[pltpu.VMEM((split, ex, ey, nz), F32), pltpu.VMEM((7, *ext), F32)] + fields,
    )

    acc = None
    for step in reversed(range(top)):
        last = step == 0
        with_acc = step == top - 1
        if not with_acc:
            sides = beside(step, coef)
        made = call(
            functools.partial(prepare_kernel, step, places[step], with_acc),
            [src, geo, held[step], *m_z, *sides] + ([] if with_acc else [acc]),
            [sds(9, *ext)] + ([sds(2, *ext)] if with_acc else []), "prepare", 8,
            scratch=[pltpu.VMEM((10 if with_acc else 8, ex, ey, nz), F32)],
        )
        coef = made[0]
        if with_acc:
            acc = made[1]

        l_z = sent(low, high, "gy")
        l_x = sent(*widen(lam, LAM_REACH, *l_z), "gx")
        outs = [sds(rx, ry, nz)] * 2 if last else lam_out
        outs = call(
            functools.partial(sweep_kernel, last, step, steps, wells),
            [table, coef, geo, held[step], lam, *l_z, *l_x, dense],
            outs + [well_out], "step", 8, scratch=[pltpu.VMEM((2, *ext), F32)] + fields,
        )
        dense = outs[-1]
        if not last:
            lam, low, high = outs[:3]

    parts = lax.all_to_all(dense[:, None, :], ("gx", "gy"), 0, 0, tiled=True)
    well_grad = jnp.sum(parts, axis=(0, 1))[: wells * steps].reshape(wells, steps)
    return outs[0], outs[1], well_grad


def solution(mesh):
    cells3 = P("gx", "gy", None)
    cells4 = P(None, "gx", "gy", None)
    flat = ("gx", "gy")
    placed = (cells4,) * 2 + (cells3,) * 5 + (cells4,) * 6 + (P(flat, None),) * 3 + (P(flat),) * 3
    return jax.shard_map(
        local,
        mesh=mesh,
        in_specs=placed,
        out_specs=(cells3, cells3, P(flat, None)),
        check_vma=False,
    )
```

```python
import functools

import jax
import jax.numpy as jnp
from jax import lax
from jax.experimental import pallas as pl
from jax.experimental.pallas import tpu as pltpu
from jax.sharding import PartitionSpec as P

SWEEPS = 8
OMEGA = 0.8
KEEP = 1.0 - OMEGA
H = 8
V = 4
HIGHEST = lax.Precision.HIGHEST
F32 = jnp.float32
BF16 = jnp.bfloat16
FLOPS = 1e9

VMEM = pl.BlockSpec(memory_space=pltpu.VMEM)
ANY = pl.BlockSpec(memory_space=pl.ANY)
HBM = pl.BlockSpec(memory_space=pltpu.HBM)


def sds(*shape):
    return jax.ShapeDtypeStruct(shape, F32)


def params(mib):
    return pltpu.CompilerParams(vmem_limit_bytes=mib * 1024 * 1024)


TIMES = {"step_top": 7, "step": 6, "sources": 3, "prepare": 1.5}


def estimate(name):
    work = TIMES.get(name, 0.5)
    return pl.CostEstimate(
        flops=int(work * FLOPS), bytes_accessed=int(work * 3.0e6), transcendentals=0
    )


def call(kernel, ins, outs, name, mib, specs=None, scratch=()):
    return pl.pallas_call(
        kernel,
        in_specs=specs or [VMEM] * len(ins),
        out_specs=[VMEM] * len(outs),
        out_shape=outs,
        scratch_shapes=list(scratch),
        compiler_params=params(mib),
        cost_estimate=estimate(name),
        name=name,
    )(*ins)


def swaps(first, second, axis):
    length = lax.axis_size(axis)
    even = [(i, i ^ 1) for i in range(length) if i ^ 1 < length]
    odd = [(i, i + 1) for i in range(1, length - 1, 2)]
    odd += [(j, i) for i, j in odd]
    return lax.ppermute(first, axis, even), lax.ppermute(second, axis, odd)


def by_side(axis, work, first, second):
    at = lax.axis_index(axis) % 2

    @pl.when(at == 1)
    def _():
        work(first, second)

    @pl.when(at == 0)
    def _():
        work(second, first)


def load_kernel(leads, *refs):
    count = len(leads)
    ins, (own, y_low, y_high, token), sems = refs[:count], refs[-5:-1], refs[-1]
    token[...] = jnp.zeros(token.shape, F32)
    copies = [
        pltpu.make_async_copy(
            ins[n] if lead is None else ins[n].at[lead], own.at[n], sems.at[n]
        )
        for n, lead in enumerate(leads)
    ]
    for c in copies:
        c.start()
    for c in copies:
        c.wait()
    by_side("gy", lambda low, high: y_edges(own, low, high), y_low, y_high)


def y_edges(own, low, high):
    ry = own.shape[2]

    def one(n, _):
        low[n] = own[n, :, 0:H, :]
        high[n] = own[n, :, ry - H :, :]
        return 0

    lax.fori_loop(0, own.shape[0], one, 0)


def load(arrays, leads, dims, after):
    n = len(leads)
    rx, ry, nz = dims
    return pl.pallas_call(
        functools.partial(load_kernel, leads),
        in_specs=[HBM] * n + [ANY] * len(after),
        out_specs=[VMEM] * 4,
        out_shape=[sds(n, *dims)] + [sds(n, rx, H, nz)] * 2 + [sds(8, 128)],
        scratch_shapes=[pltpu.SemaphoreType.DMA((n,))],
        name="load",
    )(*arrays, *after)


def more_kernel(plan, count, *refs):
    ins, holders, (y_low, y_high) = refs[:count], refs[count + 1 : -2], refs[-2:]
    rx, ry = y_low.shape[1], holders[0].shape[2]

    def work(low, high):
        def row(x, _):
            for n, (i, lead, h, m) in enumerate(plan):
                value = ins[i][x] if lead is None else ins[i][lead, x]
                holders[h][m, x] = value
                low[n, x] = value[0:H]
                high[n, x] = value[ry - H :]
            return 0

        lax.fori_loop(0, rx, row, 0)

    by_side("gy", work, y_low, y_high)


def more(arrays, plan, sizes, dims, after):
    n = len(plan)
    rx, ry, nz = dims
    return call(
        functools.partial(more_kernel, plan, len(arrays)), list(arrays) + [after],
        [sds(m, *dims) for m in sizes] + [sds(n, rx, H, nz)] * 2, "more", 4,
        [VMEM] * len(arrays) + [ANY],
    )


def tiles_of(reach):
    return reach // 2


def rows_of_array(reach):
    return reach + tiles_of(reach)


def fold(row, reach, high):
    tiles = []
    for dx in range(1, tiles_of(reach) + 1):
        near, far = row(dx), row(reach - dx)
        sub = lax.broadcasted_iota(jnp.int32, near.shape, 0)
        if high:
            tiles.append(jnp.where(sub < 8 - dx, near, pltpu.roll(far, 8 - dx, 0)))
        else:
            tiles.append(jnp.where(sub >= dx, near, pltpu.roll(far, dx, 0)))
    return tiles


def unfold(tile, dx, high):
    return tile, pltpu.roll(tile, dx if high else 8 - dx, 0)


def parts_of(reaches):
    parts, row = [], 0
    for n, reach in enumerate(reaches):
        if parts and parts[-1][2] == reach:
            parts[-1][1] += 1
        else:
            parts.append([n, 1, reach, row])
        row += rows_of_array(reach)
    return parts, row


def widen_kernel(reaches, first, own, z_first, z_second, *refs):
    rx = own.shape[1]

    def work(z_low, z_high, outs):
        for begin, count, reach, base in parts_of(reaches)[0]:

            def one(k, _):
                n = begin + k
                at = base + k * rows_of_array(reach)
                for side in (0, 1):
                    start = 0 if side == 0 else rx - reach
                    outs[side][pl.ds(at, reach)] = own[n, start : start + reach]
                    for high, z in ((0, z_low), (1, z_high)):

                        def row(dx):
                            return z[n + first, dx - 1 if side == 0 else rx - dx]

                        for t, tile in enumerate(fold(row, reach, high == 1)):
                            outs[side][at + reach + t, high * H : (high + 1) * H, :] = tile
                return 0

            lax.fori_loop(0, count, one, 0)

    def along_x(low, high):
        by_side("gy", lambda a, b: work(a, b, (low, high)), z_first, z_second)

    by_side("gx", along_x, *refs[-2:])


def widen(own, reaches, z_low, z_high, after=(), first=0):
    _, rx, ry, nz = own.shape
    return call(
        functools.partial(widen_kernel, reaches, first), [own, z_low, z_high, *after],
        [sds(parts_of(reaches)[1], ry, nz)] * 2, "widen", 4, [VMEM] * 3 + [ANY] * len(after),
    )


def table_kernel(steps, *refs):
    ins, out, held, sems = refs[:6], refs[6], refs[7:13], refs[13]
    copies = [pltpu.make_async_copy(i, h, sems.at[n]) for n, (i, h) in enumerate(zip(ins, held))]
    for c in copies:
        c.start()
    for c in copies:
        c.wait()
    rate, bhp, control, perf_well, perf_cell, perf_wi = [h[...] for h in held]
    wells = rate.shape[0]
    effective = jnp.where(control == 1, rate, bhp)
    lane = lax.broadcasted_iota(jnp.int32, (1, 128), 1)
    row = jnp.zeros((1, 128), F32)
    for u in range(wells):
        for n in range(steps):
            row = jnp.where(lane == u * steps + n, effective[u : u + 1, n : n + 1], row)
    mine = jnp.concatenate([row, perf_cell.astype(F32), perf_well.astype(F32), perf_wi])
    out[...] = jnp.broadcast_to(mine[None], out.shape)


def spot():
    n_x, n_y = lax.axis_size("gx"), lax.axis_size("gy")
    x, y = lax.axis_index("gx"), lax.axis_index("gy")
    return x, y, n_x, n_y


def source_kernel(steps, wells, table_ref, _, src_ref):
    here_x, here_y, n_x, n_y = spot()
    count = table_ref.shape[0]
    rx, ry = src_ref.shape[1] - 2 * H, src_ref.shape[2] - 2 * H
    of_wells = table_ref[:, 0, :]
    columns = [
        jnp.broadcast_to(of_wells[:, c : c + 1], (count, 128)) for c in range(wells * steps)
    ]
    owner_iota = lax.broadcasted_iota(jnp.int32, (count, 128), 0)
    sub = lax.broadcasted_iota(jnp.int32, (128, 128), 0)

    def spans(length):
        return ((0, H, length - H), (H, length, 0), (H + length, H, 0))

    for dx, (x0, size_x, from_x) in enumerate(spans(rx)):
        for dy, (y0, size_y, from_y) in enumerate(spans(ry)):
            at_x, at_y = here_x + dx - 1, here_y + dy - 1
            inside = (at_x >= 0) & (at_x < n_x) & (at_y >= 0) & (at_y < n_y)
            slot = table_ref[jnp.where(inside, at_x * n_y + at_y, 0)]
            cell = slot[1:2, :].astype(jnp.int32)
            well = slot[2:3, :].astype(jnp.int32)
            wi = slot[3:4, :] * inside.astype(F32)
            owner = well // wells
            within = well - owner * wells
            hot = owner_iota == owner
            in_lane = sub == (cell & 127)
            pieces = []
            for step in range(steps):
                chosen = columns[step]
                for u in range(1, wells):
                    chosen = jnp.where(within == u, columns[u * steps + step], chosen)
                value = jnp.sum(jnp.where(hot, chosen, 0.0), axis=0, keepdims=True) * wi
                high = value.astype(BF16).astype(F32)
                for piece in (high, value - high):
                    pieces.append(jnp.where(in_lane, piece, 0.0).astype(BF16))
            xi = lax.broadcasted_iota(jnp.int32, (size_x, size_y, 128), 0) + from_x
            yi = lax.broadcasted_iota(jnp.int32, (size_x, size_y, 128), 1) + from_y
            target = (xi * ry + yi).reshape(size_x * size_y, 128)
            by_row = jnp.where(target == (cell >> 7), 1.0, 0.0).astype(BF16)
            found = lax.dot_general(
                by_row, jnp.concatenate(pieces), (((1,), (1,)), ((), ())),
                preferred_element_type=F32,
            )
            for step in range(steps):
                part = found[:, step * 256 : step * 256 + 128]
                part = part + found[:, step * 256 + 128 : step * 256 + 256]
                src_ref[step, x0 : x0 + size_x, y0 : y0 + size_y, :] = part.reshape(
                    size_x, size_y, 128
                )


def by_v(ref, lead, x):
    return jnp.stack([ref[(*lead, x, pl.ds(v, 8, stride=V), slice(None))] for v in range(V)])


def up_v(value):
    return jnp.concatenate([value[1:], pltpu.roll(value[0], 7, 0)[None]])


def down_v(value):
    return jnp.concatenate([pltpu.roll(value[V - 1], 1, 0)[None], value[:-1]])


def roll_z(value, by):
    return pltpu.roll(value, by, 2)


def fill(dst, own, reaches, z_got, x_got, first=0):
    rx, ry, nz = own.shape[1:]

    def middle(z_low, z_high):
        def one(n, _):
            dst[n, H : H + rx, 0:H, :] = z_low[n + first]
            dst[n, H : H + rx, H : H + ry, :] = own[n]
            dst[n, H : H + rx, H + ry : 2 * H + ry, :] = z_high[n + first]
            return 0

        lax.fori_loop(0, len(reaches), one, 0)

    def outer(x_low, x_high):
        sides = (x_low, x_high)
        for begin, count, reach, base in parts_of(reaches)[0]:

            def one(k, _):
                n = begin + k
                row = base + k * rows_of_array(reach)
                for side in (0, 1):
                    at = H - reach if side == 0 else H + rx
                    dst[n, at : at + reach, H : H + ry, :] = sides[side][pl.ds(row, reach)]
                    known = set()
                    for y in (0, 1):
                        to = y * (H + ry)
                        for t in range(tiles_of(reach)):
                            tile = sides[side][row + reach + t, y * H : (y + 1) * H, :]
                            near, far = unfold(tile, t + 1, y == 1)
                            for dx, value in ((t + 1, near), (reach - t - 1, far)):
                                x = H - dx if side == 0 else H + rx + dx - 1
                                dst[n, x, to : to + H, :] = value
                                known.add(dx)
                    for dx in range(1, H + 1):
                        x = H - dx if side == 0 else H + rx + dx - 1
                        if dx not in known:
                            for y in (0, H + ry):
                                dst[n, x, y : y + H, :] = jnp.zeros((H, nz), F32)
                        if dx > reach:
                            dst[n, x, H : H + ry, :] = jnp.zeros((ry, nz), F32)
                return 0

            lax.fori_loop(0, count, one, 0)

    by_side("gy", middle, *z_got)
    by_side("gx", outer, *x_got)


GEO, COEF = 8, 7
TOP_REACH = (GEO,) * 3 + (COEF,) * 8
LAM_REACH = (GEO,) * 2


SA, RA, PC, FR, RB, QC, MC, AA, AB = range(9)
TX, TY, TZ, TU, WS = range(5)


def coefficients(raw, base, src_ref, step, x, total):
    c_pp, c_ss, c_ps, c_sp, frac, mob, g_p, g_s = [by_v(raw, (base + n,), x) for n in range(8)]
    den_a = c_pp + total
    den_b = c_ss + mob * total
    s_a = jnp.where(den_a > 0, OMEGA / den_a, 0.0)
    s_b = jnp.where(den_b > 0, OMEGA / den_b, 0.0)
    r_a = g_p + by_v(src_ref, (step,), x)
    return s_a, r_a, c_sp + frac * total, frac, s_b * g_s, s_b * c_ps, s_b * mob, s_b


BLOCK = 2
UNROLL = 4


def sweeps(coef, geo, bufs, lin, begin, ex):
    def work(number, x, count):
        old, new = bufs[(number - 1) % 2], bufs[number % 2]
        tx = [geo[TX, x + r] for r in range(count + 1)]
        values = [[old[f][x - 1 + r] for r in range(count + 2)] for f in range(2)]
        results = []
        for r in range(count):
            at = x + r
            ty = geo[TY, at]
            ty_up = up_v(ty)
            tz, tz_up = geo[TZ, at], geo[TU, at]

            def around(v):
                c = v[r + 1]
                total = tx[r + 1] * v[r + 2] + tx[r] * v[r]
                total = total + (ty_up * up_v(c) + ty * down_v(c))
                total = total + (tz_up * roll_z(c, 127) + tz * roll_z(c, 1))
                return c, total

            a, n_a = around(values[0])
            b, n_b = around(values[1])
            new_a = KEEP * a + coef[SA, at] * (
                (coef[RA, at] + n_a) + (coef[FR, at] * n_b - coef[PC, at] * b)
            )
            new_b = (KEEP * b + coef[RB, at]) + (coef[MC, at] * n_b - coef[QC, at] * a)
            results.append((new_a, new_b))
        for r in range(count):
            for f in range(2):
                if number == SWEEPS:
                    for v in range(V):
                        lin[f, x + r, pl.ds(v, 8, stride=V), :] = results[r][f][v]
                else:
                    new[f][x + r] = results[r][f]

    for number in range(begin, SWEEPS + 1):
        size = BLOCK * UNROLL
        total = ex - 2 * number

        def many(i, _):
            for u in range(UNROLL):
                work(number, number + i * size + u * BLOCK, BLOCK)
            return 0

        lax.fori_loop(0, total // size, many, 0)
        for at in range(total - total % size, total, BLOCK):
            work(number, number + at, BLOCK)


def finish(last, step, steps, wells, lin, frac, table_ref, before, outs):
    rx, ry, nz = frac.shape[-3:]
    out_wells = outs[-1]

    def copies(low, high):
        def copy(x, _):
            for f in range(2):
                row = lin[f, H + x, H : H + ry, :]
                if last:
                    outs[f][x] = row
                else:
                    outs[0][f, x] = row
                    low[f, x] = row[0:H]
                    high[f, x] = row[ry - H :]
            return 0

        lax.fori_loop(0, rx, copy, 0, unroll=2)

    if last:
        copies(None, None)
    else:
        by_side("gy", copies, outs[1], outs[2])
    mix = lin[0, H : H + rx, H : H + ry, :] + frac[...] * lin[1, H : H + rx, H : H + ry, :]
    mix = mix.reshape(rx * ry, nz)
    here_x, here_y, _, n_y = spot()
    slot = table_ref[here_x * n_y + here_y]
    lane = lax.broadcasted_iota(jnp.int32, (128, 128), 1)
    diagonal = lax.broadcasted_iota(jnp.int32, (128, 128), 0) == lane

    def upright(row):
        return jnp.sum(jnp.where(diagonal, row, 0.0), axis=1, keepdims=True)

    cell = upright(slot[1:2, :]).astype(jnp.int32)
    well = upright(slot[2:3, :]).astype(jnp.int32)
    wi = upright(slot[3:4, :])
    by_row = jnp.where(
        lax.broadcasted_iota(jnp.int32, (128, rx * ry), 1) == (cell >> 7), 1.0, 0.0
    ).astype(BF16)
    picked = None
    for _ in range(3):
        piece = mix.astype(BF16)
        mix = mix - piece.astype(F32)
        add = jnp.dot(by_row, piece, preferred_element_type=F32)
        picked = add if picked is None else picked + add
    values = jnp.sum(jnp.where(lane == (cell & 127), picked, 0.0), axis=1, keepdims=True)
    values = values * wi
    owner = well // wells
    spread = jnp.where(lane == (well - owner * wells) * steps + step, values, 0.0)
    flat = slot[2:3, :].astype(jnp.int32) // wells
    count = table_ref.shape[0]
    hot = jnp.where(
        lax.broadcasted_iota(jnp.int32, (count, 128), 0) == flat, 1.0, 0.0
    ).astype(F32)
    dense = jnp.dot(hot, spread, precision=HIGHEST, preferred_element_type=F32)
    if before is not None:
        dense = dense + before[...]
    out_wells[...] = dense


def first_kernel(step, steps, wells, *refs):
    table_ref, src_ref, own, z_low, z_high, x_low, x_high = refs[:7]
    geo = refs[7]
    outs = refs[8:12]
    raw, coef, fa0, fb0, fa1, fb1, lin = refs[12:]
    rx, ry, nz = own.shape[1:]
    ex = rx + 2 * H
    fill(raw, own, TOP_REACH, (z_low, z_high), (x_low, x_high))
    here_x, here_y, _, _ = spot()

    @pl.when(here_x == 0)
    def _():
        raw[0, H, :, :] = jnp.zeros(raw.shape[2:], F32)

    @pl.when(here_y == 0)
    def _():
        def clear(x, _):
            raw[1, x, H : H + 1, :] = jnp.zeros((1, nz), F32)
            return 0

        lax.fori_loop(0, ex, clear, 0)

    def geometry(x, _):
        lane = lax.broadcasted_iota(jnp.int32, (V, 8, nz), 2)
        tz = jnp.where(lane == 0, 0.0, by_v(raw, (2,), x))
        geo[TX, x] = by_v(raw, (0,), x)
        geo[TY, x] = by_v(raw, (1,), x)
        geo[TZ, x] = tz
        geo[TU, x] = roll_z(tz, 127)
        return 0

    lax.fori_loop(0, ex, geometry, 0, unroll=4)

    def prepare(x, _):
        ty = geo[TY, x]
        total = (
            (geo[TX, x + 1] + geo[TX, x]) + (up_v(ty) + ty) + (geo[TU, x] + geo[TZ, x])
        )
        geo[WS, x] = total
        s_a, r_a, p, frac, r_b, q, m, _ = coefficients(
            raw, 3, src_ref, step, x, total
        )
        coef[SA, x] = s_a
        coef[RA, x] = r_a
        coef[PC, x] = p
        coef[FR, x] = frac
        coef[RB, x] = r_b
        coef[QC, x] = q
        coef[MC, x] = m
        fa1[x] = s_a * r_a
        fb1[x] = r_b
        return 0

    lax.fori_loop(0, ex - 1, prepare, 0)
    sweeps(coef, geo, ((fa0, fb0), (fa1, fb1)), lin, 2, ex)
    finish(False, step, steps, wells, lin, own.at[7], table_ref, None, outs)


def prepare_kernel(step, first, with_acc, *refs):
    src_ref, geo, own, z_low, z_high, x_low, x_high = refs[:7]
    if with_acc:
        coef, acc_out, raw = refs[7:]
    else:
        acc, coef, raw = refs[7:]
    rx, ry, nz = own.shape[1:]
    ex = rx + 2 * H
    fill(raw, own, (COEF,) * own.shape[0], (z_low, z_high), (x_low, x_high), first)

    def prepare(x, _):
        s_a, r_a, p, frac, r_b, q, m, s_b = coefficients(
            raw, 0, src_ref, step, x, geo[WS, x]
        )
        coef[SA, x] = s_a
        coef[RA, x] = r_a
        coef[PC, x] = p
        coef[FR, x] = frac
        coef[RB, x] = r_b
        coef[QC, x] = q
        coef[MC, x] = m
        if with_acc:
            a, b = by_v(raw, (8,), x), by_v(raw, (9,), x)
            acc_out[0, x] = a
            acc_out[1, x] = b
        else:
            a, b = acc[0, x], acc[1, x]
        coef[AA, x] = a
        coef[AB, x] = s_b * b
        return 0

    lax.fori_loop(0, ex - 1, prepare, 0)


def sweep_kernel(last, step, steps, wells, *refs):
    table_ref, coef, geo, own, lam, z_low, z_high, x_low, x_high, before = refs[:10]
    outs = refs[10:-6]
    now, fa0, fb0, fa1, fb1, lin = refs[-6:]
    rx, ry, nz = own.shape[1:]
    ex = rx + 2 * H
    fill(lin, lam, LAM_REACH, (z_low, z_high), (x_low, x_high))

    def begin(x, _):
        a, b = by_v(lin, (0,), x), by_v(lin, (1,), x)
        fa0[x] = a
        fb0[x] = b
        now[0, x] = coef[RA, x] + coef[AA, x] * a
        now[1, x] = coef[RB, x] + coef[AB, x] * b
        return 0

    lax.fori_loop(0, ex, begin, 0, unroll=4)

    class Joined:
        def __getitem__(self, at):
            n, x = at
            return now[0, x] if n == RA else now[1, x] if n == RB else coef[n, x]

    sweeps(Joined(), geo, ((fa0, fb0), (fa1, fb1)), lin, 1, ex)
    finish(last, step, steps, wells, lin, own.at[4], table_ref, before, outs)


def local(
    grad_p, grad_s, acc_p, acc_s, trans_x, trans_y, trans_z, c_pp, c_ss, c_ps, c_sp,
    frac, mobility, rate_mis, bhp_mis, control, perf_well, perf_cell, perf_wi,
):
    dims = rx, ry, nz = trans_x.shape
    ex, ey = rx + 2 * H, ry + 2 * H
    steps = grad_p.shape[0]
    wells = rate_mis.shape[0]
    devices = lax.axis_size("gx") * lax.axis_size("gy")
    own = [c_pp, c_ss, c_ps, c_sp, frac, mobility, grad_p, grad_s]
    top = steps - 1

    arrays = [trans_x, trans_y, trans_z] + own
    leads = [None] * 3 + [top] * 8
    split = len(arrays)
    small = [rate_mis, bhp_mis, control] + [p[None] for p in (perf_well, perf_cell, perf_wi)]
    mine = pl.pallas_call(
        functools.partial(table_kernel, steps),
        in_specs=[HBM] * 6,
        out_specs=VMEM,
        out_shape=sds(devices, 4, 128),
        scratch_shapes=[pltpu.VMEM(p.shape, p.dtype) for p in small]
        + [pltpu.SemaphoreType.DMA((6,))],
        name="table",
    )(*small)
    blocks, y_low, y_high, token = load(arrays, leads, dims, (mine,))
    z_got = swaps(y_low, y_high, "gy")
    mine, _ = lax.optimization_barrier((mine, token))
    table = lax.all_to_all(mine, ("gx", "gy"), 0, 0, tiled=True)

    wide = widen(blocks, TOP_REACH, *z_got, (table,))
    x_got = swaps(*wide, "gx")
    src = call(
        functools.partial(source_kernel, steps, wells), [table, wide[0]],
        [sds(steps, ex, ey, nz)], "sources", 8, [VMEM, ANY],
    )[0]

    plan, places, sizes = [], {}, []
    for h, step in enumerate(reversed(range(top))):
        places[step] = len(plan)
        plan += [(n, step, h, n) for n in range(8)]
        if h == 0:
            plan += [(8, None, h, 8), (9, None, h, 9)]
        sizes.append(len(plan) - places[step])
    *holders, m_low, m_high = more(own + [acc_p, acc_s], plan, sizes, dims, table)
    m_z = swaps(m_low, m_high, "gy")
    held = dict(zip(reversed(range(top)), holders))

    def beside(step, after):
        group = held[step]
        return swaps(
            *widen(group, (COEF,) * group.shape[0], *m_z, (after,), places[step]), "gx"
        )

    sides = beside(top - 1, src)

    ext = (ex, V, 8, nz)
    lam_out = [sds(2, rx, ry, nz), sds(2, rx, H, nz), sds(2, rx, H, nz)]
    well_out = sds(devices, 128)
    fields = [pltpu.VMEM(ext, F32)] * 4 + [pltpu.VMEM((2, ex, ey, nz), F32)]

    geo, lam, low, high, dense = call(
        functools.partial(first_kernel, top, steps, wells),
        [table, src, blocks, *z_got, *x_got],
        [sds(5, *ext)] + lam_out + [well_out], "step_top", 16,
        scratch=[pltpu.VMEM((split, ex, ey, nz), F32), pltpu.VMEM((7, *ext), F32)] + fields,
    )

    acc = None
    for step in reversed(range(top)):
        last = step == 0
        with_acc = step == top - 1
        if not with_acc:
            sides = beside(step, coef)
        made = call(
            functools.partial(prepare_kernel, step, places[step], with_acc),
            [src, geo, held[step], *m_z, *sides] + ([] if with_acc else [acc]),
            [sds(9, *ext)] + ([sds(2, *ext)] if with_acc else []), "prepare", 8,
            scratch=[pltpu.VMEM((10 if with_acc else 8, ex, ey, nz), F32)],
        )
        coef = made[0]
        if with_acc:
            acc = made[1]

        l_z = swaps(low, high, "gy")
        l_x = swaps(*widen(lam, LAM_REACH, *l_z), "gx")
        outs = [sds(rx, ry, nz)] * 2 if last else lam_out
        outs = call(
            functools.partial(sweep_kernel, last, step, steps, wells),
            [table, coef, geo, held[step], lam, *l_z, *l_x, dense],
            outs + [well_out], "step", 8, scratch=[pltpu.VMEM((2, *ext), F32)] + fields,
        )
        dense = outs[-1]
        if not last:
            lam, low, high = outs[:3]

    parts = lax.all_to_all(dense[:, None, :], ("gx", "gy"), 0, 0, tiled=True)
    well_grad = jnp.sum(parts, axis=(0, 1))[: wells * steps].reshape(wells, steps)
    return outs[0], outs[1], well_grad


def solution(mesh):
    cells3 = P("gx", "gy", None)
    cells4 = P(None, "gx", "gy", None)
    flat = ("gx", "gy")
    placed = (cells4,) * 2 + (cells3,) * 5 + (cells4,) * 6 + (P(flat, None),) * 3 + (P(flat),) * 3
    return jax.shard_map(
        local,
        mesh=mesh,
        in_specs=placed,
        out_specs=(cells3, cells3, P(flat, None)),
        check_vma=False,
    )
```

```python
import functools

import jax
import jax.numpy as jnp
from jax import lax
from jax.experimental import pallas as pl
from jax.experimental.pallas import tpu as pltpu
from jax.sharding import PartitionSpec as P

SWEEPS = 8
OMEGA = 0.8
KEEP = 1.0 - OMEGA
H = 8
V = 4
HIGHEST = lax.Precision.HIGHEST
F32 = jnp.float32
BF16 = jnp.bfloat16
FLOPS = 1e9

VMEM = pl.BlockSpec(memory_space=pltpu.VMEM)
ANY = pl.BlockSpec(memory_space=pl.ANY)
HBM = pl.BlockSpec(memory_space=pltpu.HBM)


def sds(*shape):
    return jax.ShapeDtypeStruct(shape, F32)


def params(mib):
    return pltpu.CompilerParams(vmem_limit_bytes=mib * 1024 * 1024)


TIMES = {"step_top": 7, "step": 6, "sources": 3, "prepare": 1.5}


def estimate(name):
    work = TIMES.get(name, 0.5)
    return pl.CostEstimate(
        flops=int(work * FLOPS), bytes_accessed=int(work * 3.0e6), transcendentals=0
    )


def call(kernel, ins, outs, name, mib, specs=None, scratch=()):
    return pl.pallas_call(
        kernel,
        in_specs=specs or [VMEM] * len(ins),
        out_specs=[VMEM] * len(outs),
        out_shape=outs,
        scratch_shapes=list(scratch),
        compiler_params=params(mib),
        cost_estimate=estimate(name),
        name=name,
    )(*ins)


def swaps(first, second, axis):
    length = lax.axis_size(axis)
    even = [(i, i ^ 1) for i in range(length) if i ^ 1 < length]
    odd = [(i, i + 1) for i in range(1, length - 1, 2)]
    odd += [(j, i) for i, j in odd]
    return lax.ppermute(first, axis, even), lax.ppermute(second, axis, odd)


def by_side(axis, work, first, second):
    at = lax.axis_index(axis) % 2

    @pl.when(at == 1)
    def _():
        work(first, second)

    @pl.when(at == 0)
    def _():
        work(second, first)


def load_kernel(leads, *refs):
    count = len(leads)
    ins, (own, y_low, y_high, token), sems = refs[:count], refs[-5:-1], refs[-1]
    token[...] = jnp.zeros(token.shape, F32)
    copies = [
        pltpu.make_async_copy(
            ins[n] if lead is None else ins[n].at[lead], own.at[n], sems.at[n]
        )
        for n, lead in enumerate(leads)
    ]
    for c in copies:
        c.start()
    for c in copies:
        c.wait()
    by_side("gy", lambda low, high: y_edges(own, low, high), y_low, y_high)


def y_edges(own, low, high):
    ry = own.shape[2]

    def one(n, _):
        low[n] = own[n, :, 0:H, :]
        high[n] = own[n, :, ry - H :, :]
        return 0

    lax.fori_loop(0, own.shape[0], one, 0)


def load(arrays, leads, dims, after):
    n = len(leads)
    rx, ry, nz = dims
    return pl.pallas_call(
        functools.partial(load_kernel, leads),
        in_specs=[HBM] * n + [ANY] * len(after),
        out_specs=[VMEM] * 4,
        out_shape=[sds(n, *dims)] + [sds(n, rx, H, nz)] * 2 + [sds(8, 128)],
        scratch_shapes=[pltpu.SemaphoreType.DMA((n,))],
        name="load",
    )(*arrays, *after)


def more_kernel(plan, count, parts, *refs):
    ins, outs = refs[:count], refs[count + 1 :]
    holders, firsts, seconds = outs[:parts], outs[parts::2], outs[parts + 1 :: 2]
    rx, ry = holders[0].shape[1:3]

    def work(lows, highs):
        def row(x, _):
            for i, lead, h, m in plan:
                value = ins[i][x] if lead is None else ins[i][lead, x]
                holders[h][m, x] = value
                lows[h][m, x] = value[0:H]
                highs[h][m, x] = value[ry - H :]
            return 0

        lax.fori_loop(0, rx, row, 0)

    by_side("gy", work, firsts, seconds)


def more(arrays, plan, sizes, dims, after):
    rx, ry, nz = dims
    return call(
        functools.partial(more_kernel, plan, len(arrays), len(sizes)), list(arrays) + [after],
        [sds(m, *dims) for m in sizes] + [sds(m, rx, H, nz) for m in sizes for _ in range(2)],
        "more", 4, [VMEM] * len(arrays) + [ANY],
    )


def tiles_of(reach):
    return reach // 2


def rows_of_array(reach):
    return reach + tiles_of(reach)


def fold(row, reach, high):
    tiles = []
    for dx in range(1, tiles_of(reach) + 1):
        near, far = row(dx), row(reach - dx)
        sub = lax.broadcasted_iota(jnp.int32, near.shape, 0)
        if high:
            tiles.append(jnp.where(sub < 8 - dx, near, pltpu.roll(far, 8 - dx, 0)))
        else:
            tiles.append(jnp.where(sub >= dx, near, pltpu.roll(far, dx, 0)))
    return tiles


def unfold(tile, dx, high):
    return tile, pltpu.roll(tile, dx if high else 8 - dx, 0)


def parts_of(reaches):
    parts, row = [], 0
    for n, reach in enumerate(reaches):
        if parts and parts[-1][2] == reach:
            parts[-1][1] += 1
        else:
            parts.append([n, 1, reach, row])
        row += rows_of_array(reach)
    return parts, row


def widen_kernel(reaches, first, own, z_first, z_second, *refs):
    rx = own.shape[1]

    def work(z_low, z_high, outs):
        for begin, count, reach, base in parts_of(reaches)[0]:

            def one(k, _):
                n = begin + k
                at = base + k * rows_of_array(reach)
                for side in (0, 1):
                    start = 0 if side == 0 else rx - reach
                    outs[side][pl.ds(at, reach)] = own[n, start : start + reach]
                    for high, z in ((0, z_low), (1, z_high)):

                        def row(dx):
                            return z[n + first, dx - 1 if side == 0 else rx - dx]

                        for t, tile in enumerate(fold(row, reach, high == 1)):
                            outs[side][at + reach + t, high * H : (high + 1) * H, :] = tile
                return 0

            lax.fori_loop(0, count, one, 0)

    def along_x(low, high):
        by_side("gy", lambda a, b: work(a, b, (low, high)), z_first, z_second)

    by_side("gx", along_x, *refs[-2:])


def widen(own, reaches, z_low, z_high, after=(), first=0):
    _, rx, ry, nz = own.shape
    return call(
        functools.partial(widen_kernel, reaches, first), [own, z_low, z_high, *after],
        [sds(parts_of(reaches)[1], ry, nz)] * 2, "widen", 4, [VMEM] * 3 + [ANY] * len(after),
    )


def table_kernel(steps, *refs):
    ins, out, held, sems = refs[:6], refs[6], refs[7:13], refs[13]
    copies = [pltpu.make_async_copy(i, h, sems.at[n]) for n, (i, h) in enumerate(zip(ins, held))]
    for c in copies:
        c.start()
    for c in copies:
        c.wait()
    rate, bhp, control, perf_well, perf_cell, perf_wi = [h[...] for h in held]
    wells = rate.shape[0]
    effective = jnp.where(control == 1, rate, bhp)
    lane = lax.broadcasted_iota(jnp.int32, (1, 128), 1)
    row = jnp.zeros((1, 128), F32)
    for u in range(wells):
        for n in range(steps):
            row = jnp.where(lane == u * steps + n, effective[u : u + 1, n : n + 1], row)
    mine = jnp.concatenate([row, perf_cell.astype(F32), perf_well.astype(F32), perf_wi])
    out[...] = jnp.broadcast_to(mine[None], out.shape)


def spot():
    n_x, n_y = lax.axis_size("gx"), lax.axis_size("gy")
    x, y = lax.axis_index("gx"), lax.axis_index("gy")
    return x, y, n_x, n_y


def source_kernel(steps, wells, table_ref, _, src_ref):
    here_x, here_y, n_x, n_y = spot()
    count = table_ref.shape[0]
    rx, ry = src_ref.shape[1] - 2 * H, src_ref.shape[2] - 2 * H
    of_wells = table_ref[:, 0, :]
    columns = [
        jnp.broadcast_to(of_wells[:, c : c + 1], (count, 128)) for c in range(wells * steps)
    ]
    owner_iota = lax.broadcasted_iota(jnp.int32, (count, 128), 0)
    sub = lax.broadcasted_iota(jnp.int32, (128, 128), 0)

    def spans(length):
        return ((0, H, length - H), (H, length, 0), (H + length, H, 0))

    for dx, (x0, size_x, from_x) in enumerate(spans(rx)):
        for dy, (y0, size_y, from_y) in enumerate(spans(ry)):
            at_x, at_y = here_x + dx - 1, here_y + dy - 1
            inside = (at_x >= 0) & (at_x < n_x) & (at_y >= 0) & (at_y < n_y)
            slot = table_ref[jnp.where(inside, at_x * n_y + at_y, 0)]
            cell = slot[1:2, :].astype(jnp.int32)
            well = slot[2:3, :].astype(jnp.int32)
            wi = slot[3:4, :] * inside.astype(F32)
            owner = well // wells
            within = well - owner * wells
            hot = owner_iota == owner
            in_lane = sub == (cell & 127)
            pieces = []
            for step in range(steps):
                chosen = columns[step]
                for u in range(1, wells):
                    chosen = jnp.where(within == u, columns[u * steps + step], chosen)
                value = jnp.sum(jnp.where(hot, chosen, 0.0), axis=0, keepdims=True) * wi
                high = value.astype(BF16).astype(F32)
                for piece in (high, value - high):
                    pieces.append(jnp.where(in_lane, piece, 0.0).astype(BF16))
            xi = lax.broadcasted_iota(jnp.int32, (size_x, size_y, 128), 0) + from_x
            yi = lax.broadcasted_iota(jnp.int32, (size_x, size_y, 128), 1) + from_y
            target = (xi * ry + yi).reshape(size_x * size_y, 128)
            by_row = jnp.where(target == (cell >> 7), 1.0, 0.0).astype(BF16)
            found = lax.dot_general(
                by_row, jnp.concatenate(pieces), (((1,), (1,)), ((), ())),
                preferred_element_type=F32,
            )
            for step in range(steps):
                part = found[:, step * 256 : step * 256 + 128]
                part = part + found[:, step * 256 + 128 : step * 256 + 256]
                src_ref[step, x0 : x0 + size_x, y0 : y0 + size_y, :] = part.reshape(
                    size_x, size_y, 128
                )


def by_v(ref, lead, x):
    return jnp.stack([ref[(*lead, x, pl.ds(v, 8, stride=V), slice(None))] for v in range(V)])


def up_v(value):
    return jnp.concatenate([value[1:], pltpu.roll(value[0], 7, 0)[None]])


def down_v(value):
    return jnp.concatenate([pltpu.roll(value[V - 1], 1, 0)[None], value[:-1]])


def roll_z(value, by):
    return pltpu.roll(value, by, 2)


def fill(dst, own, reaches, z_got, x_got, first=0):
    rx, ry, nz = own.shape[1:]

    def middle(z_low, z_high):
        def one(n, _):
            dst[n, H : H + rx, 0:H, :] = z_low[n + first]
            dst[n, H : H + rx, H : H + ry, :] = own[n]
            dst[n, H : H + rx, H + ry : 2 * H + ry, :] = z_high[n + first]
            return 0

        lax.fori_loop(0, len(reaches), one, 0)

    def outer(x_low, x_high):
        sides = (x_low, x_high)
        for begin, count, reach, base in parts_of(reaches)[0]:

            def one(k, _):
                n = begin + k
                row = base + k * rows_of_array(reach)
                for side in (0, 1):
                    at = H - reach if side == 0 else H + rx
                    dst[n, at : at + reach, H : H + ry, :] = sides[side][pl.ds(row, reach)]
                    known = set()
                    for y in (0, 1):
                        to = y * (H + ry)
                        for t in range(tiles_of(reach)):
                            tile = sides[side][row + reach + t, y * H : (y + 1) * H, :]
                            near, far = unfold(tile, t + 1, y == 1)
                            for dx, value in ((t + 1, near), (reach - t - 1, far)):
                                x = H - dx if side == 0 else H + rx + dx - 1
                                dst[n, x, to : to + H, :] = value
                                known.add(dx)
                    for dx in range(1, H + 1):
                        x = H - dx if side == 0 else H + rx + dx - 1
                        if dx not in known:
                            for y in (0, H + ry):
                                dst[n, x, y : y + H, :] = jnp.zeros((H, nz), F32)
                        if dx > reach:
                            dst[n, x, H : H + ry, :] = jnp.zeros((ry, nz), F32)
                return 0

            lax.fori_loop(0, count, one, 0)

    by_side("gy", middle, *z_got)
    by_side("gx", outer, *x_got)


GEO, COEF = 8, 7
TOP_REACH = (GEO,) * 3 + (COEF,) * 8
LAM_REACH = (GEO,) * 2


SA, RA, PC, FR, RB, QC, MC, AA, AB = range(9)
TX, TY, TZ, TU, WS = range(5)


def coefficients(raw, base, src_ref, step, x, total):
    c_pp, c_ss, c_ps, c_sp, frac, mob, g_p, g_s = [by_v(raw, (base + n,), x) for n in range(8)]
    den_a = c_pp + total
    den_b = c_ss + mob * total
    s_a = jnp.where(den_a > 0, OMEGA / den_a, 0.0)
    s_b = jnp.where(den_b > 0, OMEGA / den_b, 0.0)
    r_a = g_p + by_v(src_ref, (step,), x)
    return s_a, r_a, c_sp + frac * total, frac, s_b * g_s, s_b * c_ps, s_b * mob, s_b


BLOCK = 2
UNROLL = 4


def sweeps(coef, geo, bufs, lin, begin, ex):
    def work(number, x, count):
        old, new = bufs[(number - 1) % 2], bufs[number % 2]
        tx = [geo[TX, x + r] for r in range(count + 1)]
        values = [[old[f][x - 1 + r] for r in range(count + 2)] for f in range(2)]
        results = []
        for r in range(count):
            at = x + r
            ty = geo[TY, at]
            ty_up = up_v(ty)
            tz, tz_up = geo[TZ, at], geo[TU, at]

            def around(v):
                c = v[r + 1]
                total = tx[r + 1] * v[r + 2] + tx[r] * v[r]
                total = total + (ty_up * up_v(c) + ty * down_v(c))
                total = total + (tz_up * roll_z(c, 127) + tz * roll_z(c, 1))
                return c, total

            a, n_a = around(values[0])
            b, n_b = around(values[1])
            new_a = KEEP * a + coef[SA, at] * (
                (coef[RA, at] + n_a) + (coef[FR, at] * n_b - coef[PC, at] * b)
            )
            new_b = (KEEP * b + coef[RB, at]) + (coef[MC, at] * n_b - coef[QC, at] * a)
            results.append((new_a, new_b))
        for r in range(count):
            for f in range(2):
                if number == SWEEPS:
                    for v in range(V):
                        lin[f, x + r, pl.ds(v, 8, stride=V), :] = results[r][f][v]
                else:
                    new[f][x + r] = results[r][f]

    for number in range(begin, SWEEPS + 1):
        size = BLOCK * UNROLL
        total = ex - 2 * number

        def many(i, _):
            for u in range(UNROLL):
                work(number, number + i * size + u * BLOCK, BLOCK)
            return 0

        lax.fori_loop(0, total // size, many, 0)
        for at in range(total - total % size, total, BLOCK):
            work(number, number + at, BLOCK)


def finish(last, step, steps, wells, lin, frac, table_ref, before, outs):
    rx, ry, nz = frac.shape[-3:]
    out_wells = outs[-1]

    def copies(low, high):
        def copy(x, _):
            for f in range(2):
                row = lin[f, H + x, H : H + ry, :]
                if last:
                    outs[f][x] = row
                else:
                    outs[0][f, x] = row
                    low[f, x] = row[0:H]
                    high[f, x] = row[ry - H :]
            return 0

        lax.fori_loop(0, rx, copy, 0, unroll=2)

    if last:
        copies(None, None)
    else:
        by_side("gy", copies, outs[1], outs[2])
    mix = lin[0, H : H + rx, H : H + ry, :] + frac[...] * lin[1, H : H + rx, H : H + ry, :]
    mix = mix.reshape(rx * ry, nz)
    here_x, here_y, _, n_y = spot()
    slot = table_ref[here_x * n_y + here_y]
    lane = lax.broadcasted_iota(jnp.int32, (128, 128), 1)
    diagonal = lax.broadcasted_iota(jnp.int32, (128, 128), 0) == lane

    def upright(row):
        return jnp.sum(jnp.where(diagonal, row, 0.0), axis=1, keepdims=True)

    cell = upright(slot[1:2, :]).astype(jnp.int32)
    well = upright(slot[2:3, :]).astype(jnp.int32)
    wi = upright(slot[3:4, :])
    by_row = jnp.where(
        lax.broadcasted_iota(jnp.int32, (128, rx * ry), 1) == (cell >> 7), 1.0, 0.0
    ).astype(BF16)
    picked = None
    for _ in range(3):
        piece = mix.astype(BF16)
        mix = mix - piece.astype(F32)
        add = jnp.dot(by_row, piece, preferred_element_type=F32)
        picked = add if picked is None else picked + add
    values = jnp.sum(jnp.where(lane == (cell & 127), picked, 0.0), axis=1, keepdims=True)
    values = values * wi
    owner = well // wells
    spread = jnp.where(lane == (well - owner * wells) * steps + step, values, 0.0)
    flat = slot[2:3, :].astype(jnp.int32) // wells
    count = table_ref.shape[0]
    hot = jnp.where(
        lax.broadcasted_iota(jnp.int32, (count, 128), 0) == flat, 1.0, 0.0
    ).astype(F32)
    dense = jnp.dot(hot, spread, precision=HIGHEST, preferred_element_type=F32)
    if before is not None:
        dense = dense + before[...]
    out_wells[...] = dense


def first_kernel(step, steps, wells, *refs):
    table_ref, src_ref, own, z_low, z_high, x_low, x_high = refs[:7]
    geo = refs[7]
    outs = refs[8:12]
    raw, coef, fa0, fb0, fa1, fb1, lin = refs[12:]
    rx, ry, nz = own.shape[1:]
    ex = rx + 2 * H
    fill(raw, own, TOP_REACH, (z_low, z_high), (x_low, x_high))
    here_x, here_y, _, _ = spot()

    @pl.when(here_x == 0)
    def _():
        raw[0, H, :, :] = jnp.zeros(raw.shape[2:], F32)

    @pl.when(here_y == 0)
    def _():
        def clear(x, _):
            raw[1, x, H : H + 1, :] = jnp.zeros((1, nz), F32)
            return 0

        lax.fori_loop(0, ex, clear, 0)

    def geometry(x, _):
        lane = lax.broadcasted_iota(jnp.int32, (V, 8, nz), 2)
        tz = jnp.where(lane == 0, 0.0, by_v(raw, (2,), x))
        geo[TX, x] = by_v(raw, (0,), x)
        geo[TY, x] = by_v(raw, (1,), x)
        geo[TZ, x] = tz
        geo[TU, x] = roll_z(tz, 127)
        return 0

    lax.fori_loop(0, ex, geometry, 0, unroll=4)

    def prepare(x, _):
        ty = geo[TY, x]
        total = (
            (geo[TX, x + 1] + geo[TX, x]) + (up_v(ty) + ty) + (geo[TU, x] + geo[TZ, x])
        )
        geo[WS, x] = total
        s_a, r_a, p, frac, r_b, q, m, _ = coefficients(
            raw, 3, src_ref, step, x, total
        )
        coef[SA, x] = s_a
        coef[RA, x] = r_a
        coef[PC, x] = p
        coef[FR, x] = frac
        coef[RB, x] = r_b
        coef[QC, x] = q
        coef[MC, x] = m
        fa1[x] = s_a * r_a
        fb1[x] = r_b
        return 0

    lax.fori_loop(0, ex - 1, prepare, 0)
    sweeps(coef, geo, ((fa0, fb0), (fa1, fb1)), lin, 2, ex)
    finish(False, step, steps, wells, lin, own.at[7], table_ref, None, outs)


def prepare_kernel(step, first, with_acc, *refs):
    src_ref, geo, own, z_low, z_high, x_low, x_high = refs[:7]
    if with_acc:
        coef, acc_out, raw = refs[7:]
    else:
        acc, coef, raw = refs[7:]
    rx, ry, nz = own.shape[1:]
    ex = rx + 2 * H
    fill(raw, own, (COEF,) * own.shape[0], (z_low, z_high), (x_low, x_high), first)

    def prepare(x, _):
        s_a, r_a, p, frac, r_b, q, m, s_b = coefficients(
            raw, 0, src_ref, step, x, geo[WS, x]
        )
        coef[SA, x] = s_a
        coef[RA, x] = r_a
        coef[PC, x] = p
        coef[FR, x] = frac
        coef[RB, x] = r_b
        coef[QC, x] = q
        coef[MC, x] = m
        if with_acc:
            a, b = by_v(raw, (8,), x), by_v(raw, (9,), x)
            acc_out[0, x] = a
            acc_out[1, x] = b
        else:
            a, b = acc[0, x], acc[1, x]
        coef[AA, x] = a
        coef[AB, x] = s_b * b
        return 0

    lax.fori_loop(0, ex - 1, prepare, 0)


def sweep_kernel(last, step, steps, wells, *refs):
    table_ref, coef, geo, own, lam, z_low, z_high, x_low, x_high, before = refs[:10]
    outs = refs[10:-6]
    now, fa0, fb0, fa1, fb1, lin = refs[-6:]
    rx, ry, nz = own.shape[1:]
    ex = rx + 2 * H
    fill(lin, lam, LAM_REACH, (z_low, z_high), (x_low, x_high))

    def begin(x, _):
        a, b = by_v(lin, (0,), x), by_v(lin, (1,), x)
        fa0[x] = a
        fb0[x] = b
        now[0, x] = coef[RA, x] + coef[AA, x] * a
        now[1, x] = coef[RB, x] + coef[AB, x] * b
        return 0

    lax.fori_loop(0, ex, begin, 0, unroll=4)

    class Joined:
        def __getitem__(self, at):
            n, x = at
            return now[0, x] if n == RA else now[1, x] if n == RB else coef[n, x]

    sweeps(Joined(), geo, ((fa0, fb0), (fa1, fb1)), lin, 1, ex)
    finish(last, step, steps, wells, lin, own.at[4], table_ref, before, outs)


def local(
    grad_p, grad_s, acc_p, acc_s, trans_x, trans_y, trans_z, c_pp, c_ss, c_ps, c_sp,
    frac, mobility, rate_mis, bhp_mis, control, perf_well, perf_cell, perf_wi,
):
    dims = rx, ry, nz = trans_x.shape
    ex, ey = rx + 2 * H, ry + 2 * H
    steps = grad_p.shape[0]
    wells = rate_mis.shape[0]
    devices = lax.axis_size("gx") * lax.axis_size("gy")
    own = [c_pp, c_ss, c_ps, c_sp, frac, mobility, grad_p, grad_s]
    top = steps - 1

    arrays = [trans_x, trans_y, trans_z] + own
    leads = [None] * 3 + [top] * 8
    split = len(arrays)
    small = [rate_mis, bhp_mis, control] + [p[None] for p in (perf_well, perf_cell, perf_wi)]
    mine = pl.pallas_call(
        functools.partial(table_kernel, steps),
        in_specs=[HBM] * 6,
        out_specs=VMEM,
        out_shape=sds(devices, 4, 128),
        scratch_shapes=[pltpu.VMEM(p.shape, p.dtype) for p in small]
        + [pltpu.SemaphoreType.DMA((6,))],
        name="table",
    )(*small)
    blocks, y_low, y_high, token = load(arrays, leads, dims, (mine,))
    z_got = swaps(y_low, y_high, "gy")
    mine, _ = lax.optimization_barrier((mine, token))
    table = lax.all_to_all(mine, ("gx", "gy"), 0, 0, tiled=True)

    wide = widen(blocks, TOP_REACH, *z_got, (table,))
    x_got = swaps(*wide, "gx")
    src = call(
        functools.partial(source_kernel, steps, wells), [table, wide[0]],
        [sds(steps, ex, ey, nz)], "sources", 8, [VMEM, ANY],
    )[0]

    plan, sizes = [], []
    for h, step in enumerate(reversed(range(top))):
        plan += [(n, step, h, n) for n in range(8)]
        if h == 0:
            plan += [(8, None, h, 8), (9, None, h, 9)]
        sizes.append(10 if h == 0 else 8)
    made = more(own + [acc_p, acc_s], plan, sizes, dims, table)
    held = dict(zip(reversed(range(top)), made[:top]))
    ends = {step: made[top + 2 * h : top + 2 * h + 2] for h, step in enumerate(reversed(range(top)))}
    m_z = {}

    def beside(step, after):
        group = held[step]
        return widen(group, (COEF,) * group.shape[0], *m_z[step], (after,))

    first, second = ends[top - 1]
    first, second, _ = lax.optimization_barrier((first, second, src))
    m_z[top - 1] = swaps(first, second, "gy")
    sides = beside(top - 1, src)
    late = sides[0]
    sides = swaps(*sides, "gx")

    ext = (ex, V, 8, nz)
    lam_out = [sds(2, rx, ry, nz), sds(2, rx, H, nz), sds(2, rx, H, nz)]
    well_out = sds(devices, 128)
    fields = [pltpu.VMEM(ext, F32)] * 4 + [pltpu.VMEM((2, ex, ey, nz), F32)]

    geo, lam, low, high, dense = call(
        functools.partial(first_kernel, top, steps, wells),
        [table, src, blocks, *z_got, *x_got],
        [sds(5, *ext)] + lam_out + [well_out], "step_top", 16,
        scratch=[pltpu.VMEM((split, ex, ey, nz), F32), pltpu.VMEM((7, *ext), F32)] + fields,
    )

    acc = None
    for step in reversed(range(top)):
        last = step == 0
        with_acc = step == top - 1
        if not with_acc:
            sides = swaps(*beside(step, coef), "gx")
        else:
            first, second, _ = lax.optimization_barrier((*ends[step - 1], late))
            m_z[step - 1] = swaps(first, second, "gy")
            low, high, *_ = lax.optimization_barrier((low, high, *m_z[step - 1]))
        made = call(
            functools.partial(prepare_kernel, step, 0, with_acc),
            [src, geo, held[step], *m_z[step], *sides] + ([] if with_acc else [acc]),
            [sds(9, *ext)] + ([sds(2, *ext)] if with_acc else []), "prepare", 8,
            scratch=[pltpu.VMEM((10 if with_acc else 8, ex, ey, nz), F32)],
        )
        coef = made[0]
        if with_acc:
            acc = made[1]

        l_z = swaps(low, high, "gy")
        l_x = swaps(*widen(lam, LAM_REACH, *l_z), "gx")
        outs = [sds(rx, ry, nz)] * 2 if last else lam_out
        outs = call(
            functools.partial(sweep_kernel, last, step, steps, wells),
            [table, coef, geo, held[step], lam, *l_z, *l_x, dense],
            outs + [well_out], "step", 8, scratch=[pltpu.VMEM((2, *ext), F32)] + fields,
        )
        dense = outs[-1]
        if not last:
            lam, low, high = outs[:3]

    parts = lax.all_to_all(dense[:, None, :], ("gx", "gy"), 0, 0, tiled=True)
    well_grad = jnp.sum(parts, axis=(0, 1))[: wells * steps].reshape(wells, steps)
    return outs[0], outs[1], well_grad


def solution(mesh):
    cells3 = P("gx", "gy", None)
    cells4 = P(None, "gx", "gy", None)
    flat = ("gx", "gy")
    placed = (cells4,) * 2 + (cells3,) * 5 + (cells4,) * 6 + (P(flat, None),) * 3 + (P(flat),) * 3
    return jax.shard_map(
        local,
        mesh=mesh,
        in_specs=placed,
        out_specs=(cells3, cells3, P(flat, None)),
        check_vma=False,
    )
```

```python
import functools

import jax
import jax.numpy as jnp
from jax import lax
from jax.experimental import pallas as pl
from jax.experimental.pallas import tpu as pltpu
from jax.sharding import PartitionSpec as P

SWEEPS = 8
OMEGA = 0.8
KEEP = 1.0 - OMEGA
H = 8
V = 4
HIGHEST = lax.Precision.HIGHEST
F32 = jnp.float32
BF16 = jnp.bfloat16
FLOPS = 1e9

VMEM = pl.BlockSpec(memory_space=pltpu.VMEM)
ANY = pl.BlockSpec(memory_space=pl.ANY)
HBM = pl.BlockSpec(memory_space=pltpu.HBM)


def sds(*shape):
    return jax.ShapeDtypeStruct(shape, F32)


def params(mib):
    return pltpu.CompilerParams(vmem_limit_bytes=mib * 1024 * 1024)


TIMES = {"step_top": 7, "step": 6, "sources": 3, "prepare": 1.5}


def estimate(name):
    work = TIMES.get(name, 0.5)
    return pl.CostEstimate(
        flops=int(work * FLOPS), bytes_accessed=int(work * 3.0e6), transcendentals=0
    )


def call(kernel, ins, outs, name, mib, specs=None, scratch=()):
    return pl.pallas_call(
        kernel,
        in_specs=specs or [VMEM] * len(ins),
        out_specs=[VMEM] * len(outs),
        out_shape=outs,
        scratch_shapes=list(scratch),
        compiler_params=params(mib),
        cost_estimate=estimate(name),
        name=name,
    )(*ins)


def swaps(first, second, axis):
    length = lax.axis_size(axis)
    even = [(i, i ^ 1) for i in range(length) if i ^ 1 < length]
    odd = [(i, i + 1) for i in range(1, length - 1, 2)]
    odd += [(j, i) for i, j in odd]
    return lax.ppermute(first, axis, even), lax.ppermute(second, axis, odd)


def by_side(axis, work, first, second):
    at = lax.axis_index(axis) % 2

    @pl.when(at == 1)
    def _():
        work(first, second)

    @pl.when(at == 0)
    def _():
        work(second, first)


def load_kernel(leads, *refs):
    count = len(leads)
    ins, (own, y_low, y_high, token), sems = refs[:count], refs[-5:-1], refs[-1]
    token[...] = jnp.zeros(token.shape, F32)
    copies = [
        pltpu.make_async_copy(
            ins[n] if lead is None else ins[n].at[lead], own.at[n], sems.at[n]
        )
        for n, lead in enumerate(leads)
    ]
    for c in copies:
        c.start()
    for c in copies:
        c.wait()
    by_side("gy", lambda low, high: y_edges(own, low, high), y_low, y_high)


def y_edges(own, low, high):
    ry = own.shape[2]

    def one(n, _):
        low[n] = own[n, :, 0:H, :]
        high[n] = own[n, :, ry - H :, :]
        return 0

    lax.fori_loop(0, own.shape[0], one, 0)


def load(arrays, leads, dims, after):
    n = len(leads)
    rx, ry, nz = dims
    return pl.pallas_call(
        functools.partial(load_kernel, leads),
        in_specs=[HBM] * n + [ANY] * len(after),
        out_specs=[VMEM] * 4,
        out_shape=[sds(n, *dims)] + [sds(n, rx, H, nz)] * 2 + [sds(8, 128)],
        scratch_shapes=[pltpu.SemaphoreType.DMA((n,))],
        name="load",
    )(*arrays, *after)


def more_kernel(plan, count, parts, *refs):
    ins, outs = refs[:count], refs[count + 1 :]
    holders, firsts, seconds = outs[:parts], outs[parts::2], outs[parts + 1 :: 2]
    rx, ry = holders[0].shape[1:3]

    def work(lows, highs):
        def row(x, _):
            for i, lead, h, m in plan:
                value = ins[i][x] if lead is None else ins[i][lead, x]
                holders[h][m, x] = value
                lows[h][m, x] = value[0:H]
                highs[h][m, x] = value[ry - H :]
            return 0

        lax.fori_loop(0, rx, row, 0)

    by_side("gy", work, firsts, seconds)


def more(arrays, plan, sizes, dims, after):
    rx, ry, nz = dims
    return call(
        functools.partial(more_kernel, plan, len(arrays), len(sizes)), list(arrays) + [after],
        [sds(m, *dims) for m in sizes] + [sds(m, rx, H, nz) for m in sizes for _ in range(2)],
        "more", 4, [VMEM] * len(arrays) + [ANY],
    )


def tiles_of(reach):
    return reach // 2


def rows_of_array(reach):
    return reach + tiles_of(reach)


def fold(row, reach, high):
    tiles = []
    for dx in range(1, tiles_of(reach) + 1):
        near, far = row(dx), row(reach - dx)
        sub = lax.broadcasted_iota(jnp.int32, near.shape, 0)
        if high:
            tiles.append(jnp.where(sub < 8 - dx, near, pltpu.roll(far, 8 - dx, 0)))
        else:
            tiles.append(jnp.where(sub >= dx, near, pltpu.roll(far, dx, 0)))
    return tiles


def unfold(tile, dx, high):
    return tile, pltpu.roll(tile, dx if high else 8 - dx, 0)


def parts_of(reaches):
    parts, row = [], 0
    for n, reach in enumerate(reaches):
        if parts and parts[-1][2] == reach:
            parts[-1][1] += 1
        else:
            parts.append([n, 1, reach, row])
        row += rows_of_array(reach)
    return parts, row


def widen_kernel(reaches, first, own, z_first, z_second, *refs):
    rx = own.shape[1]

    def work(z_low, z_high, outs):
        for begin, count, reach, base in parts_of(reaches)[0]:

            def one(k, _):
                n = begin + k
                at = base + k * rows_of_array(reach)
                for side in (0, 1):
                    start = 0 if side == 0 else rx - reach
                    outs[side][pl.ds(at, reach)] = own[n, start : start + reach]
                    for high, z in ((0, z_low), (1, z_high)):

                        def row(dx):
                            return z[n + first, dx - 1 if side == 0 else rx - dx]

                        for t, tile in enumerate(fold(row, reach, high == 1)):
                            outs[side][at + reach + t, high * H : (high + 1) * H, :] = tile
                return 0

            lax.fori_loop(0, count, one, 0)

    def along_x(low, high):
        by_side("gy", lambda a, b: work(a, b, (low, high)), z_first, z_second)

    by_side("gx", along_x, *refs[-2:])


def widen(own, reaches, z_low, z_high, after=(), first=0):
    _, rx, ry, nz = own.shape
    return call(
        functools.partial(widen_kernel, reaches, first), [own, z_low, z_high, *after],
        [sds(parts_of(reaches)[1], ry, nz)] * 2, "widen", 4, [VMEM] * 3 + [ANY] * len(after),
    )


def table_kernel(steps, *refs):
    ins, out, held, sems = refs[:6], refs[6], refs[7:13], refs[13]
    copies = [pltpu.make_async_copy(i, h, sems.at[n]) for n, (i, h) in enumerate(zip(ins, held))]
    for c in copies:
        c.start()
    for c in copies:
        c.wait()
    rate, bhp, control, perf_well, perf_cell, perf_wi = [h[...] for h in held]
    wells = rate.shape[0]
    effective = jnp.where(control == 1, rate, bhp)
    lane = lax.broadcasted_iota(jnp.int32, (1, 128), 1)
    row = jnp.zeros((1, 128), F32)
    for u in range(wells):
        for n in range(steps):
            row = jnp.where(lane == u * steps + n, effective[u : u + 1, n : n + 1], row)
    mine = jnp.concatenate([row, perf_cell.astype(F32), perf_well.astype(F32), perf_wi])
    out[...] = jnp.broadcast_to(mine[None], out.shape)


def spot():
    n_x, n_y = lax.axis_size("gx"), lax.axis_size("gy")
    x, y = lax.axis_index("gx"), lax.axis_index("gy")
    return x, y, n_x, n_y


def source_kernel(steps, wells, table_ref, _, src_ref):
    here_x, here_y, n_x, n_y = spot()
    count = table_ref.shape[0]
    rx, ry = src_ref.shape[1] - 2 * H, src_ref.shape[2] - 2 * H
    of_wells = table_ref[:, 0, :]
    columns = [
        jnp.broadcast_to(of_wells[:, c : c + 1], (count, 128)) for c in range(wells * steps)
    ]
    owner_iota = lax.broadcasted_iota(jnp.int32, (count, 128), 0)
    sub = lax.broadcasted_iota(jnp.int32, (128, 128), 0)

    def spans(length):
        return ((0, H, length - H), (H, length, 0), (H + length, H, 0))

    for dx, (x0, size_x, from_x) in enumerate(spans(rx)):
        for dy, (y0, size_y, from_y) in enumerate(spans(ry)):
            at_x, at_y = here_x + dx - 1, here_y + dy - 1
            inside = (at_x >= 0) & (at_x < n_x) & (at_y >= 0) & (at_y < n_y)
            slot = table_ref[jnp.where(inside, at_x * n_y + at_y, 0)]
            cell = slot[1:2, :].astype(jnp.int32)
            well = slot[2:3, :].astype(jnp.int32)
            wi = slot[3:4, :] * inside.astype(F32)
            owner = well // wells
            within = well - owner * wells
            hot = owner_iota == owner
            in_lane = sub == (cell & 127)
            pieces = []
            for step in range(steps):
                chosen = columns[step]
                for u in range(1, wells):
                    chosen = jnp.where(within == u, columns[u * steps + step], chosen)
                value = jnp.sum(jnp.where(hot, chosen, 0.0), axis=0, keepdims=True) * wi
                high = value.astype(BF16).astype(F32)
                for piece in (high, value - high):
                    pieces.append(jnp.where(in_lane, piece, 0.0).astype(BF16))
            xi = lax.broadcasted_iota(jnp.int32, (size_x, size_y, 128), 0) + from_x
            yi = lax.broadcasted_iota(jnp.int32, (size_x, size_y, 128), 1) + from_y
            target = (xi * ry + yi).reshape(size_x * size_y, 128)
            by_row = jnp.where(target == (cell >> 7), 1.0, 0.0).astype(BF16)
            found = lax.dot_general(
                by_row, jnp.concatenate(pieces), (((1,), (1,)), ((), ())),
                preferred_element_type=F32,
            )
            for step in range(steps):
                part = found[:, step * 256 : step * 256 + 128]
                part = part + found[:, step * 256 + 128 : step * 256 + 256]
                src_ref[step, x0 : x0 + size_x, y0 : y0 + size_y, :] = part.reshape(
                    size_x, size_y, 128
                )


def by_v(ref, lead, x):
    return jnp.stack([ref[(*lead, x, pl.ds(v, 8, stride=V), slice(None))] for v in range(V)])


def up_v(value):
    return jnp.concatenate([value[1:], pltpu.roll(value[0], 7, 0)[None]])


def down_v(value):
    return jnp.concatenate([pltpu.roll(value[V - 1], 1, 0)[None], value[:-1]])


def roll_z(value, by):
    return pltpu.roll(value, by, 2)


def fill(dst, own, reaches, z_got, x_got, first=0):
    rx, ry, nz = own.shape[1:]

    def middle(z_low, z_high):
        def one(n, _):
            dst[n, H : H + rx, 0:H, :] = z_low[n + first]
            dst[n, H : H + rx, H : H + ry, :] = own[n]
            dst[n, H : H + rx, H + ry : 2 * H + ry, :] = z_high[n + first]
            return 0

        lax.fori_loop(0, len(reaches), one, 0)

    def outer(x_low, x_high):
        sides = (x_low, x_high)
        for begin, count, reach, base in parts_of(reaches)[0]:

            def one(k, _):
                n = begin + k
                row = base + k * rows_of_array(reach)
                for side in (0, 1):
                    at = H - reach if side == 0 else H + rx
                    dst[n, at : at + reach, H : H + ry, :] = sides[side][pl.ds(row, reach)]
                    known = set()
                    for y in (0, 1):
                        to = y * (H + ry)
                        for t in range(tiles_of(reach)):
                            tile = sides[side][row + reach + t, y * H : (y + 1) * H, :]
                            near, far = unfold(tile, t + 1, y == 1)
                            for dx, value in ((t + 1, near), (reach - t - 1, far)):
                                x = H - dx if side == 0 else H + rx + dx - 1
                                dst[n, x, to : to + H, :] = value
                                known.add(dx)
                    for dx in range(1, H + 1):
                        x = H - dx if side == 0 else H + rx + dx - 1
                        if dx not in known:
                            for y in (0, H + ry):
                                dst[n, x, y : y + H, :] = jnp.zeros((H, nz), F32)
                        if dx > reach:
                            dst[n, x, H : H + ry, :] = jnp.zeros((ry, nz), F32)
                return 0

            lax.fori_loop(0, count, one, 0)

    by_side("gy", middle, *z_got)
    by_side("gx", outer, *x_got)


GEO, COEF = 8, 7
TOP_REACH = (GEO,) * 3 + (COEF,) * 8
LAM_REACH = (GEO,) * 2


SA, RA, PC, FR, RB, QC, MC, AA, AB = range(9)
TX, TY, TZ, TU, WS = range(5)


def coefficients(raw, base, src_ref, step, x, total):
    c_pp, c_ss, c_ps, c_sp, frac, mob, g_p, g_s = [by_v(raw, (base + n,), x) for n in range(8)]
    den_a = c_pp + total
    den_b = c_ss + mob * total
    s_a = jnp.where(den_a > 0, OMEGA / den_a, 0.0)
    s_b = jnp.where(den_b > 0, OMEGA / den_b, 0.0)
    r_a = g_p + by_v(src_ref, (step,), x)
    return s_a, r_a, c_sp + frac * total, frac, s_b * g_s, s_b * c_ps, s_b * mob, s_b


BLOCK = 2
UNROLL = 4


def sweeps(coef, geo, bufs, lin, begin, ex):
    def work(number, x, count):
        old, new = bufs[(number - 1) % 2], bufs[number % 2]
        tx = [geo[TX, x + r] for r in range(count + 1)]
        values = [[old[f][x - 1 + r] for r in range(count + 2)] for f in range(2)]
        results = []
        for r in range(count):
            at = x + r
            ty = geo[TY, at]
            ty_up = up_v(ty)
            tz, tz_up = geo[TZ, at], geo[TU, at]

            def around(v):
                c = v[r + 1]
                total = tx[r + 1] * v[r + 2] + tx[r] * v[r]
                total = total + (ty_up * up_v(c) + ty * down_v(c))
                total = total + (tz_up * roll_z(c, 127) + tz * roll_z(c, 1))
                return c, total

            a, n_a = around(values[0])
            b, n_b = around(values[1])
            new_a = KEEP * a + coef[SA, at] * (
                (coef[RA, at] + n_a) + (coef[FR, at] * n_b - coef[PC, at] * b)
            )
            new_b = (KEEP * b + coef[RB, at]) + (coef[MC, at] * n_b - coef[QC, at] * a)
            results.append((new_a, new_b))
        for r in range(count):
            for f in range(2):
                if number == SWEEPS:
                    for v in range(V):
                        lin[f, x + r, pl.ds(v, 8, stride=V), :] = results[r][f][v]
                else:
                    new[f][x + r] = results[r][f]

    for number in range(begin, SWEEPS + 1):
        size = BLOCK * UNROLL
        total = ex - 2 * number

        def many(i, _):
            for u in range(UNROLL):
                work(number, number + i * size + u * BLOCK, BLOCK)
            return 0

        lax.fori_loop(0, total // size, many, 0)
        for at in range(total - total % size, total, BLOCK):
            work(number, number + at, BLOCK)


def finish(last, step, steps, wells, lin, frac, table_ref, before, outs):
    rx, ry, nz = frac.shape[-3:]
    out_wells = outs[-1]

    def copies(low, high):
        def copy(x, _):
            for f in range(2):
                row = lin[f, H + x, H : H + ry, :]
                if last:
                    outs[f][x] = row
                else:
                    outs[0][f, x] = row
                    low[f, x] = row[0:H]
                    high[f, x] = row[ry - H :]
            return 0

        lax.fori_loop(0, rx, copy, 0, unroll=2)

    if last:
        copies(None, None)
    else:
        by_side("gy", copies, outs[1], outs[2])
    mix = lin[0, H : H + rx, H : H + ry, :] + frac[...] * lin[1, H : H + rx, H : H + ry, :]
    mix = mix.reshape(rx * ry, nz)
    here_x, here_y, _, n_y = spot()
    slot = table_ref[here_x * n_y + here_y]
    lane = lax.broadcasted_iota(jnp.int32, (128, 128), 1)
    diagonal = lax.broadcasted_iota(jnp.int32, (128, 128), 0) == lane

    def upright(row):
        return jnp.sum(jnp.where(diagonal, row, 0.0), axis=1, keepdims=True)

    cell = upright(slot[1:2, :]).astype(jnp.int32)
    wi = upright(slot[3:4, :])
    by_row = jnp.where(
        lax.broadcasted_iota(jnp.int32, (128, rx * ry), 1) == (cell >> 7), 1.0, 0.0
    ).astype(BF16)
    picked = None
    for _ in range(3):
        piece = mix.astype(BF16)
        mix = mix - piece.astype(F32)
        add = jnp.dot(by_row, piece, preferred_element_type=F32)
        picked = add if picked is None else picked + add
    values = jnp.sum(jnp.where(lane == (cell & 127), picked, 0.0), axis=1, keepdims=True)
    values = values * wi
    spread = jnp.where(lane == step, values, 0.0)
    well = slot[2:3, :].astype(jnp.int32)
    count = table_ref.shape[0] * wells
    hot = jnp.where(
        lax.broadcasted_iota(jnp.int32, (count, 128), 0) == well, 1.0, 0.0
    ).astype(F32)
    dense = jnp.dot(hot, spread, precision=HIGHEST, preferred_element_type=F32)
    if before is not None:
        dense = dense + before[...]
    out_wells[...] = dense


def first_kernel(step, steps, wells, *refs):
    table_ref, src_ref, own, z_low, z_high, x_low, x_high = refs[:7]
    geo = refs[7]
    outs = refs[8:12]
    raw, coef, fa0, fb0, fa1, fb1, lin = refs[12:]
    rx, ry, nz = own.shape[1:]
    ex = rx + 2 * H
    fill(raw, own, TOP_REACH, (z_low, z_high), (x_low, x_high))
    here_x, here_y, _, _ = spot()

    @pl.when(here_x == 0)
    def _():
        raw[0, H, :, :] = jnp.zeros(raw.shape[2:], F32)

    @pl.when(here_y == 0)
    def _():
        def clear(x, _):
            raw[1, x, H : H + 1, :] = jnp.zeros((1, nz), F32)
            return 0

        lax.fori_loop(0, ex, clear, 0)

    def geometry(x, _):
        lane = lax.broadcasted_iota(jnp.int32, (V, 8, nz), 2)
        tz = jnp.where(lane == 0, 0.0, by_v(raw, (2,), x))
        geo[TX, x] = by_v(raw, (0,), x)
        geo[TY, x] = by_v(raw, (1,), x)
        geo[TZ, x] = tz
        geo[TU, x] = roll_z(tz, 127)
        return 0

    lax.fori_loop(0, ex, geometry, 0, unroll=4)

    def prepare(x, _):
        ty = geo[TY, x]
        total = (
            (geo[TX, x + 1] + geo[TX, x]) + (up_v(ty) + ty) + (geo[TU, x] + geo[TZ, x])
        )
        geo[WS, x] = total
        s_a, r_a, p, frac, r_b, q, m, _ = coefficients(
            raw, 3, src_ref, step, x, total
        )
        coef[SA, x] = s_a
        coef[RA, x] = r_a
        coef[PC, x] = p
        coef[FR, x] = frac
        coef[RB, x] = r_b
        coef[QC, x] = q
        coef[MC, x] = m
        fa1[x] = s_a * r_a
        fb1[x] = r_b
        return 0

    lax.fori_loop(0, ex - 1, prepare, 0)
    sweeps(coef, geo, ((fa0, fb0), (fa1, fb1)), lin, 2, ex)
    finish(False, step, steps, wells, lin, own.at[7], table_ref, None, outs)


def prepare_kernel(step, first, with_acc, *refs):
    src_ref, geo, own, z_low, z_high, x_low, x_high = refs[:7]
    if with_acc:
        coef, acc_out, raw = refs[7:]
    else:
        acc, coef, raw = refs[7:]
    rx, ry, nz = own.shape[1:]
    ex = rx + 2 * H
    fill(raw, own, (COEF,) * own.shape[0], (z_low, z_high), (x_low, x_high), first)

    def prepare(x, _):
        s_a, r_a, p, frac, r_b, q, m, s_b = coefficients(
            raw, 0, src_ref, step, x, geo[WS, x]
        )
        coef[SA, x] = s_a
        coef[RA, x] = r_a
        coef[PC, x] = p
        coef[FR, x] = frac
        coef[RB, x] = r_b
        coef[QC, x] = q
        coef[MC, x] = m
        if with_acc:
            a, b = by_v(raw, (8,), x), by_v(raw, (9,), x)
            acc_out[0, x] = a
            acc_out[1, x] = b
        else:
            a, b = acc[0, x], acc[1, x]
        coef[AA, x] = a
        coef[AB, x] = s_b * b
        return 0

    lax.fori_loop(0, ex - 1, prepare, 0)


def sweep_kernel(last, step, steps, wells, *refs):
    table_ref, coef, geo, own, lam, z_low, z_high, x_low, x_high, before = refs[:10]
    outs = refs[10:-6]
    now, fa0, fb0, fa1, fb1, lin = refs[-6:]
    rx, ry, nz = own.shape[1:]
    ex = rx + 2 * H
    fill(lin, lam, LAM_REACH, (z_low, z_high), (x_low, x_high))

    def begin(x, _):
        a, b = by_v(lin, (0,), x), by_v(lin, (1,), x)
        fa0[x] = a
        fb0[x] = b
        now[0, x] = coef[RA, x] + coef[AA, x] * a
        now[1, x] = coef[RB, x] + coef[AB, x] * b
        return 0

    lax.fori_loop(0, ex, begin, 0, unroll=4)

    class Joined:
        def __getitem__(self, at):
            n, x = at
            return now[0, x] if n == RA else now[1, x] if n == RB else coef[n, x]

    sweeps(Joined(), geo, ((fa0, fb0), (fa1, fb1)), lin, 1, ex)
    finish(last, step, steps, wells, lin, own.at[4], table_ref, before, outs)


def local(
    grad_p, grad_s, acc_p, acc_s, trans_x, trans_y, trans_z, c_pp, c_ss, c_ps, c_sp,
    frac, mobility, rate_mis, bhp_mis, control, perf_well, perf_cell, perf_wi,
):
    dims = rx, ry, nz = trans_x.shape
    ex, ey = rx + 2 * H, ry + 2 * H
    steps = grad_p.shape[0]
    wells = rate_mis.shape[0]
    devices = lax.axis_size("gx") * lax.axis_size("gy")
    own = [c_pp, c_ss, c_ps, c_sp, frac, mobility, grad_p, grad_s]
    top = steps - 1

    arrays = [trans_x, trans_y, trans_z] + own
    leads = [None] * 3 + [top] * 8
    split = len(arrays)
    small = [rate_mis, bhp_mis, control] + [p[None] for p in (perf_well, perf_cell, perf_wi)]
    mine = pl.pallas_call(
        functools.partial(table_kernel, steps),
        in_specs=[HBM] * 6,
        out_specs=VMEM,
        out_shape=sds(devices, 4, 128),
        scratch_shapes=[pltpu.VMEM(p.shape, p.dtype) for p in small]
        + [pltpu.SemaphoreType.DMA((6,))],
        name="table",
    )(*small)
    blocks, y_low, y_high, token = load(arrays, leads, dims, ())
    z_got = swaps(y_low, y_high, "gy")
    mine, _ = lax.optimization_barrier((mine, token))
    table = lax.all_to_all(mine, ("gx", "gy"), 0, 0, tiled=True)

    wide = widen(blocks, TOP_REACH, *z_got, (table,))
    x_got = swaps(*wide, "gx")
    src = call(
        functools.partial(source_kernel, steps, wells), [table, wide[0]],
        [sds(steps, ex, ey, nz)], "sources", 8, [VMEM, ANY],
    )[0]

    plan, sizes = [], []
    for h, step in enumerate(reversed(range(top))):
        plan += [(n, step, h, n) for n in range(8)]
        if h == 0:
            plan += [(8, None, h, 8), (9, None, h, 9)]
        sizes.append(10 if h == 0 else 8)
    made = more(own + [acc_p, acc_s], plan, sizes, dims, table)
    held = dict(zip(reversed(range(top)), made[:top]))
    ends = {step: made[top + 2 * h : top + 2 * h + 2] for h, step in enumerate(reversed(range(top)))}
    m_z = {}

    def beside(step, after):
        group = held[step]
        return widen(group, (COEF,) * group.shape[0], *m_z[step], (after,))

    first, second = ends[top - 1]
    first, second, _ = lax.optimization_barrier((first, second, src))
    m_z[top - 1] = swaps(first, second, "gy")
    sides = beside(top - 1, src)
    late = sides[0]
    sides = swaps(*sides, "gx")

    ext = (ex, V, 8, nz)
    lam_out = [sds(2, rx, ry, nz), sds(2, rx, H, nz), sds(2, rx, H, nz)]
    well_out = sds(devices * wells, 128)
    fields = [pltpu.VMEM(ext, F32)] * 4 + [pltpu.VMEM((2, ex, ey, nz), F32)]

    geo, lam, low, high, dense = call(
        functools.partial(first_kernel, top, steps, wells),
        [table, src, blocks, *z_got, *x_got],
        [sds(5, *ext)] + lam_out + [well_out], "step_top", 16,
        scratch=[pltpu.VMEM((split, ex, ey, nz), F32), pltpu.VMEM((7, *ext), F32)] + fields,
    )

    acc = None
    for step in reversed(range(top)):
        last = step == 0
        with_acc = step == top - 1
        if not with_acc:
            sides = swaps(*beside(step, coef), "gx")
        else:
            first, second, _ = lax.optimization_barrier((*ends[step - 1], late))
            m_z[step - 1] = swaps(first, second, "gy")
            low, high, *_ = lax.optimization_barrier((low, high, *m_z[step - 1]))
        made = call(
            functools.partial(prepare_kernel, step, 0, with_acc),
            [src, geo, held[step], *m_z[step], *sides] + ([] if with_acc else [acc]),
            [sds(9, *ext)] + ([sds(2, *ext)] if with_acc else []), "prepare", 8,
            scratch=[pltpu.VMEM((10 if with_acc else 8, ex, ey, nz), F32)],
        )
        coef = made[0]
        if with_acc:
            acc = made[1]

        l_z = swaps(low, high, "gy")
        l_x = swaps(*widen(lam, LAM_REACH, *l_z), "gx")
        outs = [sds(rx, ry, nz)] * 2 if last else lam_out
        outs = call(
            functools.partial(sweep_kernel, last, step, steps, wells),
            [table, coef, geo, held[step], lam, *l_z, *l_x, dense],
            outs + [well_out], "step", 8, scratch=[pltpu.VMEM((2, *ext), F32)] + fields,
        )
        dense = outs[-1]
        if not last:
            lam, low, high = outs[:3]

    dense = dense.reshape(devices, wells, 128)
    parts = lax.all_to_all(dense, ("gx", "gy"), 0, 0, tiled=True)
    well_grad = jnp.sum(parts, axis=0)[:, :steps]
    return outs[0], outs[1], well_grad


def solution(mesh):
    cells3 = P("gx", "gy", None)
    cells4 = P(None, "gx", "gy", None)
    flat = ("gx", "gy")
    placed = (cells4,) * 2 + (cells3,) * 5 + (cells4,) * 6 + (P(flat, None),) * 3 + (P(flat),) * 3
    return jax.shard_map(
        local,
        mesh=mesh,
        in_specs=placed,
        out_specs=(cells3, cells3, P(flat, None)),
        check_vma=False,
    )
```

```python
import functools

import jax
import jax.numpy as jnp
from jax import lax
from jax.experimental import pallas as pl
from jax.experimental.pallas import tpu as pltpu
from jax.sharding import PartitionSpec as P

SWEEPS = 8
OMEGA = 0.8
KEEP = 1.0 - OMEGA
H = 8
V = 4
HIGHEST = lax.Precision.HIGHEST
F32 = jnp.float32
BF16 = jnp.bfloat16
FLOPS = 1e9

VMEM = pl.BlockSpec(memory_space=pltpu.VMEM)
ANY = pl.BlockSpec(memory_space=pl.ANY)
HBM = pl.BlockSpec(memory_space=pltpu.HBM)


def sds(*shape):
    return jax.ShapeDtypeStruct(shape, F32)


def params(mib):
    return pltpu.CompilerParams(vmem_limit_bytes=mib * 1024 * 1024)


TIMES = {"step_top": 7, "step": 6, "sources": 3, "prepare": 1.5}


def estimate(name):
    work = TIMES.get(name, 0.5)
    return pl.CostEstimate(
        flops=int(work * FLOPS), bytes_accessed=int(work * 3.0e6), transcendentals=0
    )


def call(kernel, ins, outs, name, mib, specs=None, scratch=()):
    return pl.pallas_call(
        kernel,
        in_specs=specs or [VMEM] * len(ins),
        out_specs=[VMEM] * len(outs),
        out_shape=outs,
        scratch_shapes=list(scratch),
        compiler_params=params(mib),
        cost_estimate=estimate(name),
        name=name,
    )(*ins)


def swaps(first, second, axis):
    length = lax.axis_size(axis)
    even = [(i, i ^ 1) for i in range(length) if i ^ 1 < length]
    odd = [(i, i + 1) for i in range(1, length - 1, 2)]
    odd += [(j, i) for i, j in odd]
    return lax.ppermute(first, axis, even), lax.ppermute(second, axis, odd)


def by_side(axis, work, first, second):
    at = lax.axis_index(axis) % 2

    @pl.when(at == 1)
    def _():
        work(first, second)

    @pl.when(at == 0)
    def _():
        work(second, first)


def load_kernel(leads, *refs):
    count = len(leads)
    ins, (own, y_low, y_high, token), sems = refs[:count], refs[-5:-1], refs[-1]
    token[...] = jnp.zeros(token.shape, F32)
    copies = [
        pltpu.make_async_copy(
            ins[n] if lead is None else ins[n].at[lead], own.at[n], sems.at[n]
        )
        for n, lead in enumerate(leads)
    ]
    for c in copies:
        c.start()
    for c in copies:
        c.wait()
    by_side("gy", lambda low, high: y_edges(own, low, high), y_low, y_high)


def y_edges(own, low, high):
    ry = own.shape[2]

    def one(n, _):
        low[n] = own[n, :, 0:H, :]
        high[n] = own[n, :, ry - H :, :]
        return 0

    lax.fori_loop(0, own.shape[0], one, 0)


def load(arrays, leads, dims, after):
    n = len(leads)
    rx, ry, nz = dims
    return pl.pallas_call(
        functools.partial(load_kernel, leads),
        in_specs=[HBM] * n + [ANY] * len(after),
        out_specs=[VMEM] * 4,
        out_shape=[sds(n, *dims)] + [sds(n, rx, H, nz)] * 2 + [sds(8, 128)],
        scratch_shapes=[pltpu.SemaphoreType.DMA((n,))],
        name="load",
    )(*arrays, *after)


def more_kernel(plan, count, parts, *refs):
    ins, outs = refs[:count], refs[count + 1 :]
    holders, firsts, seconds = outs[:parts], outs[parts::2], outs[parts + 1 :: 2]
    rx, ry = holders[0].shape[1:3]

    def work(lows, highs):
        def row(x, _):
            for i, lead, h, m in plan:
                value = ins[i][x] if lead is None else ins[i][lead, x]
                holders[h][m, x] = value
                lows[h][m, x] = value[0:H]
                highs[h][m, x] = value[ry - H :]
            return 0

        lax.fori_loop(0, rx, row, 0)

    by_side("gy", work, firsts, seconds)


def more(arrays, plan, sizes, dims, after):
    rx, ry, nz = dims
    return call(
        functools.partial(more_kernel, plan, len(arrays), len(sizes)), list(arrays) + [after],
        [sds(m, *dims) for m in sizes] + [sds(m, rx, H, nz) for m in sizes for _ in range(2)],
        "more", 4, [VMEM] * len(arrays) + [ANY],
    )


def tiles_of(reach):
    return reach // 2


def rows_of_array(reach):
    return reach + tiles_of(reach)


def fold(row, reach, high):
    tiles = []
    for dx in range(1, tiles_of(reach) + 1):
        near, far = row(dx), row(reach - dx)
        sub = lax.broadcasted_iota(jnp.int32, near.shape, 0)
        if high:
            tiles.append(jnp.where(sub < 8 - dx, near, pltpu.roll(far, 8 - dx, 0)))
        else:
            tiles.append(jnp.where(sub >= dx, near, pltpu.roll(far, dx, 0)))
    return tiles


def unfold(tile, dx, high):
    return tile, pltpu.roll(tile, dx if high else 8 - dx, 0)


def parts_of(reaches):
    parts, row = [], 0
    for n, reach in enumerate(reaches):
        if parts and parts[-1][2] == reach:
            parts[-1][1] += 1
        else:
            parts.append([n, 1, reach, row])
        row += rows_of_array(reach)
    return parts, row


def widen_kernel(reaches, first, own, z_first, z_second, *refs):
    rx = own.shape[1]

    def work(z_low, z_high, outs):
        for begin, count, reach, base in parts_of(reaches)[0]:

            def one(k, _):
                n = begin + k
                at = base + k * rows_of_array(reach)
                for side in (0, 1):
                    start = 0 if side == 0 else rx - reach
                    outs[side][pl.ds(at, reach)] = own[n, start : start + reach]
                    for high, z in ((0, z_low), (1, z_high)):

                        def row(dx):
                            return z[n + first, dx - 1 if side == 0 else rx - dx]

                        for t, tile in enumerate(fold(row, reach, high == 1)):
                            outs[side][at + reach + t, high * H : (high + 1) * H, :] = tile
                return 0

            lax.fori_loop(0, count, one, 0)

    def along_x(low, high):
        by_side("gy", lambda a, b: work(a, b, (low, high)), z_first, z_second)

    by_side("gx", along_x, *refs[-2:])


def widen(own, reaches, z_low, z_high, after=(), first=0):
    _, rx, ry, nz = own.shape
    return call(
        functools.partial(widen_kernel, reaches, first), [own, z_low, z_high, *after],
        [sds(parts_of(reaches)[1], ry, nz)] * 2, "widen", 4, [VMEM] * 3 + [ANY] * len(after),
    )


def table_kernel(steps, *refs):
    rate, bhp, control, perf_well, perf_cell, perf_wi = [r[...] for r in refs[:6]]
    out = refs[-1]
    wells = rate.shape[0]
    effective = jnp.where(control == 1, rate, bhp)
    lane = lax.broadcasted_iota(jnp.int32, (1, 128), 1)
    row = jnp.zeros((1, 128), F32)
    for u in range(wells):
        for n in range(steps):
            row = jnp.where(lane == u * steps + n, effective[u : u + 1, n : n + 1], row)
    mine = jnp.concatenate([row, perf_cell.astype(F32), perf_well.astype(F32), perf_wi])
    out[...] = jnp.broadcast_to(mine[None], out.shape)


def spot():
    n_x, n_y = lax.axis_size("gx"), lax.axis_size("gy")
    x, y = lax.axis_index("gx"), lax.axis_index("gy")
    return x, y, n_x, n_y


def source_kernel(steps, wells, table_ref, _, src_ref):
    here_x, here_y, n_x, n_y = spot()
    count = table_ref.shape[0]
    rx, ry = src_ref.shape[1] - 2 * H, src_ref.shape[2] - 2 * H
    of_wells = table_ref[:, 0, :]
    columns = [
        jnp.broadcast_to(of_wells[:, c : c + 1], (count, 128)) for c in range(wells * steps)
    ]
    owner_iota = lax.broadcasted_iota(jnp.int32, (count, 128), 0)
    sub = lax.broadcasted_iota(jnp.int32, (128, 128), 0)

    def spans(length):
        return ((0, H, length - H), (H, length, 0), (H + length, H, 0))

    for dx, (x0, size_x, from_x) in enumerate(spans(rx)):
        for dy, (y0, size_y, from_y) in enumerate(spans(ry)):
            at_x, at_y = here_x + dx - 1, here_y + dy - 1
            inside = (at_x >= 0) & (at_x < n_x) & (at_y >= 0) & (at_y < n_y)
            slot = table_ref[jnp.where(inside, at_x * n_y + at_y, 0)]
            cell = slot[1:2, :].astype(jnp.int32)
            well = slot[2:3, :].astype(jnp.int32)
            wi = slot[3:4, :] * inside.astype(F32)
            owner = well // wells
            within = well - owner * wells
            hot = owner_iota == owner
            in_lane = sub == (cell & 127)
            pieces = []
            for step in range(steps):
                chosen = columns[step]
                for u in range(1, wells):
                    chosen = jnp.where(within == u, columns[u * steps + step], chosen)
                value = jnp.sum(jnp.where(hot, chosen, 0.0), axis=0, keepdims=True) * wi
                high = value.astype(BF16).astype(F32)
                for piece in (high, value - high):
                    pieces.append(jnp.where(in_lane, piece, 0.0).astype(BF16))
            xi = lax.broadcasted_iota(jnp.int32, (size_x, size_y, 128), 0) + from_x
            yi = lax.broadcasted_iota(jnp.int32, (size_x, size_y, 128), 1) + from_y
            target = (xi * ry + yi).reshape(size_x * size_y, 128)
            by_row = jnp.where(target == (cell >> 7), 1.0, 0.0).astype(BF16)
            found = lax.dot_general(
                by_row, jnp.concatenate(pieces), (((1,), (1,)), ((), ())),
                preferred_element_type=F32,
            )
            for step in range(steps):
                part = found[:, step * 256 : step * 256 + 128]
                part = part + found[:, step * 256 + 128 : step * 256 + 256]
                src_ref[step, x0 : x0 + size_x, y0 : y0 + size_y, :] = part.reshape(
                    size_x, size_y, 128
                )


def by_v(ref, lead, x):
    return jnp.stack([ref[(*lead, x, pl.ds(v, 8, stride=V), slice(None))] for v in range(V)])


def up_v(value):
    return jnp.concatenate([value[1:], pltpu.roll(value[0], 7, 0)[None]])


def down_v(value):
    return jnp.concatenate([pltpu.roll(value[V - 1], 1, 0)[None], value[:-1]])


def roll_z(value, by):
    return pltpu.roll(value, by, 2)


def fill(dst, own, reaches, z_got, x_got, first=0):
    rx, ry, nz = own.shape[1:]

    def middle(z_low, z_high):
        def one(n, _):
            dst[n, H : H + rx, 0:H, :] = z_low[n + first]
            dst[n, H : H + rx, H : H + ry, :] = own[n]
            dst[n, H : H + rx, H + ry : 2 * H + ry, :] = z_high[n + first]
            return 0

        lax.fori_loop(0, len(reaches), one, 0)

    def outer(x_low, x_high):
        sides = (x_low, x_high)
        for begin, count, reach, base in parts_of(reaches)[0]:

            def one(k, _):
                n = begin + k
                row = base + k * rows_of_array(reach)
                for side in (0, 1):
                    at = H - reach if side == 0 else H + rx
                    dst[n, at : at + reach, H : H + ry, :] = sides[side][pl.ds(row, reach)]
                    known = set()
                    for y in (0, 1):
                        to = y * (H + ry)
                        for t in range(tiles_of(reach)):
                            tile = sides[side][row + reach + t, y * H : (y + 1) * H, :]
                            near, far = unfold(tile, t + 1, y == 1)
                            for dx, value in ((t + 1, near), (reach - t - 1, far)):
                                x = H - dx if side == 0 else H + rx + dx - 1
                                dst[n, x, to : to + H, :] = value
                                known.add(dx)
                    for dx in range(1, H + 1):
                        x = H - dx if side == 0 else H + rx + dx - 1
                        if dx not in known:
                            for y in (0, H + ry):
                                dst[n, x, y : y + H, :] = jnp.zeros((H, nz), F32)
                        if dx > reach:
                            dst[n, x, H : H + ry, :] = jnp.zeros((ry, nz), F32)
                return 0

            lax.fori_loop(0, count, one, 0)

    by_side("gy", middle, *z_got)
    by_side("gx", outer, *x_got)


GEO, COEF = 8, 7
TOP_REACH = (GEO,) * 3 + (COEF,) * 8
LAM_REACH = (GEO,) * 2


SA, RA, PC, FR, RB, QC, MC, AA, AB = range(9)
TX, TY, TZ, TU, WS = range(5)


def coefficients(raw, base, src_ref, step, x, total):
    c_pp, c_ss, c_ps, c_sp, frac, mob, g_p, g_s = [by_v(raw, (base + n,), x) for n in range(8)]
    den_a = c_pp + total
    den_b = c_ss + mob * total
    s_a = jnp.where(den_a > 0, OMEGA / den_a, 0.0)
    s_b = jnp.where(den_b > 0, OMEGA / den_b, 0.0)
    r_a = g_p + by_v(src_ref, (step,), x)
    return s_a, r_a, c_sp + frac * total, frac, s_b * g_s, s_b * c_ps, s_b * mob, s_b


BLOCK = 2
UNROLL = 4


def sweeps(coef, geo, bufs, lin, begin, ex):
    def work(number, x, count):
        old, new = bufs[(number - 1) % 2], bufs[number % 2]
        tx = [geo[TX, x + r] for r in range(count + 1)]
        values = [[old[f][x - 1 + r] for r in range(count + 2)] for f in range(2)]
        results = []
        for r in range(count):
            at = x + r
            ty = geo[TY, at]
            ty_up = up_v(ty)
            tz, tz_up = geo[TZ, at], geo[TU, at]

            def around(v):
                c = v[r + 1]
                total = tx[r + 1] * v[r + 2] + tx[r] * v[r]
                total = total + (ty_up * up_v(c) + ty * down_v(c))
                total = total + (tz_up * roll_z(c, 127) + tz * roll_z(c, 1))
                return c, total

            a, n_a = around(values[0])
            b, n_b = around(values[1])
            new_a = KEEP * a + coef[SA, at] * (
                (coef[RA, at] + n_a) + (coef[FR, at] * n_b - coef[PC, at] * b)
            )
            new_b = (KEEP * b + coef[RB, at]) + (coef[MC, at] * n_b - coef[QC, at] * a)
            results.append((new_a, new_b))
        for r in range(count):
            for f in range(2):
                if number == SWEEPS:
                    for v in range(V):
                        lin[f, x + r, pl.ds(v, 8, stride=V), :] = results[r][f][v]
                else:
                    new[f][x + r] = results[r][f]

    for number in range(begin, SWEEPS + 1):
        size = BLOCK * UNROLL
        total = ex - 2 * number

        def many(i, _):
            for u in range(UNROLL):
                work(number, number + i * size + u * BLOCK, BLOCK)
            return 0

        lax.fori_loop(0, total // size, many, 0)
        for at in range(total - total % size, total, BLOCK):
            work(number, number + at, BLOCK)


def finish(last, step, steps, wells, lin, frac, table_ref, before, outs):
    rx, ry, nz = frac.shape[-3:]
    out_wells = outs[-1]

    def copies(low, high):
        def copy(x, _):
            for f in range(2):
                row = lin[f, H + x, H : H + ry, :]
                if last:
                    outs[f][x] = row
                else:
                    outs[0][f, x] = row
                    low[f, x] = row[0:H]
                    high[f, x] = row[ry - H :]
            return 0

        lax.fori_loop(0, rx, copy, 0, unroll=2)

    if last:
        copies(None, None)
    else:
        by_side("gy", copies, outs[1], outs[2])
    mix = lin[0, H : H + rx, H : H + ry, :] + frac[...] * lin[1, H : H + rx, H : H + ry, :]
    mix = mix.reshape(rx * ry, nz)
    here_x, here_y, _, n_y = spot()
    slot = table_ref[here_x * n_y + here_y]
    lane = lax.broadcasted_iota(jnp.int32, (128, 128), 1)
    diagonal = lax.broadcasted_iota(jnp.int32, (128, 128), 0) == lane

    def upright(row):
        return jnp.sum(jnp.where(diagonal, row, 0.0), axis=1, keepdims=True)

    cell = upright(slot[1:2, :]).astype(jnp.int32)
    wi = upright(slot[3:4, :])
    by_row = jnp.where(
        lax.broadcasted_iota(jnp.int32, (128, rx * ry), 1) == (cell >> 7), 1.0, 0.0
    ).astype(BF16)
    picked = None
    for _ in range(3):
        piece = mix.astype(BF16)
        mix = mix - piece.astype(F32)
        add = jnp.dot(by_row, piece, preferred_element_type=F32)
        picked = add if picked is None else picked + add
    values = jnp.sum(jnp.where(lane == (cell & 127), picked, 0.0), axis=1, keepdims=True)
    values = values * wi
    spread = jnp.where(lane == step, values, 0.0)
    well = slot[2:3, :].astype(jnp.int32)
    count = table_ref.shape[0] * wells
    hot = jnp.where(
        lax.broadcasted_iota(jnp.int32, (count, 128), 0) == well, 1.0, 0.0
    ).astype(F32)
    dense = jnp.dot(hot, spread, precision=HIGHEST, preferred_element_type=F32)
    if before is not None:
        dense = dense + before[...]
    out_wells[...] = dense


def first_kernel(step, steps, wells, *refs):
    table_ref, src_ref, own, z_low, z_high, x_low, x_high = refs[:7]
    geo = refs[7]
    outs = refs[8:12]
    raw, coef, fa0, fb0, fa1, fb1, lin = refs[12:]
    rx, ry, nz = own.shape[1:]
    ex = rx + 2 * H
    fill(raw, own, TOP_REACH, (z_low, z_high), (x_low, x_high))
    here_x, here_y, _, _ = spot()

    @pl.when(here_x == 0)
    def _():
        raw[0, H, :, :] = jnp.zeros(raw.shape[2:], F32)

    @pl.when(here_y == 0)
    def _():
        def clear(x, _):
            raw[1, x, H : H + 1, :] = jnp.zeros((1, nz), F32)
            return 0

        lax.fori_loop(0, ex, clear, 0)

    def geometry(x, _):
        lane = lax.broadcasted_iota(jnp.int32, (V, 8, nz), 2)
        tz = jnp.where(lane == 0, 0.0, by_v(raw, (2,), x))
        geo[TX, x] = by_v(raw, (0,), x)
        geo[TY, x] = by_v(raw, (1,), x)
        geo[TZ, x] = tz
        geo[TU, x] = roll_z(tz, 127)
        return 0

    lax.fori_loop(0, ex, geometry, 0, unroll=4)

    def prepare(x, _):
        ty = geo[TY, x]
        total = (
            (geo[TX, x + 1] + geo[TX, x]) + (up_v(ty) + ty) + (geo[TU, x] + geo[TZ, x])
        )
        geo[WS, x] = total
        s_a, r_a, p, frac, r_b, q, m, _ = coefficients(
            raw, 3, src_ref, step, x, total
        )
        coef[SA, x] = s_a
        coef[RA, x] = r_a
        coef[PC, x] = p
        coef[FR, x] = frac
        coef[RB, x] = r_b
        coef[QC, x] = q
        coef[MC, x] = m
        fa1[x] = s_a * r_a
        fb1[x] = r_b
        return 0

    lax.fori_loop(0, ex - 1, prepare, 0)
    sweeps(coef, geo, ((fa0, fb0), (fa1, fb1)), lin, 2, ex)
    finish(False, step, steps, wells, lin, own.at[7], table_ref, None, outs)


def prepare_kernel(step, first, with_acc, *refs):
    src_ref, geo, own, z_low, z_high, x_low, x_high = refs[:7]
    if with_acc:
        coef, acc_out, raw = refs[7:]
    else:
        acc, coef, raw = refs[7:]
    rx, ry, nz = own.shape[1:]
    ex = rx + 2 * H
    fill(raw, own, (COEF,) * own.shape[0], (z_low, z_high), (x_low, x_high), first)

    def prepare(x, _):
        s_a, r_a, p, frac, r_b, q, m, s_b = coefficients(
            raw, 0, src_ref, step, x, geo[WS, x]
        )
        coef[SA, x] = s_a
        coef[RA, x] = r_a
        coef[PC, x] = p
        coef[FR, x] = frac
        coef[RB, x] = r_b
        coef[QC, x] = q
        coef[MC, x] = m
        if with_acc:
            a, b = by_v(raw, (8,), x), by_v(raw, (9,), x)
            acc_out[0, x] = a
            acc_out[1, x] = b
        else:
            a, b = acc[0, x], acc[1, x]
        coef[AA, x] = a
        coef[AB, x] = s_b * b
        return 0

    lax.fori_loop(0, ex - 1, prepare, 0)


def sweep_kernel(last, step, steps, wells, *refs):
    table_ref, coef, geo, own, lam, z_low, z_high, x_low, x_high, before = refs[:10]
    outs = refs[10:-6]
    now, fa0, fb0, fa1, fb1, lin = refs[-6:]
    rx, ry, nz = own.shape[1:]
    ex = rx + 2 * H
    fill(lin, lam, LAM_REACH, (z_low, z_high), (x_low, x_high))

    def begin(x, _):
        a, b = by_v(lin, (0,), x), by_v(lin, (1,), x)
        fa0[x] = a
        fb0[x] = b
        now[0, x] = coef[RA, x] + coef[AA, x] * a
        now[1, x] = coef[RB, x] + coef[AB, x] * b
        return 0

    lax.fori_loop(0, ex, begin, 0, unroll=4)

    class Joined:
        def __getitem__(self, at):
            n, x = at
            return now[0, x] if n == RA else now[1, x] if n == RB else coef[n, x]

    sweeps(Joined(), geo, ((fa0, fb0), (fa1, fb1)), lin, 1, ex)
    finish(last, step, steps, wells, lin, own.at[4], table_ref, before, outs)


def local(
    grad_p, grad_s, acc_p, acc_s, trans_x, trans_y, trans_z, c_pp, c_ss, c_ps, c_sp,
    frac, mobility, rate_mis, bhp_mis, control, perf_well, perf_cell, perf_wi,
):
    dims = rx, ry, nz = trans_x.shape
    ex, ey = rx + 2 * H, ry + 2 * H
    steps = grad_p.shape[0]
    wells = rate_mis.shape[0]
    devices = lax.axis_size("gx") * lax.axis_size("gy")
    own = [c_pp, c_ss, c_ps, c_sp, frac, mobility, grad_p, grad_s]
    top = steps - 1

    arrays = [trans_x, trans_y, trans_z] + own
    leads = [None] * 3 + [top] * 8
    split = len(arrays)
    small = [rate_mis, bhp_mis, control] + [p[None] for p in (perf_well, perf_cell, perf_wi)]
    mine = call(
        functools.partial(table_kernel, steps), small, [sds(devices, 4, 128)], "table", 4
    )[0]
    blocks, y_low, y_high, token = load(arrays, leads, dims, ())
    z_got = swaps(y_low, y_high, "gy")
    mine, _ = lax.optimization_barrier((mine, token))
    table = lax.all_to_all(mine, ("gx", "gy"), 0, 0, tiled=True)

    wide = widen(blocks, TOP_REACH, *z_got, (table,))
    x_got = swaps(*wide, "gx")
    src = call(
        functools.partial(source_kernel, steps, wells), [table, wide[0]],
        [sds(steps, ex, ey, nz)], "sources", 8, [VMEM, ANY],
    )[0]

    plan, sizes = [], []
    for h, step in enumerate(reversed(range(top))):
        plan += [(n, step, h, n) for n in range(8)]
        if h == 0:
            plan += [(8, None, h, 8), (9, None, h, 9)]
        sizes.append(10 if h == 0 else 8)
    made = more(own + [acc_p, acc_s], plan, sizes, dims, table)
    held = dict(zip(reversed(range(top)), made[:top]))
    ends = {step: made[top + 2 * h : top + 2 * h + 2] for h, step in enumerate(reversed(range(top)))}
    m_z = {}

    def beside(step, after):
        group = held[step]
        return widen(group, (COEF,) * group.shape[0], *m_z[step], (after,))

    first, second = ends[top - 1]
    first, second, _ = lax.optimization_barrier((first, second, src))
    m_z[top - 1] = swaps(first, second, "gy")
    sides = beside(top - 1, src)
    late = sides[0]
    sides = swaps(*sides, "gx")

    ext = (ex, V, 8, nz)
    lam_out = [sds(2, rx, ry, nz), sds(2, rx, H, nz), sds(2, rx, H, nz)]
    well_out = sds(devices * wells, 128)
    fields = [pltpu.VMEM(ext, F32)] * 4 + [pltpu.VMEM((2, ex, ey, nz), F32)]

    geo, lam, low, high, dense = call(
        functools.partial(first_kernel, top, steps, wells),
        [table, src, blocks, *z_got, *x_got],
        [sds(5, *ext)] + lam_out + [well_out], "step_top", 16,
        scratch=[pltpu.VMEM((split, ex, ey, nz), F32), pltpu.VMEM((7, *ext), F32)] + fields,
    )

    acc = None
    for step in reversed(range(top)):
        last = step == 0
        with_acc = step == top - 1
        if not with_acc:
            sides = swaps(*beside(step, coef), "gx")
        else:
            first, second, _ = lax.optimization_barrier((*ends[step - 1], late))
            m_z[step - 1] = swaps(first, second, "gy")
            low, high, *_ = lax.optimization_barrier((low, high, *m_z[step - 1]))
        made = call(
            functools.partial(prepare_kernel, step, 0, with_acc),
            [src, geo, held[step], *m_z[step], *sides] + ([] if with_acc else [acc]),
            [sds(9, *ext)] + ([sds(2, *ext)] if with_acc else []), "prepare", 8,
            scratch=[pltpu.VMEM((10 if with_acc else 8, ex, ey, nz), F32)],
        )
        coef = made[0]
        if with_acc:
            acc = made[1]

        l_z = swaps(low, high, "gy")
        l_x = swaps(*widen(lam, LAM_REACH, *l_z), "gx")
        outs = [sds(rx, ry, nz)] * 2 if last else lam_out
        outs = call(
            functools.partial(sweep_kernel, last, step, steps, wells),
            [table, coef, geo, held[step], lam, *l_z, *l_x, dense],
            outs + [well_out], "step", 8, scratch=[pltpu.VMEM((2, *ext), F32)] + fields,
        )
        dense = outs[-1]
        if not last:
            lam, low, high = outs[:3]

    dense = dense.reshape(devices, wells, 128)
    parts = lax.all_to_all(dense, ("gx", "gy"), 0, 0, tiled=True)
    well_grad = jnp.sum(parts, axis=0)[:, :steps]
    return outs[0], outs[1], well_grad


def solution(mesh):
    cells3 = P("gx", "gy", None)
    cells4 = P(None, "gx", "gy", None)
    flat = ("gx", "gy")
    placed = (cells4,) * 2 + (cells3,) * 5 + (cells4,) * 6 + (P(flat, None),) * 3 + (P(flat),) * 3
    return jax.shard_map(
        local,
        mesh=mesh,
        in_specs=placed,
        out_specs=(cells3, cells3, P(flat, None)),
        check_vma=False,
    )
```

```python
import functools

import jax
import jax.numpy as jnp
from jax import lax
from jax.experimental import pallas as pl
from jax.experimental.pallas import tpu as pltpu
from jax.sharding import PartitionSpec as P

SWEEPS = 8
OMEGA = 0.8
KEEP = 1.0 - OMEGA
H = 8
V = 4
HIGHEST = lax.Precision.HIGHEST
F32 = jnp.float32
BF16 = jnp.bfloat16
FLOPS = 1e9

VMEM = pl.BlockSpec(memory_space=pltpu.VMEM)
ANY = pl.BlockSpec(memory_space=pl.ANY)
HBM = pl.BlockSpec(memory_space=pltpu.HBM)


def sds(*shape):
    return jax.ShapeDtypeStruct(shape, F32)


def params(mib):
    return pltpu.CompilerParams(vmem_limit_bytes=mib * 1024 * 1024)


TIMES = {"step_top": 7, "step": 6, "sources": 3, "prepare": 1.5}


def estimate(name):
    work = TIMES.get(name, 0.5)
    return pl.CostEstimate(
        flops=int(work * FLOPS), bytes_accessed=int(work * 3.0e6), transcendentals=0
    )


def call(kernel, ins, outs, name, mib, specs=None, scratch=()):
    return pl.pallas_call(
        kernel,
        in_specs=specs or [VMEM] * len(ins),
        out_specs=[VMEM] * len(outs),
        out_shape=outs,
        scratch_shapes=list(scratch),
        compiler_params=params(mib),
        cost_estimate=estimate(name),
        name=name,
    )(*ins)


def swaps(first, second, axis):
    length = lax.axis_size(axis)
    even = [(i, i ^ 1) for i in range(length) if i ^ 1 < length]
    odd = [(i, i + 1) for i in range(1, length - 1, 2)]
    odd += [(j, i) for i, j in odd]
    return lax.ppermute(first, axis, even), lax.ppermute(second, axis, odd)


def by_side(axis, work, first, second):
    at = lax.axis_index(axis) % 2

    @pl.when(at == 1)
    def _():
        work(first, second)

    @pl.when(at == 0)
    def _():
        work(second, first)


def load_kernel(leads, *refs):
    count = len(leads)
    ins, (own, y_low, y_high, token), sems = refs[:count], refs[-5:-1], refs[-1]
    token[...] = jnp.zeros(token.shape, F32)
    copies = [
        pltpu.make_async_copy(
            ins[n] if lead is None else ins[n].at[lead], own.at[n], sems.at[n]
        )
        for n, lead in enumerate(leads)
    ]
    for c in copies:
        c.start()
    for c in copies:
        c.wait()
    by_side("gy", lambda low, high: y_edges(own, low, high), y_low, y_high)


def y_edges(own, low, high):
    ry = own.shape[2]

    def one(n, _):
        low[n] = own[n, :, 0:H, :]
        high[n] = own[n, :, ry - H :, :]
        return 0

    lax.fori_loop(0, own.shape[0], one, 0)


def load(arrays, leads, dims, after):
    n = len(leads)
    rx, ry, nz = dims
    return pl.pallas_call(
        functools.partial(load_kernel, leads),
        in_specs=[HBM] * n + [ANY] * len(after),
        out_specs=[VMEM] * 4,
        out_shape=[sds(n, *dims)] + [sds(n, rx, H, nz)] * 2 + [sds(8, 128)],
        scratch_shapes=[pltpu.SemaphoreType.DMA((n,))],
        name="load",
    )(*arrays, *after)


def more_kernel(plan, count, parts, *refs):
    ins, outs = refs[:count], refs[count + 1 :]
    holders, firsts, seconds = outs[:parts], outs[parts::2], outs[parts + 1 :: 2]
    rx, ry = holders[0].shape[1:3]

    def work(lows, highs):
        def row(x, _):
            for i, lead, h, m in plan:
                value = ins[i][x] if lead is None else ins[i][lead, x]
                holders[h][m, x] = value
                lows[h][m, x] = value[0:H]
                highs[h][m, x] = value[ry - H :]
            return 0

        lax.fori_loop(0, rx, row, 0)

    by_side("gy", work, firsts, seconds)


def more(arrays, plan, sizes, dims, after):
    rx, ry, nz = dims
    return call(
        functools.partial(more_kernel, plan, len(arrays), len(sizes)), list(arrays) + [after],
        [sds(m, *dims) for m in sizes] + [sds(m, rx, H, nz) for m in sizes for _ in range(2)],
        "more", 4, [VMEM] * len(arrays) + [ANY],
    )


def tiles_of(reach):
    return reach // 2


def rows_of_array(reach):
    return reach + tiles_of(reach)


def fold(row, reach, high):
    tiles = []
    for dx in range(1, tiles_of(reach) + 1):
        near, far = row(dx), row(reach - dx)
        sub = lax.broadcasted_iota(jnp.int32, near.shape, 0)
        if high:
            tiles.append(jnp.where(sub < 8 - dx, near, pltpu.roll(far, 8 - dx, 0)))
        else:
            tiles.append(jnp.where(sub >= dx, near, pltpu.roll(far, dx, 0)))
    return tiles


def unfold(tile, dx, high):
    return tile, pltpu.roll(tile, dx if high else 8 - dx, 0)


def parts_of(reaches):
    parts, row = [], 0
    for n, reach in enumerate(reaches):
        if parts and parts[-1][2] == reach:
            parts[-1][1] += 1
        else:
            parts.append([n, 1, reach, row])
        row += rows_of_array(reach)
    return parts, row


def widen_kernel(reaches, first, own, z_first, z_second, *refs):
    rx = own.shape[1]

    def work(z_low, z_high, outs):
        for begin, count, reach, base in parts_of(reaches)[0]:

            def one(k, _):
                n = begin + k
                at = base + k * rows_of_array(reach)
                for side in (0, 1):
                    start = 0 if side == 0 else rx - reach
                    outs[side][pl.ds(at, reach)] = own[n, start : start + reach]
                    for high, z in ((0, z_low), (1, z_high)):

                        def row(dx):
                            return z[n + first, dx - 1 if side == 0 else rx - dx]

                        for t, tile in enumerate(fold(row, reach, high == 1)):
                            outs[side][at + reach + t, high * H : (high + 1) * H, :] = tile
                return 0

            lax.fori_loop(0, count, one, 0)

    def along_x(low, high):
        by_side("gy", lambda a, b: work(a, b, (low, high)), z_first, z_second)

    by_side("gx", along_x, *refs[-2:])


def widen(own, reaches, z_low, z_high, after=(), first=0):
    _, rx, ry, nz = own.shape
    return call(
        functools.partial(widen_kernel, reaches, first), [own, z_low, z_high, *after],
        [sds(parts_of(reaches)[1], ry, nz)] * 2, "widen", 4, [VMEM] * 3 + [ANY] * len(after),
    )


def table_kernel(steps, *refs):
    rate, bhp, control, perf_well, perf_cell, perf_wi = [r[...] for r in refs[:6]]
    out = refs[-1]
    wells = rate.shape[0]
    effective = jnp.where(control == 1, rate, bhp)
    lane = lax.broadcasted_iota(jnp.int32, (1, 128), 1)
    row = jnp.zeros((1, 128), F32)
    for u in range(wells):
        for n in range(steps):
            row = jnp.where(lane == u * steps + n, effective[u : u + 1, n : n + 1], row)
    mine = jnp.concatenate([row, perf_cell.astype(F32), perf_well.astype(F32), perf_wi])
    out[...] = jnp.broadcast_to(mine[None], out.shape)


def spot():
    n_x, n_y = lax.axis_size("gx"), lax.axis_size("gy")
    x, y = lax.axis_index("gx"), lax.axis_index("gy")
    return x, y, n_x, n_y


def source_kernel(steps, wells, table_ref, _, src_ref):
    here_x, here_y, n_x, n_y = spot()
    count = table_ref.shape[0]
    rx, ry = src_ref.shape[1] - 2 * H, src_ref.shape[2] - 2 * H
    of_wells = table_ref[:, 0, :]
    columns = [
        jnp.broadcast_to(of_wells[:, c : c + 1], (count, 128)) for c in range(wells * steps)
    ]
    owner_iota = lax.broadcasted_iota(jnp.int32, (count, 128), 0)
    sub = lax.broadcasted_iota(jnp.int32, (128, 128), 0)

    def spans(length):
        return ((0, H, length - H), (H, length, 0), (H + length, H, 0))

    for dx, (x0, size_x, from_x) in enumerate(spans(rx)):
        for dy, (y0, size_y, from_y) in enumerate(spans(ry)):
            at_x, at_y = here_x + dx - 1, here_y + dy - 1
            inside = (at_x >= 0) & (at_x < n_x) & (at_y >= 0) & (at_y < n_y)
            slot = table_ref[jnp.where(inside, at_x * n_y + at_y, 0)]
            cell = slot[1:2, :].astype(jnp.int32)
            well = slot[2:3, :].astype(jnp.int32)
            wi = slot[3:4, :] * inside.astype(F32)
            owner = well // wells
            within = well - owner * wells
            hot = owner_iota == owner
            in_lane = sub == (cell & 127)
            pieces = []
            for step in range(steps):
                chosen = columns[step]
                for u in range(1, wells):
                    chosen = jnp.where(within == u, columns[u * steps + step], chosen)
                value = jnp.sum(jnp.where(hot, chosen, 0.0), axis=0, keepdims=True) * wi
                high = value.astype(BF16).astype(F32)
                for piece in (high, value - high):
                    pieces.append(jnp.where(in_lane, piece, 0.0).astype(BF16))
            xi = lax.broadcasted_iota(jnp.int32, (size_x, size_y, 128), 0) + from_x
            yi = lax.broadcasted_iota(jnp.int32, (size_x, size_y, 128), 1) + from_y
            target = (xi * ry + yi).reshape(size_x * size_y, 128)
            by_row = jnp.where(target == (cell >> 7), 1.0, 0.0).astype(BF16)
            found = lax.dot_general(
                by_row, jnp.concatenate(pieces), (((1,), (1,)), ((), ())),
                preferred_element_type=F32,
            )
            for step in range(steps):
                part = found[:, step * 256 : step * 256 + 128]
                part = part + found[:, step * 256 + 128 : step * 256 + 256]
                src_ref[step, x0 : x0 + size_x, y0 : y0 + size_y, :] = part.reshape(
                    size_x, size_y, 128
                )


def by_v(ref, lead, x):
    return jnp.stack([ref[(*lead, x, pl.ds(v, 8, stride=V), slice(None))] for v in range(V)])


def up_v(value):
    return jnp.concatenate([value[1:], pltpu.roll(value[0], 7, 0)[None]])


def down_v(value):
    return jnp.concatenate([pltpu.roll(value[V - 1], 1, 0)[None], value[:-1]])


def roll_z(value, by):
    return pltpu.roll(value, by, 2)


def fill(dst, own, reaches, z_got, x_got, first=0):
    rx, ry, nz = own.shape[1:]

    def middle(z_low, z_high):
        def one(n, _):
            dst[n, H : H + rx, 0:H, :] = z_low[n + first]
            dst[n, H : H + rx, H : H + ry, :] = own[n]
            dst[n, H : H + rx, H + ry : 2 * H + ry, :] = z_high[n + first]
            return 0

        lax.fori_loop(0, len(reaches), one, 0)

    def outer(x_low, x_high):
        sides = (x_low, x_high)
        for begin, count, reach, base in parts_of(reaches)[0]:

            def one(k, _):
                n = begin + k
                row = base + k * rows_of_array(reach)
                for side in (0, 1):
                    at = H - reach if side == 0 else H + rx
                    dst[n, at : at + reach, H : H + ry, :] = sides[side][pl.ds(row, reach)]
                    known = set()
                    for y in (0, 1):
                        to = y * (H + ry)
                        for t in range(tiles_of(reach)):
                            tile = sides[side][row + reach + t, y * H : (y + 1) * H, :]
                            near, far = unfold(tile, t + 1, y == 1)
                            for dx, value in ((t + 1, near), (reach - t - 1, far)):
                                x = H - dx if side == 0 else H + rx + dx - 1
                                dst[n, x, to : to + H, :] = value
                                known.add(dx)
                    for dx in range(1, H + 1):
                        x = H - dx if side == 0 else H + rx + dx - 1
                        if dx not in known:
                            for y in (0, H + ry):
                                dst[n, x, y : y + H, :] = jnp.zeros((H, nz), F32)
                        if dx > reach:
                            dst[n, x, H : H + ry, :] = jnp.zeros((ry, nz), F32)
                return 0

            lax.fori_loop(0, count, one, 0)

    by_side("gy", middle, *z_got)
    by_side("gx", outer, *x_got)


GEO, COEF = 8, 7
TOP_REACH = (GEO,) * 3 + (COEF,) * 8
LAM_REACH = (GEO,) * 2


SA, RA, PC, FR, RB, QC, MC, AA, AB = range(9)
TX, TY, TZ, TU, WS = range(5)


def coefficients(raw, base, src_ref, step, x, total):
    c_pp, c_ss, c_ps, c_sp, frac, mob, g_p, g_s = [by_v(raw, (base + n,), x) for n in range(8)]
    den_a = c_pp + total
    den_b = c_ss + mob * total
    s_a = jnp.where(den_a > 0, OMEGA / den_a, 0.0)
    s_b = jnp.where(den_b > 0, OMEGA / den_b, 0.0)
    r_a = g_p + by_v(src_ref, (step,), x)
    return s_a, r_a, c_sp + frac * total, frac, s_b * g_s, s_b * c_ps, s_b * mob, s_b


BLOCK = 2
UNROLL = 4


def sweeps(coef, geo, bufs, lin, begin, ex):
    def work(number, x, count):
        old, new = bufs[(number - 1) % 2], bufs[number % 2]
        tx = [geo[TX, x + r] for r in range(count + 1)]
        values = [[old[f][x - 1 + r] for r in range(count + 2)] for f in range(2)]
        results = []
        for r in range(count):
            at = x + r
            ty = geo[TY, at]
            ty_up = up_v(ty)
            tz, tz_up = geo[TZ, at], geo[TU, at]

            def around(v):
                c = v[r + 1]
                total = tx[r + 1] * v[r + 2] + tx[r] * v[r]
                total = total + (ty_up * up_v(c) + ty * down_v(c))
                total = total + (tz_up * roll_z(c, 127) + tz * roll_z(c, 1))
                return c, total

            a, n_a = around(values[0])
            b, n_b = around(values[1])
            new_a = KEEP * a + coef[SA, at] * (
                (coef[RA, at] + n_a) + (coef[FR, at] * n_b - coef[PC, at] * b)
            )
            new_b = (KEEP * b + coef[RB, at]) + (coef[MC, at] * n_b - coef[QC, at] * a)
            results.append((new_a, new_b))
        for r in range(count):
            for f in range(2):
                if number == SWEEPS:
                    for v in range(V):
                        lin[f, x + r, pl.ds(v, 8, stride=V), :] = results[r][f][v]
                else:
                    new[f][x + r] = results[r][f]

    for number in range(begin, SWEEPS + 1):
        size = BLOCK * UNROLL
        total = ex - 2 * number

        def many(i, _):
            for u in range(UNROLL):
                work(number, number + i * size + u * BLOCK, BLOCK)
            return 0

        lax.fori_loop(0, total // size, many, 0)
        for at in range(total - total % size, total, BLOCK):
            work(number, number + at, BLOCK)


def finish(last, step, steps, wells, lin, frac, table_ref, before, outs):
    rx, ry, nz = frac.shape[-3:]
    out_wells = outs[-1]

    def copies(low, high):
        def copy(x, _):
            for f in range(2):
                row = lin[f, H + x, H : H + ry, :]
                if last:
                    outs[f][x] = row
                else:
                    outs[0][f, x] = row
                    low[f, x] = row[0:H]
                    high[f, x] = row[ry - H :]
            return 0

        lax.fori_loop(0, rx, copy, 0, unroll=2)

    if last:
        copies(None, None)
    else:
        by_side("gy", copies, outs[1], outs[2])
    mix = lin[0, H : H + rx, H : H + ry, :] + frac[...] * lin[1, H : H + rx, H : H + ry, :]
    mix = mix.reshape(rx * ry, nz)
    here_x, here_y, _, n_y = spot()
    slot = table_ref[here_x * n_y + here_y]
    lane = lax.broadcasted_iota(jnp.int32, (128, 128), 1)
    diagonal = lax.broadcasted_iota(jnp.int32, (128, 128), 0) == lane

    def upright(row):
        return jnp.sum(jnp.where(diagonal, row, 0.0), axis=1, keepdims=True)

    cell = upright(slot[1:2, :]).astype(jnp.int32)
    wi = upright(slot[3:4, :])
    by_row = jnp.where(
        lax.broadcasted_iota(jnp.int32, (128, rx * ry), 1) == (cell >> 7), 1.0, 0.0
    ).astype(BF16)
    picked = None
    for _ in range(3):
        piece = mix.astype(BF16)
        mix = mix - piece.astype(F32)
        add = jnp.dot(by_row, piece, preferred_element_type=F32)
        picked = add if picked is None else picked + add
    values = jnp.sum(jnp.where(lane == (cell & 127), picked, 0.0), axis=1, keepdims=True)
    values = values * wi
    spread = jnp.where(lane == step, values, 0.0)
    well = slot[2:3, :].astype(jnp.int32)
    count = table_ref.shape[0] * wells
    hot = jnp.where(
        lax.broadcasted_iota(jnp.int32, (count, 128), 0) == well, 1.0, 0.0
    ).astype(F32)
    dense = jnp.dot(hot, spread, precision=HIGHEST, preferred_element_type=F32)
    if before is not None:
        dense = dense + before[...]
    out_wells[...] = dense


def first_kernel(step, steps, wells, *refs):
    table_ref, src_ref, own, z_low, z_high, x_low, x_high = refs[:7]
    geo = refs[7]
    outs = refs[8:12]
    raw, coef, fa0, fb0, fa1, fb1, lin = refs[12:]
    rx, ry, nz = own.shape[1:]
    ex = rx + 2 * H
    fill(raw, own, TOP_REACH, (z_low, z_high), (x_low, x_high))
    here_x, here_y, _, _ = spot()

    @pl.when(here_x == 0)
    def _():
        raw[0, H, :, :] = jnp.zeros(raw.shape[2:], F32)

    @pl.when(here_y == 0)
    def _():
        def clear(x, _):
            raw[1, x, H : H + 1, :] = jnp.zeros((1, nz), F32)
            return 0

        lax.fori_loop(0, ex, clear, 0)

    def geometry(x, _):
        lane = lax.broadcasted_iota(jnp.int32, (V, 8, nz), 2)
        tz = jnp.where(lane == 0, 0.0, by_v(raw, (2,), x))
        geo[TX, x] = by_v(raw, (0,), x)
        geo[TY, x] = by_v(raw, (1,), x)
        geo[TZ, x] = tz
        geo[TU, x] = roll_z(tz, 127)
        return 0

    lax.fori_loop(0, ex, geometry, 0, unroll=4)

    def prepare(x, _):
        ty = geo[TY, x]
        total = (
            (geo[TX, x + 1] + geo[TX, x]) + (up_v(ty) + ty) + (geo[TU, x] + geo[TZ, x])
        )
        geo[WS, x] = total
        s_a, r_a, p, frac, r_b, q, m, _ = coefficients(
            raw, 3, src_ref, step, x, total
        )
        coef[SA, x] = s_a
        coef[RA, x] = r_a
        coef[PC, x] = p
        coef[FR, x] = frac
        coef[RB, x] = r_b
        coef[QC, x] = q
        coef[MC, x] = m
        fa1[x] = s_a * r_a
        fb1[x] = r_b
        return 0

    lax.fori_loop(0, ex - 1, prepare, 0)
    sweeps(coef, geo, ((fa0, fb0), (fa1, fb1)), lin, 2, ex)
    finish(False, step, steps, wells, lin, own.at[7], table_ref, None, outs)


def prepare_kernel(step, first, with_acc, *refs):
    src_ref, geo, own, z_low, z_high, x_low, x_high = refs[:7]
    if with_acc:
        coef, acc_out, raw = refs[7:]
    else:
        acc, coef, raw = refs[7:]
    rx, ry, nz = own.shape[1:]
    ex = rx + 2 * H
    fill(raw, own, (COEF,) * own.shape[0], (z_low, z_high), (x_low, x_high), first)

    def prepare(x, _):
        s_a, r_a, p, frac, r_b, q, m, s_b = coefficients(
            raw, 0, src_ref, step, x, geo[WS, x]
        )
        coef[SA, x] = s_a
        coef[RA, x] = r_a
        coef[PC, x] = p
        coef[FR, x] = frac
        coef[RB, x] = r_b
        coef[QC, x] = q
        coef[MC, x] = m
        if with_acc:
            a, b = by_v(raw, (8,), x), by_v(raw, (9,), x)
            acc_out[0, x] = a
            acc_out[1, x] = b
        else:
            a, b = acc[0, x], acc[1, x]
        coef[AA, x] = a
        coef[AB, x] = s_b * b
        return 0

    lax.fori_loop(0, ex, prepare, 0, unroll=4)


def sweep_kernel(last, step, steps, wells, *refs):
    table_ref, coef, geo, own, lam, z_low, z_high, x_low, x_high, before = refs[:10]
    outs = refs[10:-6]
    now, fa0, fb0, fa1, fb1, lin = refs[-6:]
    rx, ry, nz = own.shape[1:]
    ex = rx + 2 * H
    fill(lin, lam, LAM_REACH, (z_low, z_high), (x_low, x_high))

    def begin(x, _):
        a, b = by_v(lin, (0,), x), by_v(lin, (1,), x)
        fa0[x] = a
        fb0[x] = b
        now[0, x] = coef[RA, x] + coef[AA, x] * a
        now[1, x] = coef[RB, x] + coef[AB, x] * b
        return 0

    lax.fori_loop(0, ex, begin, 0, unroll=4)

    class Joined:
        def __getitem__(self, at):
            n, x = at
            return now[0, x] if n == RA else now[1, x] if n == RB else coef[n, x]

    sweeps(Joined(), geo, ((fa0, fb0), (fa1, fb1)), lin, 1, ex)
    finish(last, step, steps, wells, lin, own.at[4], table_ref, before, outs)


def local(
    grad_p, grad_s, acc_p, acc_s, trans_x, trans_y, trans_z, c_pp, c_ss, c_ps, c_sp,
    frac, mobility, rate_mis, bhp_mis, control, perf_well, perf_cell, perf_wi,
):
    dims = rx, ry, nz = trans_x.shape
    ex, ey = rx + 2 * H, ry + 2 * H
    steps = grad_p.shape[0]
    wells = rate_mis.shape[0]
    devices = lax.axis_size("gx") * lax.axis_size("gy")
    own = [c_pp, c_ss, c_ps, c_sp, frac, mobility, grad_p, grad_s]
    top = steps - 1

    arrays = [trans_x, trans_y, trans_z] + own
    leads = [None] * 3 + [top] * 8
    split = len(arrays)
    small = [rate_mis, bhp_mis, control] + [p[None] for p in (perf_well, perf_cell, perf_wi)]
    mine = call(
        functools.partial(table_kernel, steps), small, [sds(devices, 4, 128)], "table", 4
    )[0]
    blocks, y_low, y_high, token = load(arrays, leads, dims, ())
    z_got = swaps(y_low, y_high, "gy")
    mine, _ = lax.optimization_barrier((mine, token))
    table = lax.all_to_all(mine, ("gx", "gy"), 0, 0, tiled=True)

    wide = widen(blocks, TOP_REACH, *z_got, (table,))
    x_got = swaps(*wide, "gx")
    src = call(
        functools.partial(source_kernel, steps, wells), [table, wide[0]],
        [sds(steps, ex, ey, nz)], "sources", 8, [VMEM, ANY],
    )[0]

    plan, sizes = [], []
    for h, step in enumerate(reversed(range(top))):
        plan += [(n, step, h, n) for n in range(8)]
        if h == 0:
            plan += [(8, None, h, 8), (9, None, h, 9)]
        sizes.append(10 if h == 0 else 8)
    made = more(own + [acc_p, acc_s], plan, sizes, dims, table)
    held = dict(zip(reversed(range(top)), made[:top]))
    ends = {step: made[top + 2 * h : top + 2 * h + 2] for h, step in enumerate(reversed(range(top)))}
    m_z = {}

    def beside(step, after):
        group = held[step]
        return widen(group, (COEF,) * group.shape[0], *m_z[step], (after,))

    first, second = ends[top - 1]
    first, second, _ = lax.optimization_barrier((first, second, src))
    m_z[top - 1] = swaps(first, second, "gy")
    sides = beside(top - 1, src)
    late = sides[0]
    sides = swaps(*sides, "gx")

    ext = (ex, V, 8, nz)
    lam_out = [sds(2, rx, ry, nz), sds(2, rx, H, nz), sds(2, rx, H, nz)]
    well_out = sds(devices * wells, 128)
    fields = [pltpu.VMEM(ext, F32)] * 4 + [pltpu.VMEM((2, ex, ey, nz), F32)]

    geo, lam, low, high, dense = call(
        functools.partial(first_kernel, top, steps, wells),
        [table, src, blocks, *z_got, *x_got],
        [sds(5, *ext)] + lam_out + [well_out], "step_top", 16,
        scratch=[pltpu.VMEM((split, ex, ey, nz), F32), pltpu.VMEM((7, *ext), F32)] + fields,
    )

    acc = None
    for step in reversed(range(top)):
        last = step == 0
        with_acc = step == top - 1
        if not with_acc:
            sides = swaps(*beside(step, coef), "gx")
        else:
            first, second, _ = lax.optimization_barrier((*ends[step - 1], late))
            m_z[step - 1] = swaps(first, second, "gy")
            low, high, *_ = lax.optimization_barrier((low, high, *m_z[step - 1]))
        made = call(
            functools.partial(prepare_kernel, step, 0, with_acc),
            [src, geo, held[step], *m_z[step], *sides] + ([] if with_acc else [acc]),
            [sds(9, *ext)] + ([sds(2, *ext)] if with_acc else []), "prepare", 8,
            scratch=[pltpu.VMEM((10 if with_acc else 8, ex, ey, nz), F32)],
        )
        coef = made[0]
        if with_acc:
            acc = made[1]

        l_z = swaps(low, high, "gy")
        l_x = swaps(*widen(lam, LAM_REACH, *l_z), "gx")
        outs = [sds(rx, ry, nz)] * 2 if last else lam_out
        outs = call(
            functools.partial(sweep_kernel, last, step, steps, wells),
            [table, coef, geo, held[step], lam, *l_z, *l_x, dense],
            outs + [well_out], "step", 8, scratch=[pltpu.VMEM((2, *ext), F32)] + fields,
        )
        dense = outs[-1]
        if not last:
            lam, low, high = outs[:3]

    dense = dense.reshape(devices, wells, 128)
    parts = lax.all_to_all(dense, ("gx", "gy"), 0, 0, tiled=True)
    well_grad = jnp.sum(parts, axis=0)[:, :steps]
    return outs[0], outs[1], well_grad


def solution(mesh):
    cells3 = P("gx", "gy", None)
    cells4 = P(None, "gx", "gy", None)
    flat = ("gx", "gy")
    placed = (cells4,) * 2 + (cells3,) * 5 + (cells4,) * 6 + (P(flat, None),) * 3 + (P(flat),) * 3
    return jax.shard_map(
        local,
        mesh=mesh,
        in_specs=placed,
        out_specs=(cells3, cells3, P(flat, None)),
        check_vma=False,
    )
```
